32 devices in a mesh: groups: 2 (over x), rows: 16 (over z, y, core).
Axes of the slice: x: 2, y: 2, z: 4, core: 2. Of those that a mesh axis runs over, the one named last changes fastest.
Arguments:
- tokens: bfloat16 [64, 256, 1024], P(('groups', 'rows')), parts along dimension 0, may hold values from -6 to 6
- peg_weight: float32 [3, 3, 1024], replicated, may hold values from -2 to 2
- peg_bias: float32 [1024], replicated, may hold values from -3 to 3
- norm_gain: float32 [1024], replicated, may hold values from 0.25 to 1.75
- norm_bias: float32 [1024], replicated, may hold values from -3 to 3
- qkv_weight: bfloat16 [1024, 3072], replicated, may hold values from -1 to 1
- qkv_bias: float32 [3072], replicated, may hold values from -3 to 3
- out_weight: bfloat16 [1024, 1024], replicated, may hold values from -0.1875 to 0.1875
- out_bias: float32 [1024], replicated, may hold values from -3 to 3
Outputs:
- result: bfloat16 [64, 256, 1024], P(('groups', 'rows')), parts along dimension 0
The draws below stay inside these ranges and needn't reach their ends.
There are 2 independent parts, one for each index of `groups`. The reference program is written for one: setup_inputs(seed, part) draws one part's arguments, and reference() takes and returns one part's arrays. A program takes and returns all parts, laid end to end along the dimension named above; an argument that names none is the same for every part. Nothing has to cross between parts.
All inputs are finite; a program needn't handle non-finite values.
Results may differ from the reference program's by a relative error of at most 0.006.
Values may be sent and summed in bfloat16 or wider, within the bound.
No kernel may reach another device: no remote copies, remote signals or barrier semaphores. Data moves between devices by JAX's collectives and lax.ppermute only.
A program may use at most 64 MiB of HBM per device.

```python
import math
import jax
import jax.numpy as jnp
from jax import lax

D = 1024
HEADS = 16
DH = 64
ROW_HEADS = 8
W = 256
H = 32


def draw_tokens(key, part):
    return jax.random.truncated_normal(jax.random.fold_in(key, 14), -6.0, 6.0, (H, W, D), jnp.float32).astype(jnp.bfloat16)


def draw_qkv_weight(key, part):
    first = jax.random.normal(jax.random.fold_in(key, 21), (D, D), jnp.float32) * D ** (-0.5)
    second = jax.random.normal(jax.random.fold_in(key, 22), (D, D), jnp.float32) * D ** (-0.5)
    third = jax.random.normal(jax.random.fold_in(key, 23), (D, D), jnp.float32) * D ** (-0.5)
    whole = jnp.concatenate([first, second, third], axis=1)
    return jnp.clip(whole, -1.0, 1.0).astype(jnp.bfloat16)


def scatter_about(key, extent, scale, reach, dtype=jnp.bfloat16):
    return jnp.clip(scale * jax.random.normal(key, extent, jnp.float32), -reach, reach).astype(dtype)


def setup_inputs(seed: int = 0, part: int = 0) -> dict:
    arg_keys = jax.random.split(jax.random.key(seed), 10)
    part_keys = jax.random.split(jax.random.fold_in(arg_keys[9], part), 10)
    tokens = draw_tokens(jax.random.fold_in(jax.random.fold_in(arg_keys[9], part), 71), part)
    peg_weight = scatter_about(arg_keys[1], (3, 3, D), 9 ** -0.5, 2.0, jnp.float32)
    peg_bias = scatter_about(arg_keys[2], (D,), 0.5, 3.0, jnp.float32)
    norm_gain = jnp.clip(1.0 + 0.15 * jax.random.normal(arg_keys[3], (D,), jnp.float32), 0.25, 1.75)
    norm_bias = scatter_about(arg_keys[4], (D,), 0.3, 3.0, jnp.float32)
    qkv_weight = draw_qkv_weight(jax.random.fold_in(arg_keys[9], 71), part)
    qkv_bias = scatter_about(arg_keys[6], (3 * D,), 0.3, 3.0, jnp.float32)
    out_weight = scatter_about(arg_keys[7], (D, D), D ** -0.5, 0.1875)
    out_bias = scatter_about(arg_keys[8], (D,), 0.3, 3.0, jnp.float32)
    return {"tokens": tokens, "peg_weight": peg_weight, "peg_bias": peg_bias, "norm_gain": norm_gain, "norm_bias": norm_bias, "qkv_weight": qkv_weight, "qkv_bias": qkv_bias, "out_weight": out_weight, "out_bias": out_bias}


def convolve(padded, peg_weight, peg_bias, count_rows, count_cols):
    total = padded[1:count_rows + 1, 1:count_cols + 1, :].astype(jnp.float32) + peg_bias
    for offset_row in range(3):
        for offset_col in range(3):
            piece = padded[offset_row:offset_row + count_rows, offset_col:offset_col + count_cols, :]
            total = total + piece.astype(jnp.float32) * peg_weight[offset_row, offset_col]
    return total.astype(jnp.bfloat16)

def layer_norm(mixed, norm_gain, norm_bias):
    values = mixed.astype(jnp.float32)
    center = lax.optimization_barrier(jnp.mean(values, axis=-1, keepdims=True))
    spread = lax.optimization_barrier(jnp.mean((values - center) ** 2, axis=-1, keepdims=True))
    return ((values - center) * lax.rsqrt(spread + 1e-06) * norm_gain + norm_bias).astype(jnp.bfloat16)

def attend_single_line(query_key_value, softmax_divisor):
    query_rows, key_operand, value_operand = query_key_value
    attention_logits = jnp.einsum('gvu,ovu->vgo', query_rows.astype(jnp.float32), key_operand.astype(jnp.float32)) * softmax_divisor
    highest = lax.optimization_barrier(jnp.max(attention_logits, axis=-1, keepdims=True))
    attention_weights = jnp.exp(attention_logits - highest)
    attention_weights = (attention_weights / lax.optimization_barrier(jnp.sum(attention_weights, axis=-1, keepdims=True))).astype(jnp.bfloat16)
    return jnp.einsum('pxw,wpa->xpa', attention_weights.astype(jnp.float32), value_operand.astype(jnp.float32)).astype(jnp.bfloat16)

def reference(tokens, peg_weight, peg_bias, norm_gain, norm_bias, qkv_weight, qkv_bias, out_weight, out_bias):
    padded = jnp.pad(tokens, ((1, 1), (1, 1), (0, 0)))
    mixed = convolve(padded, peg_weight, peg_bias, H, W)
    normed = layer_norm(mixed, norm_gain, norm_bias)
    qkv = jnp.dot(normed.reshape(H * W, D), qkv_weight, preferred_element_type=jnp.float32) + qkv_bias
    qkv = qkv.astype(jnp.bfloat16).reshape(H, W, 3, HEADS, DH)
    tau_row = math.log(W) / (math.log(16.0) * math.sqrt(DH))
    tau_col = math.log(H) / (math.log(16.0) * math.sqrt(DH))
    row_trio = (qkv[:, :, 0, :ROW_HEADS], qkv[:, :, 1, :ROW_HEADS], qkv[:, :, 2, :ROW_HEADS])
    row_heads = lax.map(lambda query_key_value: attend_single_line(query_key_value, tau_row), row_trio)
    col_trio = tuple((jnp.transpose(qkv[:, :, part_index, ROW_HEADS:], (1, 0, 2, 3)) for part_index in range(3)))
    col_heads = lax.map(lambda query_key_value: attend_single_line(query_key_value, tau_col), col_trio)
    col_heads = jnp.transpose(col_heads, (1, 0, 2, 3))
    attended = jnp.concatenate([row_heads, col_heads], axis=2).reshape(H * W, D)
    result = mixed.reshape(H * W, D).astype(jnp.float32) + jnp.dot(attended, out_weight, preferred_element_type=jnp.float32) + out_bias
    return result.astype(jnp.bfloat16).reshape(H, W, D)
```

```python
import functools
import math

import jax
import jax.numpy as jnp
from jax import lax
from jax.experimental import pallas as pl
from jax.experimental.pallas import tpu as pltpu
from jax.sharding import PartitionSpec as P

HEADS = 16
DH = 64
ROW_HEADS = 8
LANES = 128
SUB = 8
HALF = SUB // 2
PAIR = LANES // DH
EPS = 1e-06
LOG2E = math.log2(math.e)
MIB = 1024 * 1024


def halo_rows(tokens):
    devices, bands = lax.axis_size("rows"), tokens.shape[0]
    up = [(i, i + 1) for i in range(devices - 1)]
    down = [(j, i) for i, j in up]
    before = lax.ppermute(tokens[bands - 1 :], "rows", up)
    after = lax.ppermute(tokens[:1], "rows", down)
    return before, after


def plain_convolve(padded, peg_weight, peg_bias, count_rows, count_cols):
    total = padded[1 : count_rows + 1, 1 : count_cols + 1, :].astype(jnp.float32) + peg_bias
    for offset_row in range(3):
        for offset_col in range(3):
            piece = padded[
                offset_row : offset_row + count_rows, offset_col : offset_col + count_cols, :
            ]
            total = total + piece.astype(jnp.float32) * peg_weight[offset_row, offset_col]
    return total.astype(jnp.bfloat16)


def plain_layer_norm(mixed, norm_gain, norm_bias):
    values = mixed.astype(jnp.float32)
    center = jnp.mean(values, axis=-1, keepdims=True)
    spread = jnp.mean((values - center) ** 2, axis=-1, keepdims=True)
    return ((values - center) * lax.rsqrt(spread + EPS) * norm_gain + norm_bias).astype(
        jnp.bfloat16
    )


def plain_project(normed, qkv_weight, qkv_bias, first_col, last_col):
    model = normed.shape[-1]
    flat_rows = normed.reshape(-1, model)
    outputs = []
    for part_index in range(3):
        lower = part_index * model + first_col
        upper = part_index * model + last_col
        projected = (
            jnp.dot(flat_rows, qkv_weight[:, lower:upper], preferred_element_type=jnp.float32)
            + qkv_bias[lower:upper]
        )
        outputs.append(
            projected.astype(jnp.bfloat16).reshape(normed.shape[:-1] + (last_col - first_col,))
        )
    return outputs


def plain_attend(query, key, value, head_count, tau, scoring, mixing):
    outputs = []
    for head in range(head_count):
        cols = slice(head * DH, (head + 1) * DH)
        logits = (
            jnp.einsum(
                scoring, query[..., cols], key[..., cols], preferred_element_type=jnp.float32
            )
            * tau
        )
        probs = jnp.exp(logits - jnp.max(logits, axis=-1, keepdims=True))
        probs = (probs / jnp.sum(probs, axis=-1, keepdims=True)).astype(jnp.bfloat16)
        outputs.append(
            jnp.einsum(
                mixing, probs, value[..., cols], preferred_element_type=jnp.float32
            ).astype(jnp.bfloat16)
        )
    return jnp.concatenate(outputs, axis=-1)


def plain(
    tokens, peg_weight, peg_bias, norm_gain, norm_bias, qkv_weight, qkv_bias, out_weight, out_bias
):
    bands, width, model = tokens.shape
    height = bands * lax.axis_size("rows")
    row_features = ROW_HEADS * DH
    before, after = halo_rows(tokens)
    padded = jnp.pad(
        jnp.concatenate([before, tokens, after], axis=0), ((0, 0), (1, 1), (0, 0))
    )
    mixed = plain_convolve(padded, peg_weight, peg_bias, bands, width)
    normed = plain_layer_norm(mixed, norm_gain, norm_bias)
    row_qkv = plain_project(normed, qkv_weight, qkv_bias, 0, row_features)
    arrived = lax.all_to_all(normed, "rows", split_axis=1, concat_axis=0, tiled=True)
    col_qkv = plain_project(arrived, qkv_weight, qkv_bias, row_features, model)
    row_heads = plain_attend(
        *row_qkv, ROW_HEADS, score_scale(width), "bld,bmd->blm", "blm,bmd->bld"
    )
    col_heads = plain_attend(
        *col_qkv, HEADS - ROW_HEADS, score_scale(height), "lbd,mbd->blm", "blm,mbd->lbd"
    )
    returned = lax.all_to_all(col_heads, "rows", split_axis=0, concat_axis=1, tiled=True)
    attended = jnp.concatenate([row_heads, returned], axis=2).reshape(bands * width, model)
    result = (
        mixed.reshape(bands * width, model).astype(jnp.float32)
        + jnp.dot(attended, out_weight, preferred_element_type=jnp.float32)
        + out_bias
    )
    return result.astype(jnp.bfloat16).reshape(bands, width, model)


def score_scale(count):
    return math.log(count) / (math.log(16.0) * math.sqrt(DH))


def interleave(first, second):
    upper = lax.broadcasted_iota(jnp.int32, first.shape, 0) < HALF
    low = jnp.where(upper, first, pltpu.roll(second, HALF, 0))
    high = jnp.where(upper, pltpu.roll(first, HALF, 0), second)
    return low, high


def pack_kernel(devices, per_step, own_ref, left_ref, right_ref, out_ref):
    model = own_ref.shape[2]
    cols = own_ref.shape[1] // per_step
    slabs = model // LANES
    tiles = cols // HALF
    step = pl.program_id(0)
    place = lax.broadcasted_iota(jnp.int32, (SUB, LANES), 0)
    for k in range(per_step):
        dest = step * per_step + k
        for eight in range(cols // SUB):
            start = k * cols + eight * SUB
            pair = interleave(
                own_ref[0, start : start + SUB, :].astype(jnp.float32),
                own_ref[1, start : start + SUB, :].astype(jnp.float32),
            )
            for which in range(2):
                tile = pair[which].astype(jnp.bfloat16)
                for slab in range(slabs):
                    base = (slab * tiles + eight * 2 + which) * SUB
                    out_ref[k, base : base + SUB, :] = tile[:, slab * LANES : (slab + 1) * LANES]
        lefts, rights = [], []
        for band in range(2):
            if k == 0:
                left = left_ref[band].astype(jnp.float32)[cols - 1 : cols]
            else:
                left = own_ref[band, (k - 1) * cols : k * cols, :].astype(jnp.float32)
                left = left[cols - 1 : cols]
            if k == per_step - 1:
                right = right_ref[band].astype(jnp.float32)[0:1]
            else:
                right = own_ref[band, (k + 1) * cols : (k + 2) * cols, :]
                right = right.astype(jnp.float32)[0:1]
            lefts.append(jnp.where(dest > 0, left, 0.0))
            rights.append(jnp.where(dest < devices - 1, right, 0.0))
        for two in range(slabs // 2):
            one = slice(2 * two * LANES, (2 * two + 1) * LANES)
            other = slice((2 * two + 1) * LANES, (2 * two + 2) * LANES)
            order = [rights[0][:, one], rights[0][:, other], lefts[0][:, other], lefts[0][:, one]]
            order += [rights[1][:, one], rights[1][:, other], lefts[1][:, other], lefts[1][:, one]]
            tile = jnp.broadcast_to(order[0], (SUB, LANES))
            for index in range(1, SUB):
                tile = jnp.where(place == index, order[index], tile)
            base = (slabs * tiles + two) * SUB
            out_ref[k, base : base + SUB, :] = tile.astype(jnp.bfloat16)


def pack(tokens, devices):
    bands, width, model = tokens.shape
    cols = width // devices
    slabs = model // LANES
    rows = slabs * bands * (cols + 2)
    per_step = 4
    last = devices - 1
    return pl.pallas_call(
        functools.partial(pack_kernel, devices, per_step),
        grid=(devices // per_step,),
        in_specs=[
            pl.BlockSpec((bands, per_step * cols, model), lambda i: (0, i, 0)),
            pl.BlockSpec(
                (bands, cols, model), lambda i: (0, jnp.maximum(i * per_step - 1, 0), 0)
            ),
            pl.BlockSpec(
                (bands, cols, model), lambda i: (0, jnp.minimum((i + 1) * per_step, last), 0)
            ),
        ],
        out_specs=pl.BlockSpec((per_step, rows, LANES), lambda i: (i, 0, 0)),
        out_shape=jax.ShapeDtypeStruct((devices, rows, LANES), jnp.bfloat16),
        compiler_params=pltpu.CompilerParams(vmem_limit_bytes=6 * MIB),
        name="pack_columns",
    )(*[in_hbm(tokens)] * 3)


def gate_kernel(*refs):
    pass


def gate(values, *after):
    hbm = pl.BlockSpec(memory_space=pltpu.HBM)
    anywhere = pl.BlockSpec(memory_space=pl.ANY)
    count = len(values)
    return pl.pallas_call(
        gate_kernel,
        in_specs=[hbm] * count + [anywhere] * len(after),
        out_specs=[hbm] * count,
        out_shape=[jax.ShapeDtypeStruct(value.shape, value.dtype) for value in values],
        input_output_aliases={index: index for index in range(count)},
        name="gate",
    )(*values, *after)


def in_hbm(value):
    return pltpu.with_memory_space_constraint(value, pltpu.HBM)


def normalise(values, gain, bias):
    center = jnp.mean(values, axis=-1, keepdims=True)
    shifted = values - center
    spread = jnp.mean(shifted * shifted, axis=-1, keepdims=True)
    return (shifted * lax.rsqrt(spread + EPS) * gain + bias).astype(jnp.bfloat16)


def attend_pair(query, key, value, scale, mask):
    count = query.shape[0]
    lane = lax.broadcasted_iota(jnp.int32, query.shape, 1)
    zero = jnp.zeros_like(query)
    both = jnp.concatenate(
        [jnp.where(lane < DH, query, zero), jnp.where(lane < DH, zero, query)], axis=0
    )
    scores = lax.dot_general(
        both, key, (((1,), (1,)), ((), ())), preferred_element_type=jnp.float32
    )
    if mask is not None:
        scores = jnp.where(mask, scores, -1e30)
    highest = jnp.max(scores, axis=-1, keepdims=True)
    probs = jnp.exp2((scores - highest) * (scale * LOG2E))
    total = jnp.sum(probs, axis=-1, keepdims=True)
    probs = (probs * (1.0 / total)).astype(jnp.bfloat16)
    mixed = jnp.dot(probs, value, preferred_element_type=jnp.float32)
    return jnp.where(lane < DH, mixed[:count], mixed[count:])


def weight_copies(qkv_hbm, weight_scr, sems, first):
    model = qkv_hbm.shape[0]
    width = weight_scr.shape[2]
    return [
        pltpu.make_async_copy(
            qkv_hbm.at[:, pl.ds(part * model + first, width)], weight_scr.at[part], sems.at[part]
        )
        for part in range(3)
    ]


def column_kernel(
    recv_ref,
    edge_ref,
    peg_ref,
    peg_bias_ref,
    gain_ref,
    nbias_ref,
    qkv_bias_ref,
    qkv_hbm,
    out_ref,
    mixed_scr,
    normed_scr,
    qkv_scr,
    weight_scr,
    sems,
):
    step = pl.program_id(0)
    devices = recv_ref.shape[0]
    tiles = recv_ref.shape[1] // (2 * SUB)
    height = 2 * devices
    first = ROW_HEADS * DH
    features = weight_scr.shape[2]
    group = devices * SUB

    @pl.when(step == 0)
    def _():
        for copy in weight_copies(qkv_hbm, weight_scr, sems, first):
            copy.start()

    place = lax.broadcasted_iota(jnp.int32, (1, 1, SUB, LANES), 2)
    upper = place < HALF
    column = lax.rem(place, HALF)

    def with_neighbours(value):
        swapped = pltpu.roll(value, HALF, 2)
        zero = jnp.zeros((1,) + value.shape[1:], jnp.float32)
        between = jnp.where(
            upper,
            jnp.concatenate([zero, swapped], axis=0),
            jnp.concatenate([swapped, zero], axis=0),
        )
        return between[:-1], value, between[1:]

    def stencil(triple, lanes, offset_col):
        total = None
        for offset_row in range(3):
            weight = peg_ref[offset_row, offset_col : offset_col + 1, lanes]
            term = triple[offset_row] * weight
            total = term if total is None else total + term
        return total

    edges = edge_ref[...].astype(jnp.float32).reshape(devices, 1, SUB, LANES)
    for local in range(2):
        lanes = slice(local * LANES, (local + 1) * LANES)
        own = recv_ref[:, local * tiles * SUB : (local + 1) * tiles * SUB, :]
        own = own.astype(jnp.float32).reshape(devices, tiles, SUB, LANES)
        triple = with_neighbours(own)
        if local == 0:
            left_edge = right_edge = with_neighbours(edges)
        else:
            left_edge = with_neighbours(pltpu.roll(edges, 1, 2))
            right_edge = with_neighbours(pltpu.roll(edges, SUB - 1, 2))
        wide = jnp.concatenate(
            [stencil(left_edge, lanes, 0), stencil(triple, lanes, 0)], axis=1
        )
        from_left = jnp.where(
            column == 0, pltpu.roll(wide[:, :-1], SUB - 3, 2), pltpu.roll(wide[:, 1:], 1, 2)
        )
        wide = jnp.concatenate(
            [stencil(triple, lanes, 2), stencil(right_edge, lanes, 2)], axis=1
        )
        from_right = jnp.where(
            column == HALF - 1,
            pltpu.roll(wide[:, 1:], 3, 2),
            pltpu.roll(wide[:, :-1], SUB - 1, 2),
        )
        total = (
            own + peg_bias_ref[:, lanes] + stencil(triple, lanes, 1) + from_left + from_right
        )
        mixed_scr[2 * step + local] = total.astype(jnp.bfloat16).astype(jnp.float32)

    @pl.when(step == pl.num_programs(0) - 1)
    def _():
        count = mixed_scr.shape[0]
        for tile in range(tiles):
            for start in range(0, devices, HALF):
                values = jnp.concatenate(
                    [
                        mixed_scr[slab, start : start + HALF, tile].reshape(HALF * SUB, LANES)
                        for slab in range(count)
                    ],
                    axis=1,
                )
                base = tile * group + start * SUB
                normed_scr[base : base + HALF * SUB, :] = normalise(
                    values, gain_ref[...], nbias_ref[...]
                )
        for part, copy in enumerate(weight_copies(qkv_hbm, weight_scr, sems, first)):
            copy.wait()
            projected = (
                jnp.dot(normed_scr[...], weight_scr[part], preferred_element_type=jnp.float32)
                + qkv_bias_ref[part : part + 1, :]
            )
            qkv_scr[part] = projected.astype(jnp.bfloat16)
        row_id = lax.broadcasted_iota(jnp.int32, (PAIR * group, group), 0)
        col_id = lax.broadcasted_iota(jnp.int32, (PAIR * group, group), 1)
        mask = lax.rem(row_id, HALF) == lax.rem(col_id, HALF)
        scale = score_scale(height)
        for tile in range(tiles):
            rows = slice(tile * group, (tile + 1) * group)
            for pair in range(features // LANES):
                lanes = slice(pair * LANES, (pair + 1) * LANES)
                heads = attend_pair(
                    qkv_scr[0, rows, lanes],
                    qkv_scr[1, rows, lanes],
                    qkv_scr[2, rows, lanes],
                    scale,
                    mask,
                )
                out_ref[:, tile, :, lanes] = heads.astype(jnp.bfloat16).reshape(
                    devices, SUB, LANES
                )


def column_part(recv, peg_weight, peg_bias, gain, nbias, qkv_weight, qkv_bias):
    devices, rows, _ = recv.shape
    model = gain.shape[-1]
    slabs = model // LANES
    cols = rows // (2 * slabs) - 2
    tiles = cols // HALF
    first = ROW_HEADS * DH
    features = model - first
    tokens = 2 * devices * cols
    whole2 = lambda i: (0, 0)
    steps = slabs // 2
    return pl.pallas_call(
        column_kernel,
        grid=(steps,),
        in_specs=[
            pl.BlockSpec((devices, 2 * tiles * SUB, LANES), lambda i: (0, i, 0)),
            pl.BlockSpec((devices, SUB, LANES), lambda i: (0, slabs * tiles + i, 0)),
            pl.BlockSpec((3, 3, 2 * LANES), lambda i: (0, 0, i)),
            pl.BlockSpec((1, 2 * LANES), lambda i: (0, i)),
            pl.BlockSpec((1, model), whole2),
            pl.BlockSpec((1, model), whole2),
            pl.BlockSpec((3, features), whole2),
            pl.BlockSpec(memory_space=pltpu.HBM),
        ],
        out_specs=pl.BlockSpec((devices, tiles, SUB, features), lambda i: (0, 0, 0, 0)),
        out_shape=pltpu.HBM((devices, tiles, SUB, features), jnp.bfloat16),
        scratch_shapes=[
            pltpu.VMEM((slabs, devices, tiles, SUB, LANES), jnp.float32),
            pltpu.VMEM((tokens, model), jnp.bfloat16),
            pltpu.VMEM((3, tokens, features), jnp.bfloat16),
            pltpu.VMEM((3, model, features), jnp.bfloat16),
            pltpu.SemaphoreType.DMA((3,)),
        ],
        compiler_params=pltpu.CompilerParams(vmem_limit_bytes=20 * MIB),
        cost_estimate=pl.CostEstimate(
            flops=2 * tokens * model * 3 * features,
            transcendentals=tokens * LANES * features // DH,
            bytes_accessed=8 * MIB,
        ),
        name="column_heads",
    )(recv, recv, peg_weight, peg_bias, gain, nbias, qkv_bias[:, first:], in_hbm(qkv_weight))


def row_kernel(
    tokens_ref,
    intra_ref,
    inter_ref,
    peg_ref,
    peg_bias_ref,
    gain_ref,
    nbias_ref,
    qkv_bias_ref,
    out_bias_ref,
    qkv_hbm,
    out_hbm,
    partial_ref,
    mixed_scr,
    normed_scr,
    qkv_scr,
    heads_scr,
    weight_scr,
    out_scr,
    sems,
):
    step = pl.program_id(0)
    slabs = pl.num_programs(0)
    bands, width, _ = tokens_ref.shape
    features = weight_scr.shape[2]

    def copies():
        copy = pltpu.make_async_copy(out_hbm.at[pl.ds(0, features), :], out_scr, sems.at[3])
        return weight_copies(qkv_hbm, weight_scr, sems, 0) + [copy]

    @pl.when(step == 0)
    def _():
        for copy in copies():
            copy.start()

    odd = lax.rem(lax.axis_index("rows"), 2) == 1
    intra = intra_ref[0].astype(jnp.float32)
    inter = inter_ref[0].astype(jnp.float32)
    rows = [jnp.where(odd, intra, inter)]
    rows += [tokens_ref[band].astype(jnp.float32) for band in range(bands)]
    rows += [jnp.where(odd, inter, intra)]
    position = lax.broadcasted_iota(jnp.int32, (width, LANES), 0)
    for band in range(bands):

        def stencil(offset_col):
            return (
                rows[band] * peg_ref[0, offset_col : offset_col + 1, :]
                + rows[band + 1] * peg_ref[1, offset_col : offset_col + 1, :]
                + rows[band + 2] * peg_ref[2, offset_col : offset_col + 1, :]
            )

        from_left = jnp.where(position == 0, 0.0, pltpu.roll(stencil(0), 1, 0))
        from_right = jnp.where(position == width - 1, 0.0, pltpu.roll(stencil(2), width - 1, 0))
        total = rows[band + 1] + peg_bias_ref[...] + stencil(1) + from_left + from_right
        mixed_scr[step, band * width : (band + 1) * width, :] = total.astype(
            jnp.bfloat16
        ).astype(jnp.float32)

    @pl.when(step == slabs - 1)
    def _():
        count = mixed_scr.shape[0]
        chunk = 64
        for start in range(0, bands * width, chunk):
            values = jnp.concatenate(
                [mixed_scr[slab, start : start + chunk, :] for slab in range(count)], axis=1
            )
            normed_scr[start : start + chunk, :] = normalise(
                values, gain_ref[...], nbias_ref[...]
            )
        waits = copies()
        for part in range(3):
            waits[part].wait()
            projected = (
                jnp.dot(normed_scr[...], weight_scr[part], preferred_element_type=jnp.float32)
                + qkv_bias_ref[part : part + 1, :]
            )
            qkv_scr[part] = projected.astype(jnp.bfloat16)
        scale = score_scale(width)
        for band in range(bands):
            span = slice(band * width, (band + 1) * width)
            for pair in range(features // LANES):
                lanes = slice(pair * LANES, (pair + 1) * LANES)
                heads_scr[span, lanes] = attend_pair(
                    qkv_scr[0, span, lanes],
                    qkv_scr[1, span, lanes],
                    qkv_scr[2, span, lanes],
                    scale,
                    None,
                ).astype(jnp.bfloat16)
        waits[3].wait()
        for slab in range(count):
            lanes = slice(slab * LANES, (slab + 1) * LANES)
            partial_ref[:, lanes] = (
                jnp.dot(heads_scr[...], out_scr[:, lanes], preferred_element_type=jnp.float32)
                + mixed_scr[slab]
                + out_bias_ref[:, lanes]
            )


def row_part(
    tokens,
    intra,
    inter,
    peg_weight,
    peg_bias,
    gain,
    nbias,
    qkv_weight,
    qkv_bias,
    out_weight,
    out_bias,
):
    bands, width, model = tokens.shape
    slabs = model // LANES
    features = ROW_HEADS * DH
    count = bands * width
    whole2 = lambda i: (0, 0)
    return pl.pallas_call(
        row_kernel,
        grid=(slabs,),
        in_specs=[
            pl.BlockSpec((bands, width, LANES), lambda i: (0, 0, i)),
            pl.BlockSpec((1, width, LANES), lambda i: (0, 0, i)),
            pl.BlockSpec((1, width, LANES), lambda i: (0, 0, i)),
            pl.BlockSpec((3, 3, LANES), lambda i: (0, 0, i)),
            pl.BlockSpec((1, LANES), lambda i: (0, i)),
            pl.BlockSpec((1, model), whole2),
            pl.BlockSpec((1, model), whole2),
            pl.BlockSpec((3, features), whole2),
            pl.BlockSpec((1, model), whole2),
            pl.BlockSpec(memory_space=pltpu.HBM),
            pl.BlockSpec(memory_space=pltpu.HBM),
        ],
        out_specs=pl.BlockSpec((count, model), whole2),
        out_shape=pltpu.HBM((count, model), jnp.float32),
        scratch_shapes=[
            pltpu.VMEM((slabs, count, LANES), jnp.float32),
            pltpu.VMEM((count, model), jnp.bfloat16),
            pltpu.VMEM((3, count, features), jnp.bfloat16),
            pltpu.VMEM((count, features), jnp.bfloat16),
            pltpu.VMEM((3, model, features), jnp.bfloat16),
            pltpu.VMEM((features, model), jnp.bfloat16),
            pltpu.SemaphoreType.DMA((4,)),
        ],
        compiler_params=pltpu.CompilerParams(vmem_limit_bytes=20 * MIB),
        cost_estimate=pl.CostEstimate(
            flops=2 * count * model * 4 * features,
            transcendentals=count * width * ROW_HEADS,
            bytes_accessed=10 * 1024 * 1024,
        ),
        name="row_heads",
    )(
        tokens,
        intra,
        inter,
        peg_weight,
        peg_bias,
        gain,
        nbias,
        qkv_bias[:, :features],
        out_bias,
        in_hbm(qkv_weight),
        in_hbm(out_weight),
    )


def last_kernel(partial_ref, heads_ref, out_weight_ref, result_ref):
    devices, tiles, sub, features = heads_ref.shape
    lanes = result_ref.shape[2]
    heads = heads_ref[...].reshape(devices * tiles * sub, features)
    projected = jnp.dot(heads, out_weight_ref[...], preferred_element_type=jnp.float32)
    pairs = projected.reshape(devices * tiles // 2, 2, sub, lanes)
    low, high = pairs[:, 0], pairs[:, 1]
    upper = lax.broadcasted_iota(jnp.int32, (1, sub, lanes), 1) < HALF
    first = jnp.where(upper, low, pltpu.roll(high, HALF, 1))
    second = jnp.where(upper, pltpu.roll(low, HALF, 1), high)
    width = result_ref.shape[1]
    for band, value in enumerate((first, second)):
        result_ref[band] = (
            partial_ref[band * width : (band + 1) * width, :] + value.reshape(width, lanes)
        ).astype(jnp.bfloat16)


def last_part(partial, heads, out_weight, bands, width):
    devices, tiles, sub, features = heads.shape
    model = out_weight.shape[1]
    first = ROW_HEADS * DH
    lanes = model // 4
    return pl.pallas_call(
        last_kernel,
        grid=(model // lanes,),
        in_specs=[
            pl.BlockSpec((bands * width, lanes), lambda i: (0, i)),
            pl.BlockSpec((devices, tiles, sub, features), lambda i: (0, 0, 0, 0)),
            pl.BlockSpec((features, lanes), lambda i: (first // features, i)),
        ],
        out_specs=pl.BlockSpec((bands, width, lanes), lambda i: (0, 0, i)),
        out_shape=jax.ShapeDtypeStruct((bands, width, model), jnp.bfloat16),
        compiler_params=pltpu.CompilerParams(vmem_limit_bytes=10 * MIB),
        cost_estimate=pl.CostEstimate(
            flops=2 * bands * width * features * model,
            transcendentals=0,
            bytes_accessed=5 * MIB,
        ),
        name="last_projection",
    )(in_hbm(partial), heads, out_weight)


def on_device(
    tokens, peg_weight, peg_bias, norm_gain, norm_bias, qkv_weight, qkv_bias, out_weight, out_bias
):
    devices = lax.axis_size("rows")
    bands, width, model = tokens.shape
    cols = width // devices
    fits = (
        bands == 2
        and width % LANES == 0
        and cols % 16 == 0
        and devices * SUB == LANES
        and model == 2 * ROW_HEADS * DH
        and model % LANES == 0
    )
    if not fits:
        return plain(
            tokens,
            peg_weight,
            peg_bias,
            norm_gain,
            norm_bias,
            qkv_weight,
            qkv_bias,
            out_weight,
            out_bias,
        )
    peg_bias = peg_bias.reshape(1, model)
    gain = norm_gain.reshape(1, model)
    nbias = norm_bias.reshape(1, model)
    out_bias = out_bias.reshape(1, model)
    qkv_bias = qkv_bias.reshape(3, model)

    packed = pack(tokens, devices)
    received = lax.all_to_all(packed, "rows", split_axis=0, concat_axis=0, tiled=True)
    odd = lax.rem(lax.axis_index("rows"), 2)
    intra = lax.dynamic_slice_in_dim(tokens, 1 - odd, 1, axis=0)
    inter = lax.dynamic_slice_in_dim(tokens, odd, 1, axis=0)
    intra, inter = gate((intra, inter), received[0, :SUB])
    same_chip = [(i, i ^ 1) for i in range(devices)]
    other_chip = [(i, i + 1 if i % 2 else i - 1) for i in range(1, devices - 1)]
    intra = lax.ppermute(intra, "rows", same_chip)
    inter = lax.ppermute(inter, "rows", other_chip)
    col_heads = column_part(
        received, peg_weight, peg_bias, gain, nbias, qkv_weight, qkv_bias
    )
    (col_heads,) = gate((col_heads,), intra[0, :SUB, :LANES], inter[0, :SUB, :LANES])
    returned = lax.all_to_all(col_heads, "rows", split_axis=0, concat_axis=0, tiled=True)
    partial = row_part(
        tokens,
        intra,
        inter,
        peg_weight,
        peg_bias,
        gain,
        nbias,
        qkv_weight,
        qkv_bias,
        out_weight,
        out_bias,
    )
    return last_part(partial, returned, out_weight, bands, width)


def solution(mesh):
    placed = (P(("groups", "rows"), None, None), P(), P(), P(), P(), P(), P(), P(), P())
    return jax.shard_map(
        on_device,
        mesh=mesh,
        in_specs=placed,
        out_specs=P(("groups", "rows"), None, None),
        check_vma=False,
    )
```

```python
import functools
import math

import jax
import jax.numpy as jnp
from jax import lax
from jax.experimental import pallas as pl
from jax.experimental.pallas import tpu as pltpu
from jax.sharding import PartitionSpec as P

HEADS = 16
DH = 64
ROW_HEADS = 8
LANES = 128
SUB = 8
HALF = SUB // 2
PAIR = LANES // DH
EPS = 1e-06
LOG2E = math.log2(math.e)
MIB = 1024 * 1024


def halo_rows(tokens):
    devices, bands = lax.axis_size("rows"), tokens.shape[0]
    up = [(i, i + 1) for i in range(devices - 1)]
    down = [(j, i) for i, j in up]
    before = lax.ppermute(tokens[bands - 1 :], "rows", up)
    after = lax.ppermute(tokens[:1], "rows", down)
    return before, after


def plain_convolve(padded, peg_weight, peg_bias, count_rows, count_cols):
    total = padded[1 : count_rows + 1, 1 : count_cols + 1, :].astype(jnp.float32) + peg_bias
    for offset_row in range(3):
        for offset_col in range(3):
            piece = padded[
                offset_row : offset_row + count_rows, offset_col : offset_col + count_cols, :
            ]
            total = total + piece.astype(jnp.float32) * peg_weight[offset_row, offset_col]
    return total.astype(jnp.bfloat16)


def plain_layer_norm(mixed, norm_gain, norm_bias):
    values = mixed.astype(jnp.float32)
    center = jnp.mean(values, axis=-1, keepdims=True)
    spread = jnp.mean((values - center) ** 2, axis=-1, keepdims=True)
    return ((values - center) * lax.rsqrt(spread + EPS) * norm_gain + norm_bias).astype(
        jnp.bfloat16
    )


def plain_project(normed, qkv_weight, qkv_bias, first_col, last_col):
    model = normed.shape[-1]
    flat_rows = normed.reshape(-1, model)
    outputs = []
    for part_index in range(3):
        lower = part_index * model + first_col
        upper = part_index * model + last_col
        projected = (
            jnp.dot(flat_rows, qkv_weight[:, lower:upper], preferred_element_type=jnp.float32)
            + qkv_bias[lower:upper]
        )
        outputs.append(
            projected.astype(jnp.bfloat16).reshape(normed.shape[:-1] + (last_col - first_col,))
        )
    return outputs


def plain_attend(query, key, value, head_count, tau, scoring, mixing):
    outputs = []
    for head in range(head_count):
        cols = slice(head * DH, (head + 1) * DH)
        logits = (
            jnp.einsum(
                scoring, query[..., cols], key[..., cols], preferred_element_type=jnp.float32
            )
            * tau
        )
        probs = jnp.exp(logits - jnp.max(logits, axis=-1, keepdims=True))
        probs = (probs / jnp.sum(probs, axis=-1, keepdims=True)).astype(jnp.bfloat16)
        outputs.append(
            jnp.einsum(
                mixing, probs, value[..., cols], preferred_element_type=jnp.float32
            ).astype(jnp.bfloat16)
        )
    return jnp.concatenate(outputs, axis=-1)


def plain(
    tokens, peg_weight, peg_bias, norm_gain, norm_bias, qkv_weight, qkv_bias, out_weight, out_bias
):
    bands, width, model = tokens.shape
    height = bands * lax.axis_size("rows")
    row_features = ROW_HEADS * DH
    before, after = halo_rows(tokens)
    padded = jnp.pad(
        jnp.concatenate([before, tokens, after], axis=0), ((0, 0), (1, 1), (0, 0))
    )
    mixed = plain_convolve(padded, peg_weight, peg_bias, bands, width)
    normed = plain_layer_norm(mixed, norm_gain, norm_bias)
    row_qkv = plain_project(normed, qkv_weight, qkv_bias, 0, row_features)
    arrived = lax.all_to_all(normed, "rows", split_axis=1, concat_axis=0, tiled=True)
    col_qkv = plain_project(arrived, qkv_weight, qkv_bias, row_features, model)
    row_heads = plain_attend(
        *row_qkv, ROW_HEADS, score_scale(width), "bld,bmd->blm", "blm,bmd->bld"
    )
    col_heads = plain_attend(
        *col_qkv, HEADS - ROW_HEADS, score_scale(height), "lbd,mbd->blm", "blm,mbd->lbd"
    )
    returned = lax.all_to_all(col_heads, "rows", split_axis=0, concat_axis=1, tiled=True)
    attended = jnp.concatenate([row_heads, returned], axis=2).reshape(bands * width, model)
    result = (
        mixed.reshape(bands * width, model).astype(jnp.float32)
        + jnp.dot(attended, out_weight, preferred_element_type=jnp.float32)
        + out_bias
    )
    return result.astype(jnp.bfloat16).reshape(bands, width, model)


def score_scale(count):
    return math.log(count) / (math.log(16.0) * math.sqrt(DH))


def interleave(first, second):
    upper = lax.broadcasted_iota(jnp.int32, first.shape, 0) < HALF
    low = jnp.where(upper, first, pltpu.roll(second, HALF, 0))
    high = jnp.where(upper, pltpu.roll(first, HALF, 0), second)
    return low, high


def pack_kernel(devices, per_step, tokens_ref, out_ref):
    _, width, model = tokens_ref.shape
    cols = width // devices
    slabs = model // LANES
    tiles = cols // HALF
    step = pl.program_id(0)
    place = lax.broadcasted_iota(jnp.int32, (SUB, LANES), 0)
    for k in range(per_step):
        dest = step * per_step + k
        start = pl.multiple_of(dest * cols, cols)
        left_start = pl.multiple_of(jnp.maximum(dest - 1, 0) * cols, cols)
        right_start = pl.multiple_of(jnp.minimum(dest + 1, devices - 1) * cols, cols)
        own = [tokens_ref[band, pl.ds(start, cols), :].astype(jnp.float32) for band in range(2)]
        for eight in range(cols // SUB):
            rows = slice(eight * SUB, (eight + 1) * SUB)
            pair = interleave(own[0][rows], own[1][rows])
            for which in range(2):
                tile = pair[which].astype(jnp.bfloat16)
                for slab in range(slabs):
                    base = (slab * tiles + eight * 2 + which) * SUB
                    out_ref[k, base : base + SUB, :] = tile[:, slab * LANES : (slab + 1) * LANES]
        lefts, rights = [], []
        for band in range(2):
            left = tokens_ref[band, pl.ds(left_start, cols), :].astype(jnp.float32)
            right = tokens_ref[band, pl.ds(right_start, cols), :].astype(jnp.float32)
            lefts.append(jnp.where(dest > 0, left[cols - 1 : cols], 0.0))
            rights.append(jnp.where(dest < devices - 1, right[0:1], 0.0))
        for two in range(slabs // 2):
            one = slice(2 * two * LANES, (2 * two + 1) * LANES)
            other = slice((2 * two + 1) * LANES, (2 * two + 2) * LANES)
            order = [rights[0][:, one], rights[0][:, other], lefts[0][:, other], lefts[0][:, one]]
            order += [rights[1][:, one], rights[1][:, other], lefts[1][:, other], lefts[1][:, one]]
            tile = jnp.broadcast_to(order[0], (SUB, LANES))
            for index in range(1, SUB):
                tile = jnp.where(place == index, order[index], tile)
            base = (slabs * tiles + two) * SUB
            out_ref[k, base : base + SUB, :] = tile.astype(jnp.bfloat16)


def pack(tokens, devices):
    bands, width, model = tokens.shape
    cols = width // devices
    slabs = model // LANES
    rows = slabs * bands * (cols + 2)
    per_step = 4
    return pl.pallas_call(
        functools.partial(pack_kernel, devices, per_step),
        grid=(devices // per_step,),
        in_specs=[pl.BlockSpec(memory_space=pltpu.VMEM)],
        out_specs=pl.BlockSpec((per_step, rows, LANES), lambda i: (i, 0, 0)),
        out_shape=jax.ShapeDtypeStruct((devices, rows, LANES), jnp.bfloat16),
        compiler_params=pltpu.CompilerParams(vmem_limit_bytes=6 * MIB),
        name="pack_columns",
    )(tokens)


def gate_kernel(*refs):
    pass


def gate(values, *after):
    hbm = pl.BlockSpec(memory_space=pltpu.HBM)
    anywhere = pl.BlockSpec(memory_space=pl.ANY)
    count = len(values)
    return pl.pallas_call(
        gate_kernel,
        in_specs=[hbm] * count + [anywhere] * len(after),
        out_specs=[hbm] * count,
        out_shape=[jax.ShapeDtypeStruct(value.shape, value.dtype) for value in values],
        input_output_aliases={index: index for index in range(count)},
        name="gate",
    )(*values, *after)


def in_hbm(value):
    return pltpu.with_memory_space_constraint(value, pltpu.HBM)


def normalise(values, gain, bias):
    center = jnp.mean(values, axis=-1, keepdims=True)
    shifted = values - center
    spread = jnp.mean(shifted * shifted, axis=-1, keepdims=True)
    return (shifted * lax.rsqrt(spread + EPS) * gain + bias).astype(jnp.bfloat16)


def attend_pair(query, key, value, scale, mask):
    count = query.shape[0]
    lane = lax.broadcasted_iota(jnp.int32, query.shape, 1)
    zero = jnp.zeros_like(query)
    both = jnp.concatenate(
        [jnp.where(lane < DH, query, zero), jnp.where(lane < DH, zero, query)], axis=0
    )
    scores = lax.dot_general(
        both, key, (((1,), (1,)), ((), ())), preferred_element_type=jnp.float32
    )
    if mask is not None:
        scores = jnp.where(mask, scores, -1e30)
    highest = jnp.max(scores, axis=-1, keepdims=True)
    probs = jnp.exp2((scores - highest) * (scale * LOG2E))
    total = jnp.sum(probs, axis=-1, keepdims=True)
    probs = (probs * (1.0 / total)).astype(jnp.bfloat16)
    mixed = jnp.dot(probs, value, preferred_element_type=jnp.float32)
    return jnp.where(lane < DH, mixed[:count], mixed[count:])


def weight_copies(qkv_hbm, weight_scr, sems, first):
    model = qkv_hbm.shape[0]
    width = weight_scr.shape[2]
    return [
        pltpu.make_async_copy(
            qkv_hbm.at[:, pl.ds(part * model + first, width)], weight_scr.at[part], sems.at[part]
        )
        for part in range(3)
    ]


def column_kernel(
    waits,
    recv_ref,
    edge_ref,
    peg_ref,
    peg_bias_ref,
    gain_ref,
    nbias_ref,
    qkv_bias_ref,
    qkv_hbm,
    *refs,
):
    out_ref, mixed_scr, normed_scr, qkv_scr, weight_scr, sems = refs[waits:]
    step = pl.program_id(0)
    devices = recv_ref.shape[0]
    tiles = recv_ref.shape[1] // (2 * SUB)
    height = 2 * devices
    first = ROW_HEADS * DH
    features = weight_scr.shape[2]
    group = devices * SUB

    @pl.when(step == 0)
    def _():
        for copy in weight_copies(qkv_hbm, weight_scr, sems, first):
            copy.start()

    place = lax.broadcasted_iota(jnp.int32, (1, 1, SUB, LANES), 2)
    upper = place < HALF
    column = lax.rem(place, HALF)

    def with_neighbours(value):
        swapped = pltpu.roll(value, HALF, 2)
        zero = jnp.zeros((1,) + value.shape[1:], jnp.float32)
        between = jnp.where(
            upper,
            jnp.concatenate([zero, swapped], axis=0),
            jnp.concatenate([swapped, zero], axis=0),
        )
        return between[:-1], value, between[1:]

    def stencil(triple, lanes, offset_col):
        total = None
        for offset_row in range(3):
            weight = peg_ref[offset_row, offset_col : offset_col + 1, lanes]
            term = triple[offset_row] * weight
            total = term if total is None else total + term
        return total

    edges = edge_ref[...].astype(jnp.float32).reshape(devices, 1, SUB, LANES)
    for local in range(2):
        lanes = slice(local * LANES, (local + 1) * LANES)
        own = recv_ref[:, local * tiles * SUB : (local + 1) * tiles * SUB, :]
        own = own.astype(jnp.float32).reshape(devices, tiles, SUB, LANES)
        triple = with_neighbours(own)
        if local == 0:
            left_edge = right_edge = with_neighbours(edges)
        else:
            left_edge = with_neighbours(pltpu.roll(edges, 1, 2))
            right_edge = with_neighbours(pltpu.roll(edges, SUB - 1, 2))
        wide = jnp.concatenate(
            [stencil(left_edge, lanes, 0), stencil(triple, lanes, 0)], axis=1
        )
        from_left = jnp.where(
            column == 0, pltpu.roll(wide[:, :-1], SUB - 3, 2), pltpu.roll(wide[:, 1:], 1, 2)
        )
        wide = jnp.concatenate(
            [stencil(triple, lanes, 2), stencil(right_edge, lanes, 2)], axis=1
        )
        from_right = jnp.where(
            column == HALF - 1,
            pltpu.roll(wide[:, 1:], 3, 2),
            pltpu.roll(wide[:, :-1], SUB - 1, 2),
        )
        total = (
            own + peg_bias_ref[:, lanes] + stencil(triple, lanes, 1) + from_left + from_right
        )
        mixed_scr[2 * step + local] = total.astype(jnp.bfloat16).astype(jnp.float32)

    @pl.when(step == pl.num_programs(0) - 1)
    def _():
        count = mixed_scr.shape[0]
        for tile in range(tiles):
            for start in range(0, devices, HALF):
                values = jnp.concatenate(
                    [
                        mixed_scr[slab, start : start + HALF, tile].reshape(HALF * SUB, LANES)
                        for slab in range(count)
                    ],
                    axis=1,
                )
                base = tile * group + start * SUB
                normed_scr[base : base + HALF * SUB, :] = normalise(
                    values, gain_ref[...], nbias_ref[...]
                )
        for part, copy in enumerate(weight_copies(qkv_hbm, weight_scr, sems, first)):
            copy.wait()
            projected = (
                jnp.dot(normed_scr[...], weight_scr[part], preferred_element_type=jnp.float32)
                + qkv_bias_ref[part : part + 1, :]
            )
            qkv_scr[part] = projected.astype(jnp.bfloat16)
        row_id = lax.broadcasted_iota(jnp.int32, (PAIR * group, group), 0)
        col_id = lax.broadcasted_iota(jnp.int32, (PAIR * group, group), 1)
        mask = lax.rem(row_id, HALF) == lax.rem(col_id, HALF)
        scale = score_scale(height)
        for tile in range(tiles):
            rows = slice(tile * group, (tile + 1) * group)
            for pair in range(features // LANES):
                lanes = slice(pair * LANES, (pair + 1) * LANES)
                heads = attend_pair(
                    qkv_scr[0, rows, lanes],
                    qkv_scr[1, rows, lanes],
                    qkv_scr[2, rows, lanes],
                    scale,
                    mask,
                )
                out_ref[:, tile, :, lanes] = heads.astype(jnp.bfloat16).reshape(
                    devices, SUB, LANES
                )


def column_part(recv, after, peg_weight, peg_bias, gain, nbias, qkv_weight, qkv_bias):
    devices, rows, _ = recv.shape
    model = gain.shape[-1]
    slabs = model // LANES
    cols = rows // (2 * slabs) - 2
    tiles = cols // HALF
    first = ROW_HEADS * DH
    features = model - first
    tokens = 2 * devices * cols
    whole2 = lambda i: (0, 0)
    steps = slabs // 2
    return pl.pallas_call(
        functools.partial(column_kernel, len(after)),
        grid=(steps,),
        in_specs=[
            pl.BlockSpec((devices, 2 * tiles * SUB, LANES), lambda i: (0, i, 0)),
            pl.BlockSpec((devices, SUB, LANES), lambda i: (0, slabs * tiles + i, 0)),
            pl.BlockSpec((3, 3, 2 * LANES), lambda i: (0, 0, i)),
            pl.BlockSpec((1, 2 * LANES), lambda i: (0, i)),
            pl.BlockSpec((1, model), whole2),
            pl.BlockSpec((1, model), whole2),
            pl.BlockSpec((3, features), whole2),
            pl.BlockSpec(memory_space=pltpu.HBM),
        ]
        + [pl.BlockSpec(memory_space=pltpu.HBM)] * len(after),
        out_specs=pl.BlockSpec((devices, tiles, SUB, features), lambda i: (0, 0, 0, 0)),
        out_shape=pltpu.HBM((devices, tiles, SUB, features), jnp.bfloat16),
        scratch_shapes=[
            pltpu.VMEM((slabs, devices, tiles, SUB, LANES), jnp.float32),
            pltpu.VMEM((tokens, model), jnp.bfloat16),
            pltpu.VMEM((3, tokens, features), jnp.bfloat16),
            pltpu.VMEM((3, model, features), jnp.bfloat16),
            pltpu.SemaphoreType.DMA((3,)),
        ],
        compiler_params=pltpu.CompilerParams(vmem_limit_bytes=20 * MIB),
        cost_estimate=pl.CostEstimate(
            flops=2 * tokens * model * 3 * features,
            transcendentals=tokens * LANES * features // DH,
            bytes_accessed=8 * MIB,
        ),
        name="column_heads",
    )(recv, recv, peg_weight, peg_bias, gain, nbias, qkv_bias[:, first:], in_hbm(qkv_weight), *map(in_hbm, after))


def row_kernel(
    tokens_ref,
    intra_ref,
    inter_ref,
    peg_ref,
    peg_bias_ref,
    gain_ref,
    nbias_ref,
    qkv_bias_ref,
    out_bias_ref,
    qkv_hbm,
    out_hbm,
    partial_ref,
    mixed_scr,
    normed_scr,
    qkv_scr,
    heads_scr,
    weight_scr,
    out_scr,
    sems,
):
    step = pl.program_id(0)
    slabs = pl.num_programs(0)
    bands, width, _ = tokens_ref.shape
    features = weight_scr.shape[2]

    def copies():
        copy = pltpu.make_async_copy(out_hbm.at[pl.ds(0, features), :], out_scr, sems.at[3])
        return weight_copies(qkv_hbm, weight_scr, sems, 0) + [copy]

    @pl.when(step == 0)
    def _():
        for copy in copies():
            copy.start()

    odd = lax.rem(lax.axis_index("rows"), 2) == 1
    intra = intra_ref[0].astype(jnp.float32)
    inter = inter_ref[0].astype(jnp.float32)
    rows = [jnp.where(odd, intra, inter)]
    rows += [tokens_ref[band].astype(jnp.float32) for band in range(bands)]
    rows += [jnp.where(odd, inter, intra)]
    position = lax.broadcasted_iota(jnp.int32, (width, LANES), 0)
    for band in range(bands):

        def stencil(offset_col):
            return (
                rows[band] * peg_ref[0, offset_col : offset_col + 1, :]
                + rows[band + 1] * peg_ref[1, offset_col : offset_col + 1, :]
                + rows[band + 2] * peg_ref[2, offset_col : offset_col + 1, :]
            )

        from_left = jnp.where(position == 0, 0.0, pltpu.roll(stencil(0), 1, 0))
        from_right = jnp.where(position == width - 1, 0.0, pltpu.roll(stencil(2), width - 1, 0))
        total = rows[band + 1] + peg_bias_ref[...] + stencil(1) + from_left + from_right
        mixed_scr[step, band * width : (band + 1) * width, :] = total.astype(
            jnp.bfloat16
        ).astype(jnp.float32)

    @pl.when(step == slabs - 1)
    def _():
        count = mixed_scr.shape[0]
        chunk = 64
        for start in range(0, bands * width, chunk):
            values = jnp.concatenate(
                [mixed_scr[slab, start : start + chunk, :] for slab in range(count)], axis=1
            )
            normed_scr[start : start + chunk, :] = normalise(
                values, gain_ref[...], nbias_ref[...]
            )
        waits = copies()
        for part in range(3):
            waits[part].wait()
            projected = (
                jnp.dot(normed_scr[...], weight_scr[part], preferred_element_type=jnp.float32)
                + qkv_bias_ref[part : part + 1, :]
            )
            qkv_scr[part] = projected.astype(jnp.bfloat16)
        scale = score_scale(width)
        for band in range(bands):
            span = slice(band * width, (band + 1) * width)
            for pair in range(features // LANES):
                lanes = slice(pair * LANES, (pair + 1) * LANES)
                heads_scr[span, lanes] = attend_pair(
                    qkv_scr[0, span, lanes],
                    qkv_scr[1, span, lanes],
                    qkv_scr[2, span, lanes],
                    scale,
                    None,
                ).astype(jnp.bfloat16)
        waits[3].wait()
        for slab in range(count):
            lanes = slice(slab * LANES, (slab + 1) * LANES)
            partial_ref[:, lanes] = (
                jnp.dot(heads_scr[...], out_scr[:, lanes], preferred_element_type=jnp.float32)
                + mixed_scr[slab]
                + out_bias_ref[:, lanes]
            )


def row_part(
    tokens,
    intra,
    inter,
    peg_weight,
    peg_bias,
    gain,
    nbias,
    qkv_weight,
    qkv_bias,
    out_weight,
    out_bias,
):
    bands, width, model = tokens.shape
    slabs = model // LANES
    features = ROW_HEADS * DH
    count = bands * width
    whole2 = lambda i: (0, 0)
    return pl.pallas_call(
        row_kernel,
        grid=(slabs,),
        in_specs=[
            pl.BlockSpec((bands, width, LANES), lambda i: (0, 0, i)),
            pl.BlockSpec((1, width, LANES), lambda i: (0, 0, i)),
            pl.BlockSpec((1, width, LANES), lambda i: (0, 0, i)),
            pl.BlockSpec((3, 3, LANES), lambda i: (0, 0, i)),
            pl.BlockSpec((1, LANES), lambda i: (0, i)),
            pl.BlockSpec((1, model), whole2),
            pl.BlockSpec((1, model), whole2),
            pl.BlockSpec((3, features), whole2),
            pl.BlockSpec((1, model), whole2),
            pl.BlockSpec(memory_space=pltpu.HBM),
            pl.BlockSpec(memory_space=pltpu.HBM),
        ],
        out_specs=pl.BlockSpec((count, model), whole2),
        out_shape=pltpu.HBM((count, model), jnp.float32),
        scratch_shapes=[
            pltpu.VMEM((slabs, count, LANES), jnp.float32),
            pltpu.VMEM((count, model), jnp.bfloat16),
            pltpu.VMEM((3, count, features), jnp.bfloat16),
            pltpu.VMEM((count, features), jnp.bfloat16),
            pltpu.VMEM((3, model, features), jnp.bfloat16),
            pltpu.VMEM((features, model), jnp.bfloat16),
            pltpu.SemaphoreType.DMA((4,)),
        ],
        compiler_params=pltpu.CompilerParams(vmem_limit_bytes=20 * MIB),
        cost_estimate=pl.CostEstimate(
            flops=40 * count * model * 4 * features,
            transcendentals=count * width * ROW_HEADS,
            bytes_accessed=10 * 1024 * 1024,
        ),
        name="row_heads",
    )(
        tokens,
        intra,
        inter,
        peg_weight,
        peg_bias,
        gain,
        nbias,
        qkv_bias[:, :features],
        out_bias,
        in_hbm(qkv_weight),
        in_hbm(out_weight),
    )


def last_kernel(partial_ref, heads_ref, out_weight_ref, result_ref):
    devices, tiles, sub, features = heads_ref.shape
    _, width, model = result_ref.shape
    first = ROW_HEADS * DH
    heads = heads_ref[...].reshape(devices * tiles * sub, features)
    upper = lax.broadcasted_iota(jnp.int32, (1, sub, 2 * LANES), 1) < HALF
    start = pl.multiple_of(pl.program_id(0) * width, width)
    for slab in range(model // (2 * LANES)):
        lanes = slice(slab * 2 * LANES, (slab + 1) * 2 * LANES)
        projected = jnp.dot(
            heads, out_weight_ref[first:, lanes], preferred_element_type=jnp.float32
        )
        pairs = projected.reshape(devices * tiles // 2, 2, sub, 2 * LANES)
        low, high = pairs[:, 0], pairs[:, 1]
        rows = (
            jnp.where(upper, low, pltpu.roll(high, HALF, 1)),
            jnp.where(upper, pltpu.roll(low, HALF, 1), high),
        )
        for band, value in enumerate(rows):
            result_ref[band, :, lanes] = (
                partial_ref[band, pl.ds(start, width), lanes]
                + value.reshape(width, 2 * LANES)
            ).astype(jnp.bfloat16)


def last_part(partial, heads, out_weight, bands, width):
    devices, tiles, sub, features = heads.shape
    model = out_weight.shape[1]
    steps = 4
    vmem = pl.BlockSpec(memory_space=pltpu.VMEM)
    return pl.pallas_call(
        last_kernel,
        grid=(steps,),
        in_specs=[
            vmem,
            pl.BlockSpec((devices // steps, tiles, sub, features), lambda i: (i, 0, 0, 0)),
            vmem,
        ],
        out_specs=pl.BlockSpec((bands, width // steps, model), lambda i: (0, i, 0)),
        out_shape=jax.ShapeDtypeStruct((bands, width, model), jnp.bfloat16),
        compiler_params=pltpu.CompilerParams(vmem_limit_bytes=8 * MIB),
        cost_estimate=pl.CostEstimate(
            flops=2 * bands * width * features * model,
            transcendentals=0,
            bytes_accessed=5 * MIB,
        ),
        name="last_projection",
    )(partial.reshape(bands, width, model), heads, out_weight)


def on_device(
    tokens, peg_weight, peg_bias, norm_gain, norm_bias, qkv_weight, qkv_bias, out_weight, out_bias
):
    devices = lax.axis_size("rows")
    bands, width, model = tokens.shape
    cols = width // devices
    fits = (
        bands == 2
        and width % LANES == 0
        and cols % 16 == 0
        and devices * SUB == LANES
        and model == 2 * ROW_HEADS * DH
        and model % LANES == 0
    )
    if not fits:
        return plain(
            tokens,
            peg_weight,
            peg_bias,
            norm_gain,
            norm_bias,
            qkv_weight,
            qkv_bias,
            out_weight,
            out_bias,
        )
    peg_bias = peg_bias.reshape(1, model)
    gain = norm_gain.reshape(1, model)
    nbias = norm_bias.reshape(1, model)
    out_bias = out_bias.reshape(1, model)
    qkv_bias = qkv_bias.reshape(3, model)

    packed = pack(tokens, devices)
    odd = lax.rem(lax.axis_index("rows"), 2)
    intra = lax.dynamic_slice_in_dim(tokens, 1 - odd, 1, axis=0)
    inter = lax.dynamic_slice_in_dim(tokens, odd, 1, axis=0)
    same_chip = [(i, i ^ 1) for i in range(devices)]
    other_chip = [(i, i + 1 if i % 2 else i - 1) for i in range(1, devices - 1)]
    intra = lax.ppermute(intra, "rows", same_chip)
    inter = lax.ppermute(inter, "rows", other_chip)
    received = lax.all_to_all(packed, "rows", split_axis=0, concat_axis=0, tiled=True)
    partial = row_part(
        tokens,
        in_hbm(intra),
        in_hbm(inter),
        peg_weight,
        peg_bias,
        gain,
        nbias,
        qkv_weight,
        qkv_bias,
        out_weight,
        out_bias,
    )
    col_heads = column_part(
        received, (partial,), peg_weight, peg_bias, gain, nbias, qkv_weight, qkv_bias
    )
    returned = lax.all_to_all(col_heads, "rows", split_axis=0, concat_axis=0, tiled=True)
    return last_part(partial, returned, out_weight, bands, width)


def solution(mesh):
    placed = (P(("groups", "rows"), None, None), P(), P(), P(), P(), P(), P(), P(), P())
    return jax.shard_map(
        on_device,
        mesh=mesh,
        in_specs=placed,
        out_specs=P(("groups", "rows"), None, None),
        check_vma=False,
    )
```

```python
import functools
import math

import jax
import jax.numpy as jnp
from jax import lax
from jax.experimental import pallas as pl
from jax.experimental.pallas import tpu as pltpu
from jax.sharding import PartitionSpec as P

HEADS = 16
DH = 64
ROW_HEADS = 8
LANES = 128
SUB = 8
HALF = SUB // 2
PAIR = LANES // DH
EPS = 1e-06
LOG2E = math.log2(math.e)
MIB = 1024 * 1024


def halo_rows(tokens):
    devices, bands = lax.axis_size("rows"), tokens.shape[0]
    up = [(i, i + 1) for i in range(devices - 1)]
    down = [(j, i) for i, j in up]
    before = lax.ppermute(tokens[bands - 1 :], "rows", up)
    after = lax.ppermute(tokens[:1], "rows", down)
    return before, after


def plain_convolve(padded, peg_weight, peg_bias, count_rows, count_cols):
    total = padded[1 : count_rows + 1, 1 : count_cols + 1, :].astype(jnp.float32) + peg_bias
    for offset_row in range(3):
        for offset_col in range(3):
            piece = padded[
                offset_row : offset_row + count_rows, offset_col : offset_col + count_cols, :
            ]
            total = total + piece.astype(jnp.float32) * peg_weight[offset_row, offset_col]
    return total.astype(jnp.bfloat16)


def plain_layer_norm(mixed, norm_gain, norm_bias):
    values = mixed.astype(jnp.float32)
    center = jnp.mean(values, axis=-1, keepdims=True)
    spread = jnp.mean((values - center) ** 2, axis=-1, keepdims=True)
    return ((values - center) * lax.rsqrt(spread + EPS) * norm_gain + norm_bias).astype(
        jnp.bfloat16
    )


def plain_project(normed, qkv_weight, qkv_bias, first_col, last_col):
    model = normed.shape[-1]
    flat_rows = normed.reshape(-1, model)
    outputs = []
    for part_index in range(3):
        lower = part_index * model + first_col
        upper = part_index * model + last_col
        projected = (
            jnp.dot(flat_rows, qkv_weight[:, lower:upper], preferred_element_type=jnp.float32)
            + qkv_bias[lower:upper]
        )
        outputs.append(
            projected.astype(jnp.bfloat16).reshape(normed.shape[:-1] + (last_col - first_col,))
        )
    return outputs


def plain_attend(query, key, value, head_count, tau, scoring, mixing):
    outputs = []
    for head in range(head_count):
        cols = slice(head * DH, (head + 1) * DH)
        logits = (
            jnp.einsum(
                scoring, query[..., cols], key[..., cols], preferred_element_type=jnp.float32
            )
            * tau
        )
        probs = jnp.exp(logits - jnp.max(logits, axis=-1, keepdims=True))
        probs = (probs / jnp.sum(probs, axis=-1, keepdims=True)).astype(jnp.bfloat16)
        outputs.append(
            jnp.einsum(
                mixing, probs, value[..., cols], preferred_element_type=jnp.float32
            ).astype(jnp.bfloat16)
        )
    return jnp.concatenate(outputs, axis=-1)


def plain(
    tokens, peg_weight, peg_bias, norm_gain, norm_bias, qkv_weight, qkv_bias, out_weight, out_bias
):
    bands, width, model = tokens.shape
    height = bands * lax.axis_size("rows")
    row_features = ROW_HEADS * DH
    before, after = halo_rows(tokens)
    padded = jnp.pad(
        jnp.concatenate([before, tokens, after], axis=0), ((0, 0), (1, 1), (0, 0))
    )
    mixed = plain_convolve(padded, peg_weight, peg_bias, bands, width)
    normed = plain_layer_norm(mixed, norm_gain, norm_bias)
    row_qkv = plain_project(normed, qkv_weight, qkv_bias, 0, row_features)
    arrived = lax.all_to_all(normed, "rows", split_axis=1, concat_axis=0, tiled=True)
    col_qkv = plain_project(arrived, qkv_weight, qkv_bias, row_features, model)
    row_heads = plain_attend(
        *row_qkv, ROW_HEADS, score_scale(width), "bld,bmd->blm", "blm,bmd->bld"
    )
    col_heads = plain_attend(
        *col_qkv, HEADS - ROW_HEADS, score_scale(height), "lbd,mbd->blm", "blm,mbd->lbd"
    )
    returned = lax.all_to_all(col_heads, "rows", split_axis=0, concat_axis=1, tiled=True)
    attended = jnp.concatenate([row_heads, returned], axis=2).reshape(bands * width, model)
    result = (
        mixed.reshape(bands * width, model).astype(jnp.float32)
        + jnp.dot(attended, out_weight, preferred_element_type=jnp.float32)
        + out_bias
    )
    return result.astype(jnp.bfloat16).reshape(bands, width, model)


def score_scale(count):
    return math.log(count) / (math.log(16.0) * math.sqrt(DH))


def interleave(first, second):
    upper = lax.broadcasted_iota(jnp.int32, first.shape, 0) < HALF
    low = jnp.where(upper, first, pltpu.roll(second, HALF, 0))
    high = jnp.where(upper, pltpu.roll(first, HALF, 0), second)
    return low, high


def pack_kernel(devices, per_step, tokens_ref, out_hbm, out_scr, sems):
    _, width, model = tokens_ref.shape
    cols = width // devices
    slabs = model // LANES
    tiles = cols // HALF
    place = lax.broadcasted_iota(jnp.int32, (SUB, LANES), 0)

    def copy(dest):
        return pltpu.make_async_copy(out_scr.at[dest], out_hbm.at[dest], sems.at[dest])

    def fill(dest):
        start = pl.multiple_of(dest * cols, cols)
        left_start = pl.multiple_of(jnp.maximum(dest - 1, 0) * cols, cols)
        right_start = pl.multiple_of(jnp.minimum(dest + 1, devices - 1) * cols, cols)
        own = [tokens_ref[band, pl.ds(start, cols), :].astype(jnp.float32) for band in range(2)]
        for eight in range(cols // SUB):
            rows = slice(eight * SUB, (eight + 1) * SUB)
            pair = interleave(own[0][rows], own[1][rows])
            for which in range(2):
                tile = pair[which].astype(jnp.bfloat16)
                for slab in range(slabs):
                    base = (slab * tiles + eight * 2 + which) * SUB
                    out_scr[dest, base : base + SUB, :] = tile[:, slab * LANES : (slab + 1) * LANES]
        lefts, rights = [], []
        for band in range(2):
            left = tokens_ref[band, pl.ds(left_start, cols), :].astype(jnp.float32)
            right = tokens_ref[band, pl.ds(right_start, cols), :].astype(jnp.float32)
            lefts.append(jnp.where(dest > 0, left[cols - 1 : cols], 0.0))
            rights.append(jnp.where(dest < devices - 1, right[0:1], 0.0))
        for two in range(slabs // 2):
            one = slice(2 * two * LANES, (2 * two + 1) * LANES)
            other = slice((2 * two + 1) * LANES, (2 * two + 2) * LANES)
            order = [rights[0][:, one], rights[0][:, other], lefts[0][:, other], lefts[0][:, one]]
            order += [rights[1][:, one], rights[1][:, other], lefts[1][:, other], lefts[1][:, one]]
            tile = jnp.broadcast_to(order[0], (SUB, LANES))
            for index in range(1, SUB):
                tile = jnp.where(place == index, order[index], tile)
            base = (slabs * tiles + two) * SUB
            out_scr[dest, base : base + SUB, :] = tile.astype(jnp.bfloat16)

    def send(step, carry):
        for k in range(per_step):
            fill(step * per_step + k)
            copy(step * per_step + k).start()
        return carry

    def finish(dest, carry):
        copy(dest).wait()
        return carry

    lax.fori_loop(0, devices // per_step, send, 0)
    lax.fori_loop(0, devices, finish, 0)


def pack(tokens, devices):
    bands, width, model = tokens.shape
    cols = width // devices
    slabs = model // LANES
    rows = slabs * bands * (cols + 2)
    per_step = 4
    return pl.pallas_call(
        functools.partial(pack_kernel, devices, per_step),
        in_specs=[pl.BlockSpec(memory_space=pltpu.VMEM)],
        out_specs=pl.BlockSpec(memory_space=pltpu.HBM),
        out_shape=jax.ShapeDtypeStruct((devices, rows, LANES), jnp.bfloat16),
        scratch_shapes=[
            pltpu.VMEM((devices, rows, LANES), jnp.bfloat16),
            pltpu.SemaphoreType.DMA((devices,)),
        ],
        compiler_params=pltpu.CompilerParams(vmem_limit_bytes=6 * MIB),
        name="pack_columns",
    )(tokens)


def gate_kernel(*refs):
    pass


def gate(values, *after):
    hbm = pl.BlockSpec(memory_space=pltpu.HBM)
    anywhere = pl.BlockSpec(memory_space=pl.ANY)
    count = len(values)
    return pl.pallas_call(
        gate_kernel,
        in_specs=[hbm] * count + [anywhere] * len(after),
        out_specs=[hbm] * count,
        out_shape=[jax.ShapeDtypeStruct(value.shape, value.dtype) for value in values],
        input_output_aliases={index: index for index in range(count)},
        name="gate",
    )(*values, *after)


def in_hbm(value):
    return pltpu.with_memory_space_constraint(value, pltpu.HBM)


def normalise(values, gain, bias):
    center = jnp.mean(values, axis=-1, keepdims=True)
    shifted = values - center
    spread = jnp.mean(shifted * shifted, axis=-1, keepdims=True)
    return (shifted * lax.rsqrt(spread + EPS) * gain + bias).astype(jnp.bfloat16)


def attend_pair(query, key, value, scale, mask):
    count = query.shape[0]
    lane = lax.broadcasted_iota(jnp.int32, query.shape, 1)
    zero = jnp.zeros_like(query)
    both = jnp.concatenate(
        [jnp.where(lane < DH, query, zero), jnp.where(lane < DH, zero, query)], axis=0
    )
    scores = lax.dot_general(
        both, key, (((1,), (1,)), ((), ())), preferred_element_type=jnp.float32
    )
    if mask is not None:
        scores = jnp.where(mask, scores.reshape((-1,) + mask.shape[1:]), -1e30)
        scores = scores.reshape(PAIR * count, -1)
    highest = jnp.max(scores, axis=-1, keepdims=True)
    probs = jnp.exp2((scores - highest) * (scale * LOG2E))
    total = jnp.sum(probs, axis=-1, keepdims=True)
    probs = (probs * (1.0 / total)).astype(jnp.bfloat16)
    mixed = jnp.dot(probs, value, preferred_element_type=jnp.float32)
    return jnp.where(lane < DH, mixed[:count], mixed[count:])


def weight_copies(qkv_hbm, weight_scr, sems, first):
    model = qkv_hbm.shape[0]
    width = weight_scr.shape[2]
    pieces = sems.shape[1]
    depth = model // pieces
    return [
        [
            pltpu.make_async_copy(
                qkv_hbm.at[pl.ds(piece * depth, depth), pl.ds(part * model + first, width)],
                weight_scr.at[part, pl.ds(piece * depth, depth)],
                sems.at[part, piece],
            )
            for piece in range(pieces)
        ]
        for part in range(3)
    ]


def column_kernel(
    recv_ref,
    peg_ref,
    peg_bias_ref,
    gain_ref,
    nbias_ref,
    qkv_bias_ref,
    qkv_hbm,
    *refs,
):
    out_ref, mixed_scr, normed_scr, qkv_scr, weight_scr, sems = refs[-6:]

    devices = recv_ref.shape[0]
    slabs, _, tiles, _, _ = mixed_scr.shape
    height = 2 * devices
    first = ROW_HEADS * DH
    features = weight_scr.shape[2]
    group = devices * SUB

    weights = weight_copies(qkv_hbm, weight_scr, sems, first)
    for copies in weights:
        for copy in copies:
            copy.start()

    place = lax.broadcasted_iota(jnp.int32, (SUB, LANES), 0)
    upper = place < HALF
    column = lax.rem(place, HALF)
    zero = jnp.zeros((SUB, LANES), jnp.float32)

    def convolve_slab(slab, base, edge_base, local):
        lanes = pl.ds(pl.multiple_of(slab * LANES, LANES), LANES)
        weights = [
            [jnp.broadcast_to(peg_ref[a, b : b + 1, lanes], (SUB, LANES)) for b in range(3)]
            for a in range(3)
        ]
        weights[1][1] = weights[1][1] + 1.0
        bias = jnp.broadcast_to(peg_bias_ref[:, lanes], (SUB, LANES))

        def load(device):
            own = [
                recv_ref[device, pl.ds(pl.multiple_of(base + tile * SUB, SUB), SUB), :].astype(
                    jnp.float32
                )
                for tile in range(tiles)
            ]
            edge = recv_ref[device, pl.ds(pl.multiple_of(edge_base, SUB), SUB), :]
            edge = edge.astype(jnp.float32)
            if local == 0:
                return [edge] + own + [edge]
            return [pltpu.roll(edge, 1, 0)] + own + [pltpu.roll(edge, SUB - 1, 0)]

        swapped = [zero] * (tiles + 2)
        values = load(0)
        following = [pltpu.roll(value, HALF, 0) for value in values]
        above = [jnp.where(upper, p, n) for p, n in zip(swapped, following)]
        for device in range(devices):
            swapped = following
            if device + 1 < devices:
                coming = load(device + 1)
                following = [pltpu.roll(value, HALF, 0) for value in coming]
            else:
                coming, following = None, [zero] * (tiles + 2)
            below = [jnp.where(upper, p, n) for p, n in zip(swapped, following)]

            def stencil(index, offset):
                return (
                    above[index] * weights[0][offset]
                    + values[index] * weights[1][offset]
                    + below[index] * weights[2][offset]
                )

            lefts = [stencil(index, 0) for index in range(tiles + 1)]
            rights = [stencil(index, 2) for index in range(1, tiles + 2)]
            for tile in range(tiles):
                from_left = jnp.where(
                    column == 0,
                    pltpu.roll(lefts[tile], SUB - 3, 0),
                    pltpu.roll(lefts[tile + 1], 1, 0),
                )
                from_right = jnp.where(
                    column == HALF - 1,
                    pltpu.roll(rights[tile + 1], 3, 0),
                    pltpu.roll(rights[tile], SUB - 1, 0),
                )
                total = (stencil(tile + 1, 1) + bias) + (from_left + from_right)
                mixed_scr[slab, device, tile] = total.astype(jnp.bfloat16).astype(jnp.float32)
            values, above = coming, below

    def two_slabs(two, carry):
        for local in range(2):
            slab = 2 * two + local
            convolve_slab(slab, slab * tiles * SUB, (slabs * tiles + two) * SUB, local)
        return carry

    lax.fori_loop(0, slabs // 2, two_slabs, 0)

    row_id = lax.broadcasted_iota(jnp.int32, (1, SUB, group), 1)
    col_id = lax.broadcasted_iota(jnp.int32, (1, SUB, group), 2)
    mask = lax.rem(row_id, HALF) == lax.rem(col_id, HALF)
    scale = score_scale(height)
    block = 2 * group
    for half in range(tiles // 2):
        for tile in range(2 * half, 2 * half + 2):
            for start in range(0, devices, HALF):
                values = jnp.concatenate(
                    [
                        mixed_scr[slab, start : start + HALF, tile].reshape(
                            HALF * SUB, LANES
                        )
                        for slab in range(slabs)
                    ],
                    axis=1,
                )
                base = tile * group + start * SUB
                normed_scr[base : base + HALF * SUB, :] = normalise(
                    values, gain_ref[...], nbias_ref[...]
                )
        span = slice(half * block, (half + 1) * block)
        for part in range(3):
            if half == 0:
                for copy in weights[part]:
                    copy.wait()
            projected = (
                jnp.dot(
                    normed_scr[span, :],
                    weight_scr[part],
                    preferred_element_type=jnp.float32,
                )
                + qkv_bias_ref[part : part + 1, :]
            )
            qkv_scr[part, span, :] = projected.astype(jnp.bfloat16)
        for tile in range(2 * half, 2 * half + 2):
            rows = slice(tile * group, (tile + 1) * group)
            for pair in range(features // LANES):
                lanes = slice(pair * LANES, (pair + 1) * LANES)
                heads = attend_pair(
                    qkv_scr[0, rows, lanes],
                    qkv_scr[1, rows, lanes],
                    qkv_scr[2, rows, lanes],
                    scale,
                    mask,
                )
                out_ref[:, tile, :, lanes] = heads.astype(jnp.bfloat16).reshape(
                    devices, SUB, LANES
                )


def column_part(recv, after, peg_weight, peg_bias, gain, nbias, qkv_weight, qkv_bias):
    devices, rows, _ = recv.shape
    model = gain.shape[-1]
    slabs = model // LANES
    cols = rows // (2 * slabs) - 2
    tiles = cols // HALF
    first = ROW_HEADS * DH
    features = model - first
    tokens = 2 * devices * cols
    vmem = pl.BlockSpec(memory_space=pltpu.VMEM)
    return pl.pallas_call(
        column_kernel,
        in_specs=[vmem] * 6 + [pl.BlockSpec(memory_space=pltpu.HBM)] * (1 + len(after)),
        out_specs=vmem,
        out_shape=pltpu.HBM((devices, tiles, SUB, features), jnp.bfloat16),
        scratch_shapes=[
            pltpu.VMEM((slabs, devices, tiles, SUB, LANES), jnp.float32),
            pltpu.VMEM((tokens, model), jnp.bfloat16),
            pltpu.VMEM((3, tokens, features), jnp.bfloat16),
            pltpu.VMEM((3, model, features), jnp.bfloat16),
            pltpu.SemaphoreType.DMA((3, 1)),
        ],
        compiler_params=pltpu.CompilerParams(vmem_limit_bytes=9 * MIB),
        cost_estimate=pl.CostEstimate(
            flops=2 * tokens * model * 3 * features,
            transcendentals=tokens * LANES * features // DH,
            bytes_accessed=8 * MIB,
        ),
        name="column_heads",
    )(
        recv,
        peg_weight,
        peg_bias,
        gain,
        nbias,
        qkv_bias[:, first:],
        in_hbm(qkv_weight),
        *map(in_hbm, after),
    )


def row_kernel(
    tokens_ref,
    intra_ref,
    inter_ref,
    peg_ref,
    peg_bias_ref,
    gain_ref,
    nbias_ref,
    qkv_bias_ref,
    out_bias_ref,
    qkv_hbm,
    out_hbm,
    partial_ref,
    mixed_scr,
    normed_scr,
    qkv_scr,
    heads_scr,
    weight_scr,
    out_scr,
    sems,
    out_sem,
):
    step = pl.program_id(0)
    slabs = pl.num_programs(0)
    bands, width, _ = tokens_ref.shape
    features = weight_scr.shape[2]

    def copies():
        copy = pltpu.make_async_copy(out_hbm.at[pl.ds(0, features), :], out_scr, out_sem)
        return weight_copies(qkv_hbm, weight_scr, sems, 0) + [[copy]]

    @pl.when(step == 0)
    def _():
        for group in copies():
            for copy in group:
                copy.start()

    odd = lax.rem(lax.axis_index("rows"), 2) == 1
    intra = intra_ref[0].astype(jnp.float32)
    inter = inter_ref[0].astype(jnp.float32)
    rows = [jnp.where(odd, intra, inter)]
    rows += [tokens_ref[band].astype(jnp.float32) for band in range(bands)]
    rows += [jnp.where(odd, inter, intra)]
    position = lax.broadcasted_iota(jnp.int32, (width, LANES), 0)
    for band in range(bands):

        def stencil(offset_col):
            return (
                rows[band] * peg_ref[0, offset_col : offset_col + 1, :]
                + rows[band + 1] * peg_ref[1, offset_col : offset_col + 1, :]
                + rows[band + 2] * peg_ref[2, offset_col : offset_col + 1, :]
            )

        from_left = jnp.where(position == 0, 0.0, pltpu.roll(stencil(0), 1, 0))
        from_right = jnp.where(position == width - 1, 0.0, pltpu.roll(stencil(2), width - 1, 0))
        total = rows[band + 1] + peg_bias_ref[...] + stencil(1) + from_left + from_right
        mixed_scr[step, band * width : (band + 1) * width, :] = total.astype(
            jnp.bfloat16
        ).astype(jnp.float32)

    @pl.when(step == slabs - 1)
    def _():
        count = mixed_scr.shape[0]
        chunk = 64
        for start in range(0, bands * width, chunk):
            values = jnp.concatenate(
                [mixed_scr[slab, start : start + chunk, :] for slab in range(count)], axis=1
            )
            normed_scr[start : start + chunk, :] = normalise(
                values, gain_ref[...], nbias_ref[...]
            )
        waits = copies()
        for part in range(3):
            for copy in waits[part]:
                copy.wait()
            projected = (
                jnp.dot(normed_scr[...], weight_scr[part], preferred_element_type=jnp.float32)
                + qkv_bias_ref[part : part + 1, :]
            )
            qkv_scr[part] = projected.astype(jnp.bfloat16)
        scale = score_scale(width)
        for band in range(bands):
            span = slice(band * width, (band + 1) * width)
            for pair in range(features // LANES):
                lanes = slice(pair * LANES, (pair + 1) * LANES)
                heads_scr[span, lanes] = attend_pair(
                    qkv_scr[0, span, lanes],
                    qkv_scr[1, span, lanes],
                    qkv_scr[2, span, lanes],
                    scale,
                    None,
                ).astype(jnp.bfloat16)
        waits[3][0].wait()
        for slab in range(count):
            lanes = slice(slab * LANES, (slab + 1) * LANES)
            partial_ref[:, lanes] = (
                jnp.dot(heads_scr[...], out_scr[:, lanes], preferred_element_type=jnp.float32)
                + mixed_scr[slab]
                + out_bias_ref[:, lanes]
            )


def row_part(
    tokens,
    intra,
    inter,
    peg_weight,
    peg_bias,
    gain,
    nbias,
    qkv_weight,
    qkv_bias,
    out_weight,
    out_bias,
):
    bands, width, model = tokens.shape
    slabs = model // LANES
    features = ROW_HEADS * DH
    count = bands * width
    whole2 = lambda i: (0, 0)
    return pl.pallas_call(
        row_kernel,
        grid=(slabs,),
        in_specs=[
            pl.BlockSpec((bands, width, LANES), lambda i: (0, 0, i)),
            pl.BlockSpec((1, width, LANES), lambda i: (0, 0, i)),
            pl.BlockSpec((1, width, LANES), lambda i: (0, 0, i)),
            pl.BlockSpec((3, 3, LANES), lambda i: (0, 0, i)),
            pl.BlockSpec((1, LANES), lambda i: (0, i)),
            pl.BlockSpec((1, model), whole2),
            pl.BlockSpec((1, model), whole2),
            pl.BlockSpec((3, features), whole2),
            pl.BlockSpec((1, model), whole2),
            pl.BlockSpec(memory_space=pltpu.HBM),
            pl.BlockSpec(memory_space=pltpu.HBM),
        ],
        out_specs=pl.BlockSpec((count, model), whole2),
        out_shape=pltpu.HBM((count, model), jnp.float32),
        scratch_shapes=[
            pltpu.VMEM((slabs, count, LANES), jnp.float32),
            pltpu.VMEM((count, model), jnp.bfloat16),
            pltpu.VMEM((3, count, features), jnp.bfloat16),
            pltpu.VMEM((count, features), jnp.bfloat16),
            pltpu.VMEM((3, model, features), jnp.bfloat16),
            pltpu.VMEM((features, model), jnp.bfloat16),
            pltpu.SemaphoreType.DMA((3, 4)),
            pltpu.SemaphoreType.DMA,
        ],
        compiler_params=pltpu.CompilerParams(vmem_limit_bytes=14 * MIB),
        cost_estimate=pl.CostEstimate(
            flops=40 * count * model * 4 * features,
            transcendentals=count * width * ROW_HEADS,
            bytes_accessed=10 * 1024 * 1024,
        ),
        name="row_heads",
    )(
        tokens,
        intra,
        inter,
        peg_weight,
        peg_bias,
        gain,
        nbias,
        qkv_bias[:, :features],
        out_bias,
        in_hbm(qkv_weight),
        in_hbm(out_weight),
    )


def last_kernel(partial_ref, heads_ref, out_weight_ref, result_ref):
    devices, tiles, sub, features = heads_ref.shape
    _, width, model = result_ref.shape
    first = ROW_HEADS * DH
    heads = heads_ref[...].reshape(devices * tiles * sub, features)
    upper = lax.broadcasted_iota(jnp.int32, (1, sub, 2 * LANES), 1) < HALF
    start = pl.multiple_of(pl.program_id(0) * width, width)
    for slab in range(model // (2 * LANES)):
        lanes = slice(slab * 2 * LANES, (slab + 1) * 2 * LANES)
        projected = jnp.dot(
            heads, out_weight_ref[first:, lanes], preferred_element_type=jnp.float32
        )
        pairs = projected.reshape(devices * tiles // 2, 2, sub, 2 * LANES)
        low, high = pairs[:, 0], pairs[:, 1]
        rows = (
            jnp.where(upper, low, pltpu.roll(high, HALF, 1)),
            jnp.where(upper, pltpu.roll(low, HALF, 1), high),
        )
        for band, value in enumerate(rows):
            result_ref[band, :, lanes] = (
                partial_ref[band, pl.ds(start, width), lanes]
                + value.reshape(width, 2 * LANES)
            ).astype(jnp.bfloat16)


def last_part(partial, heads, out_weight, bands, width):
    devices, tiles, sub, features = heads.shape
    model = out_weight.shape[1]
    steps = 4
    vmem = pl.BlockSpec(memory_space=pltpu.VMEM)
    return pl.pallas_call(
        last_kernel,
        grid=(steps,),
        in_specs=[
            vmem,
            pl.BlockSpec((devices // steps, tiles, sub, features), lambda i: (i, 0, 0, 0)),
            vmem,
        ],
        out_specs=pl.BlockSpec((bands, width // steps, model), lambda i: (0, i, 0)),
        out_shape=jax.ShapeDtypeStruct((bands, width, model), jnp.bfloat16),
        compiler_params=pltpu.CompilerParams(vmem_limit_bytes=8 * MIB),
        cost_estimate=pl.CostEstimate(
            flops=2 * bands * width * features * model,
            transcendentals=0,
            bytes_accessed=5 * MIB,
        ),
        name="last_projection",
    )(partial.reshape(bands, width, model), heads, out_weight)


def on_device(
    tokens, peg_weight, peg_bias, norm_gain, norm_bias, qkv_weight, qkv_bias, out_weight, out_bias
):
    devices = lax.axis_size("rows")
    bands, width, model = tokens.shape
    cols = width // devices
    fits = (
        bands == 2
        and width % LANES == 0
        and cols % 16 == 0
        and devices * SUB == LANES
        and model == 2 * ROW_HEADS * DH
        and model % LANES == 0
    )
    if not fits:
        return plain(
            tokens,
            peg_weight,
            peg_bias,
            norm_gain,
            norm_bias,
            qkv_weight,
            qkv_bias,
            out_weight,
            out_bias,
        )
    peg_bias = peg_bias.reshape(1, model)
    gain = norm_gain.reshape(1, model)
    nbias = norm_bias.reshape(1, model)
    out_bias = out_bias.reshape(1, model)
    qkv_bias = qkv_bias.reshape(3, model)

    packed = pack(tokens, devices)
    odd = lax.rem(lax.axis_index("rows"), 2)
    intra = lax.dynamic_slice_in_dim(tokens, 1 - odd, 1, axis=0)
    inter = lax.dynamic_slice_in_dim(tokens, odd, 1, axis=0)
    same_chip = [(i, i ^ 1) for i in range(devices)]
    other_chip = [(i, i + 1 if i % 2 else i - 1) for i in range(1, devices - 1)]
    intra = lax.ppermute(intra, "rows", same_chip)
    inter = lax.ppermute(inter, "rows", other_chip)
    received = lax.all_to_all(packed, "rows", split_axis=0, concat_axis=0, tiled=True)
    partial = row_part(
        tokens,
        in_hbm(intra),
        in_hbm(inter),
        peg_weight,
        peg_bias,
        gain,
        nbias,
        qkv_weight,
        qkv_bias,
        out_weight,
        out_bias,
    )
    col_heads = column_part(
        received, (partial,), peg_weight, peg_bias, gain, nbias, qkv_weight, qkv_bias
    )
    returned = lax.all_to_all(col_heads, "rows", split_axis=0, concat_axis=0, tiled=True)
    return last_part(partial, returned, out_weight, bands, width)


def solution(mesh):
    placed = (P(("groups", "rows"), None, None), P(), P(), P(), P(), P(), P(), P(), P())
    return jax.shard_map(
        on_device,
        mesh=mesh,
        in_specs=placed,
        out_specs=P(("groups", "rows"), None, None),
        check_vma=False,
    )
```

```python
import functools
import math

import jax
import jax.numpy as jnp
from jax import lax
from jax.experimental import pallas as pl
from jax.experimental.pallas import tpu as pltpu
from jax.sharding import PartitionSpec as P

HEADS = 16
DH = 64
ROW_HEADS = 8
LANES = 128
SUB = 8
HALF = SUB // 2
PAIR = LANES // DH
EPS = 1e-06
LOG2E = math.log2(math.e)
MIB = 1024 * 1024


def halo_rows(tokens):
    devices, bands = lax.axis_size("rows"), tokens.shape[0]
    up = [(i, i + 1) for i in range(devices - 1)]
    down = [(j, i) for i, j in up]
    before = lax.ppermute(tokens[bands - 1 :], "rows", up)
    after = lax.ppermute(tokens[:1], "rows", down)
    return before, after


def plain_convolve(padded, peg_weight, peg_bias, count_rows, count_cols):
    total = padded[1 : count_rows + 1, 1 : count_cols + 1, :].astype(jnp.float32) + peg_bias
    for offset_row in range(3):
        for offset_col in range(3):
            piece = padded[
                offset_row : offset_row + count_rows, offset_col : offset_col + count_cols, :
            ]
            total = total + piece.astype(jnp.float32) * peg_weight[offset_row, offset_col]
    return total.astype(jnp.bfloat16)


def plain_layer_norm(mixed, norm_gain, norm_bias):
    values = mixed.astype(jnp.float32)
    center = jnp.mean(values, axis=-1, keepdims=True)
    spread = jnp.mean((values - center) ** 2, axis=-1, keepdims=True)
    return ((values - center) * lax.rsqrt(spread + EPS) * norm_gain + norm_bias).astype(
        jnp.bfloat16
    )


def plain_project(normed, qkv_weight, qkv_bias, first_col, last_col):
    model = normed.shape[-1]
    flat_rows = normed.reshape(-1, model)
    outputs = []
    for part_index in range(3):
        lower = part_index * model + first_col
        upper = part_index * model + last_col
        projected = (
            jnp.dot(flat_rows, qkv_weight[:, lower:upper], preferred_element_type=jnp.float32)
            + qkv_bias[lower:upper]
        )
        outputs.append(
            projected.astype(jnp.bfloat16).reshape(normed.shape[:-1] + (last_col - first_col,))
        )
    return outputs


def plain_attend(query, key, value, head_count, tau, scoring, mixing):
    outputs = []
    for head in range(head_count):
        cols = slice(head * DH, (head + 1) * DH)
        logits = (
            jnp.einsum(
                scoring, query[..., cols], key[..., cols], preferred_element_type=jnp.float32
            )
            * tau
        )
        probs = jnp.exp(logits - jnp.max(logits, axis=-1, keepdims=True))
        probs = (probs / jnp.sum(probs, axis=-1, keepdims=True)).astype(jnp.bfloat16)
        outputs.append(
            jnp.einsum(
                mixing, probs, value[..., cols], preferred_element_type=jnp.float32
            ).astype(jnp.bfloat16)
        )
    return jnp.concatenate(outputs, axis=-1)


def plain(
    tokens, peg_weight, peg_bias, norm_gain, norm_bias, qkv_weight, qkv_bias, out_weight, out_bias
):
    bands, width, model = tokens.shape
    height = bands * lax.axis_size("rows")
    row_features = ROW_HEADS * DH
    before, after = halo_rows(tokens)
    padded = jnp.pad(
        jnp.concatenate([before, tokens, after], axis=0), ((0, 0), (1, 1), (0, 0))
    )
    mixed = plain_convolve(padded, peg_weight, peg_bias, bands, width)
    normed = plain_layer_norm(mixed, norm_gain, norm_bias)
    row_qkv = plain_project(normed, qkv_weight, qkv_bias, 0, row_features)
    arrived = lax.all_to_all(normed, "rows", split_axis=1, concat_axis=0, tiled=True)
    col_qkv = plain_project(arrived, qkv_weight, qkv_bias, row_features, model)
    row_heads = plain_attend(
        *row_qkv, ROW_HEADS, score_scale(width), "bld,bmd->blm", "blm,bmd->bld"
    )
    col_heads = plain_attend(
        *col_qkv, HEADS - ROW_HEADS, score_scale(height), "lbd,mbd->blm", "blm,mbd->lbd"
    )
    returned = lax.all_to_all(col_heads, "rows", split_axis=0, concat_axis=1, tiled=True)
    attended = jnp.concatenate([row_heads, returned], axis=2).reshape(bands * width, model)
    result = (
        mixed.reshape(bands * width, model).astype(jnp.float32)
        + jnp.dot(attended, out_weight, preferred_element_type=jnp.float32)
        + out_bias
    )
    return result.astype(jnp.bfloat16).reshape(bands, width, model)


def score_scale(count):
    return math.log(count) / (math.log(16.0) * math.sqrt(DH))


def interleave(first, second):
    upper = lax.broadcasted_iota(jnp.int32, first.shape, 0) < HALF
    low = jnp.where(upper, first, pltpu.roll(second, HALF, 0))
    high = jnp.where(upper, pltpu.roll(first, HALF, 0), second)
    return low, high


def pack_kernel(devices, per_step, tokens_ref, out_hbm, out_scr, sems):
    _, width, model = tokens_ref.shape
    cols = width // devices
    slabs = model // LANES
    tiles = cols // HALF
    place = lax.broadcasted_iota(jnp.int32, (SUB, LANES), 0)

    def copy(dest):
        return pltpu.make_async_copy(out_scr.at[dest], out_hbm.at[dest], sems.at[dest])

    def fill(dest):
        start = pl.multiple_of(dest * cols, cols)
        left_start = pl.multiple_of(jnp.maximum(dest - 1, 0) * cols, cols)
        right_start = pl.multiple_of(jnp.minimum(dest + 1, devices - 1) * cols, cols)
        own = [tokens_ref[band, pl.ds(start, cols), :].astype(jnp.float32) for band in range(2)]
        for eight in range(cols // SUB):
            rows = slice(eight * SUB, (eight + 1) * SUB)
            pair = interleave(own[0][rows], own[1][rows])
            for which in range(2):
                tile = pair[which].astype(jnp.bfloat16)
                for slab in range(slabs):
                    base = (slab * tiles + eight * 2 + which) * SUB
                    out_scr[dest, base : base + SUB, :] = tile[:, slab * LANES : (slab + 1) * LANES]
        lefts, rights = [], []
        for band in range(2):
            left = tokens_ref[band, pl.ds(left_start, cols), :].astype(jnp.float32)
            right = tokens_ref[band, pl.ds(right_start, cols), :].astype(jnp.float32)
            lefts.append(jnp.where(dest > 0, left[cols - 1 : cols], 0.0))
            rights.append(jnp.where(dest < devices - 1, right[0:1], 0.0))
        for two in range(slabs // 2):
            one = slice(2 * two * LANES, (2 * two + 1) * LANES)
            other = slice((2 * two + 1) * LANES, (2 * two + 2) * LANES)
            order = [rights[0][:, one], rights[0][:, other], lefts[0][:, other], lefts[0][:, one]]
            order += [rights[1][:, one], rights[1][:, other], lefts[1][:, other], lefts[1][:, one]]
            tile = jnp.broadcast_to(order[0], (SUB, LANES))
            for index in range(1, SUB):
                tile = jnp.where(place == index, order[index], tile)
            base = (slabs * tiles + two) * SUB
            out_scr[dest, base : base + SUB, :] = tile.astype(jnp.bfloat16)

    def send(step, carry):
        for k in range(per_step):
            fill(step * per_step + k)
            copy(step * per_step + k).start()
        return carry

    def finish(dest, carry):
        copy(dest).wait()
        return carry

    lax.fori_loop(0, devices // per_step, send, 0)
    lax.fori_loop(0, devices, finish, 0)


def pack(tokens, devices):
    bands, width, model = tokens.shape
    cols = width // devices
    slabs = model // LANES
    rows = slabs * bands * (cols + 2)
    per_step = 4
    return pl.pallas_call(
        functools.partial(pack_kernel, devices, per_step),
        in_specs=[pl.BlockSpec(memory_space=pltpu.VMEM)],
        out_specs=pl.BlockSpec(memory_space=pltpu.HBM),
        out_shape=jax.ShapeDtypeStruct((devices, rows, LANES), jnp.bfloat16),
        scratch_shapes=[
            pltpu.VMEM((devices, rows, LANES), jnp.bfloat16),
            pltpu.SemaphoreType.DMA((devices,)),
        ],
        compiler_params=pltpu.CompilerParams(vmem_limit_bytes=6 * MIB),
        name="pack_columns",
    )(tokens)


def gate_kernel(*refs):
    pass


def gate(values, *after):
    hbm = pl.BlockSpec(memory_space=pltpu.HBM)
    anywhere = pl.BlockSpec(memory_space=pl.ANY)
    count = len(values)
    return pl.pallas_call(
        gate_kernel,
        in_specs=[hbm] * count + [anywhere] * len(after),
        out_specs=[hbm] * count,
        out_shape=[jax.ShapeDtypeStruct(value.shape, value.dtype) for value in values],
        input_output_aliases={index: index for index in range(count)},
        name="gate",
    )(*values, *after)


def in_hbm(value):
    return pltpu.with_memory_space_constraint(value, pltpu.HBM)


def normalise(values, gain, bias):
    center = jnp.mean(values, axis=-1, keepdims=True)
    shifted = values - center
    spread = jnp.mean(shifted * shifted, axis=-1, keepdims=True)
    return (shifted * lax.rsqrt(spread + EPS) * gain + bias).astype(jnp.bfloat16)


def attend_pair(query, key, value, scale, mask):
    count = query.shape[0]
    lane = lax.broadcasted_iota(jnp.int32, query.shape, 1)
    zero = jnp.zeros_like(query)
    both = jnp.concatenate(
        [jnp.where(lane < DH, query, zero), jnp.where(lane < DH, zero, query)], axis=0
    )
    scores = lax.dot_general(
        both, key, (((1,), (1,)), ((), ())), preferred_element_type=jnp.float32
    )
    if mask is not None:
        scores = jnp.where(mask, scores.reshape((-1,) + mask.shape[1:]), -1e30)
        scores = scores.reshape(PAIR * count, -1)
    highest = jnp.max(scores, axis=-1, keepdims=True)
    probs = jnp.exp2((scores - highest) * (scale * LOG2E))
    total = jnp.sum(probs, axis=-1, keepdims=True)
    probs = (probs * (1.0 / total)).astype(jnp.bfloat16)
    mixed = jnp.dot(probs, value, preferred_element_type=jnp.float32)
    return jnp.where(lane < DH, mixed[:count], mixed[count:])


def weight_copies(qkv_hbm, weight_scr, sems, first):
    model = qkv_hbm.shape[0]
    width = weight_scr.shape[2]
    pieces = sems.shape[1]
    depth = model // pieces
    return [
        [
            pltpu.make_async_copy(
                qkv_hbm.at[pl.ds(piece * depth, depth), pl.ds(part * model + first, width)],
                weight_scr.at[part, pl.ds(piece * depth, depth)],
                sems.at[part, piece],
            )
            for piece in range(pieces)
        ]
        for part in range(3)
    ]


def column_kernel(
    recv_ref,
    peg_ref,
    peg_bias_ref,
    gain_ref,
    nbias_ref,
    qkv_bias_ref,
    qkv_hbm,
    *refs,
):
    out_hbm, mixed_scr, normed_scr, qkv_scr, weight_scr, heads_scr, sems, out_sems = refs[-8:]

    devices = recv_ref.shape[0]
    slabs, _, tiles, _, _ = mixed_scr.shape
    height = 2 * devices
    first = ROW_HEADS * DH
    features = weight_scr.shape[2]
    group = devices * SUB

    weights = weight_copies(qkv_hbm, weight_scr, sems, first)
    for copies in weights:
        for copy in copies:
            copy.start()

    place = lax.broadcasted_iota(jnp.int32, (SUB, LANES), 0)
    upper = place < HALF
    column = lax.rem(place, HALF)
    zero = jnp.zeros((SUB, LANES), jnp.float32)

    def convolve_slab(slab, base, edge_base, local):
        lanes = pl.ds(pl.multiple_of(slab * LANES, LANES), LANES)
        weights = [
            [jnp.broadcast_to(peg_ref[a, b : b + 1, lanes], (SUB, LANES)) for b in range(3)]
            for a in range(3)
        ]
        weights[1][1] = weights[1][1] + 1.0
        bias = jnp.broadcast_to(peg_bias_ref[:, lanes], (SUB, LANES))

        def load(device):
            own = [
                recv_ref[device, pl.ds(pl.multiple_of(base + tile * SUB, SUB), SUB), :].astype(
                    jnp.float32
                )
                for tile in range(tiles)
            ]
            edge = recv_ref[device, pl.ds(pl.multiple_of(edge_base, SUB), SUB), :]
            edge = edge.astype(jnp.float32)
            if local == 0:
                return [edge] + own + [edge]
            return [pltpu.roll(edge, 1, 0)] + own + [pltpu.roll(edge, SUB - 1, 0)]

        swapped = [zero] * (tiles + 2)
        values = load(0)
        following = [pltpu.roll(value, HALF, 0) for value in values]
        above = [jnp.where(upper, p, n) for p, n in zip(swapped, following)]
        for device in range(devices):
            swapped = following
            if device + 1 < devices:
                coming = load(device + 1)
                following = [pltpu.roll(value, HALF, 0) for value in coming]
            else:
                coming, following = None, [zero] * (tiles + 2)
            below = [jnp.where(upper, p, n) for p, n in zip(swapped, following)]

            def stencil(index, offset):
                return (
                    above[index] * weights[0][offset]
                    + values[index] * weights[1][offset]
                    + below[index] * weights[2][offset]
                )

            lefts = [stencil(index, 0) for index in range(tiles + 1)]
            rights = [stencil(index, 2) for index in range(1, tiles + 2)]
            for tile in range(tiles):
                from_left = jnp.where(
                    column == 0,
                    pltpu.roll(lefts[tile], SUB - 3, 0),
                    pltpu.roll(lefts[tile + 1], 1, 0),
                )
                from_right = jnp.where(
                    column == HALF - 1,
                    pltpu.roll(rights[tile + 1], 3, 0),
                    pltpu.roll(rights[tile], SUB - 1, 0),
                )
                total = (stencil(tile + 1, 1) + bias) + (from_left + from_right)
                mixed_scr[slab, device, tile] = total.astype(jnp.bfloat16).astype(jnp.float32)
            values, above = coming, below

    def two_slabs(two, carry):
        for local in range(2):
            slab = 2 * two + local
            convolve_slab(slab, slab * tiles * SUB, (slabs * tiles + two) * SUB, local)
        return carry

    lax.fori_loop(0, slabs // 2, two_slabs, 0)

    row_id = lax.broadcasted_iota(jnp.int32, (1, SUB, group), 1)
    col_id = lax.broadcasted_iota(jnp.int32, (1, SUB, group), 2)
    mask = lax.rem(row_id, HALF) == lax.rem(col_id, HALF)
    scale = score_scale(height)
    block = 2 * group
    sent = []
    for half in range(tiles // 2):
        for tile in range(2 * half, 2 * half + 2):
            for start in range(0, devices, HALF):
                values = jnp.concatenate(
                    [
                        mixed_scr[slab, start : start + HALF, tile].reshape(
                            HALF * SUB, LANES
                        )
                        for slab in range(slabs)
                    ],
                    axis=1,
                )
                base = tile * group + start * SUB
                normed_scr[base : base + HALF * SUB, :] = normalise(
                    values, gain_ref[...], nbias_ref[...]
                )
        span = slice(half * block, (half + 1) * block)
        for part in range(3):
            if half == 0:
                for copy in weights[part]:
                    copy.wait()
            projected = (
                jnp.dot(
                    normed_scr[span, :],
                    weight_scr[part],
                    preferred_element_type=jnp.float32,
                )
                + qkv_bias_ref[part : part + 1, :]
            )
            qkv_scr[part, span, :] = projected.astype(jnp.bfloat16)
        for tile in range(2 * half, 2 * half + 2):
            rows = slice(tile * group, (tile + 1) * group)
            for pair in range(features // LANES):
                lanes = slice(pair * LANES, (pair + 1) * LANES)
                heads = attend_pair(
                    qkv_scr[0, rows, lanes],
                    qkv_scr[1, rows, lanes],
                    qkv_scr[2, rows, lanes],
                    scale,
                    mask,
                )
                heads_scr[tile, :, :, lanes] = heads.astype(jnp.bfloat16).reshape(
                    devices, SUB, LANES
                )
            sent.append(
                pltpu.make_async_copy(heads_scr.at[tile], out_hbm.at[:, tile], out_sems.at[tile])
            )
            sent[-1].start()
    for copy in sent:
        copy.wait()


def column_part(recv, after, peg_weight, peg_bias, gain, nbias, qkv_weight, qkv_bias):
    devices, rows, _ = recv.shape
    model = gain.shape[-1]
    slabs = model // LANES
    cols = rows // (2 * slabs) - 2
    tiles = cols // HALF
    first = ROW_HEADS * DH
    features = model - first
    tokens = 2 * devices * cols
    vmem = pl.BlockSpec(memory_space=pltpu.VMEM)
    return pl.pallas_call(
        column_kernel,
        in_specs=[vmem] * 6 + [pl.BlockSpec(memory_space=pltpu.HBM)] * (1 + len(after)),
        out_specs=pl.BlockSpec(memory_space=pltpu.HBM),
        out_shape=pltpu.HBM((devices, tiles, SUB, features), jnp.bfloat16),
        scratch_shapes=[
            pltpu.VMEM((slabs, devices, tiles, SUB, LANES), jnp.float32),
            pltpu.VMEM((tokens, model), jnp.bfloat16),
            pltpu.VMEM((3, tokens, features), jnp.bfloat16),
            pltpu.VMEM((3, model, features), jnp.bfloat16),
            pltpu.VMEM((tiles, devices, SUB, features), jnp.bfloat16),
            pltpu.SemaphoreType.DMA((3, 1)),
            pltpu.SemaphoreType.DMA((tiles,)),
        ],
        compiler_params=pltpu.CompilerParams(vmem_limit_bytes=9 * MIB),
        cost_estimate=pl.CostEstimate(
            flops=2 * tokens * model * 3 * features,
            transcendentals=tokens * LANES * features // DH,
            bytes_accessed=8 * MIB,
        ),
        name="column_heads",
    )(
        recv,
        peg_weight,
        peg_bias,
        gain,
        nbias,
        qkv_bias[:, first:],
        in_hbm(qkv_weight),
        *map(in_hbm, after),
    )


def row_kernel(
    tokens_ref,
    intra_ref,
    inter_ref,
    peg_ref,
    peg_bias_ref,
    gain_ref,
    nbias_ref,
    qkv_bias_ref,
    out_bias_ref,
    qkv_hbm,
    out_hbm,
    partial_ref,
    mixed_scr,
    normed_scr,
    qkv_scr,
    heads_scr,
    weight_scr,
    out_scr,
    sems,
    out_sem,
):
    step = pl.program_id(0)
    slabs = pl.num_programs(0)
    bands, width, _ = tokens_ref.shape
    features = weight_scr.shape[2]

    def copies():
        copy = pltpu.make_async_copy(out_hbm.at[pl.ds(0, features), :], out_scr, out_sem)
        return weight_copies(qkv_hbm, weight_scr, sems, 0) + [[copy]]

    @pl.when(step == 0)
    def _():
        for group in copies():
            for copy in group:
                copy.start()

    odd = lax.rem(lax.axis_index("rows"), 2) == 1
    intra = intra_ref[0].astype(jnp.float32)
    inter = inter_ref[0].astype(jnp.float32)
    rows = [jnp.where(odd, intra, inter)]
    rows += [tokens_ref[band].astype(jnp.float32) for band in range(bands)]
    rows += [jnp.where(odd, inter, intra)]
    position = lax.broadcasted_iota(jnp.int32, (width, LANES), 0)
    for band in range(bands):

        def stencil(offset_col):
            return (
                rows[band] * peg_ref[0, offset_col : offset_col + 1, :]
                + rows[band + 1] * peg_ref[1, offset_col : offset_col + 1, :]
                + rows[band + 2] * peg_ref[2, offset_col : offset_col + 1, :]
            )

        from_left = jnp.where(position == 0, 0.0, pltpu.roll(stencil(0), 1, 0))
        from_right = jnp.where(position == width - 1, 0.0, pltpu.roll(stencil(2), width - 1, 0))
        total = rows[band + 1] + peg_bias_ref[...] + stencil(1) + from_left + from_right
        mixed_scr[step, band * width : (band + 1) * width, :] = total.astype(
            jnp.bfloat16
        ).astype(jnp.float32)

    @pl.when(step == slabs - 1)
    def _():
        count = mixed_scr.shape[0]
        chunk = 64
        for start in range(0, bands * width, chunk):
            values = jnp.concatenate(
                [mixed_scr[slab, start : start + chunk, :] for slab in range(count)], axis=1
            )
            normed_scr[start : start + chunk, :] = normalise(
                values, gain_ref[...], nbias_ref[...]
            )
        waits = copies()
        for part in range(3):
            for copy in waits[part]:
                copy.wait()
            projected = (
                jnp.dot(normed_scr[...], weight_scr[part], preferred_element_type=jnp.float32)
                + qkv_bias_ref[part : part + 1, :]
            )
            qkv_scr[part] = projected.astype(jnp.bfloat16)
        scale = score_scale(width)
        for band in range(bands):
            span = slice(band * width, (band + 1) * width)
            for pair in range(features // LANES):
                lanes = slice(pair * LANES, (pair + 1) * LANES)
                heads_scr[span, lanes] = attend_pair(
                    qkv_scr[0, span, lanes],
                    qkv_scr[1, span, lanes],
                    qkv_scr[2, span, lanes],
                    scale,
                    None,
                ).astype(jnp.bfloat16)
        waits[3][0].wait()
        for slab in range(count):
            lanes = slice(slab * LANES, (slab + 1) * LANES)
            partial_ref[:, lanes] = (
                jnp.dot(heads_scr[...], out_scr[:, lanes], preferred_element_type=jnp.float32)
                + mixed_scr[slab]
                + out_bias_ref[:, lanes]
            )


def row_part(
    tokens,
    intra,
    inter,
    peg_weight,
    peg_bias,
    gain,
    nbias,
    qkv_weight,
    qkv_bias,
    out_weight,
    out_bias,
):
    bands, width, model = tokens.shape
    slabs = model // LANES
    features = ROW_HEADS * DH
    count = bands * width
    whole2 = lambda i: (0, 0)
    return pl.pallas_call(
        row_kernel,
        grid=(slabs,),
        in_specs=[
            pl.BlockSpec((bands, width, LANES), lambda i: (0, 0, i)),
            pl.BlockSpec((1, width, LANES), lambda i: (0, 0, i)),
            pl.BlockSpec((1, width, LANES), lambda i: (0, 0, i)),
            pl.BlockSpec((3, 3, LANES), lambda i: (0, 0, i)),
            pl.BlockSpec((1, LANES), lambda i: (0, i)),
            pl.BlockSpec((1, model), whole2),
            pl.BlockSpec((1, model), whole2),
            pl.BlockSpec((3, features), whole2),
            pl.BlockSpec((1, model), whole2),
            pl.BlockSpec(memory_space=pltpu.HBM),
            pl.BlockSpec(memory_space=pltpu.HBM),
        ],
        out_specs=pl.BlockSpec((count, model), whole2),
        out_shape=pltpu.HBM((count, model), jnp.float32),
        scratch_shapes=[
            pltpu.VMEM((slabs, count, LANES), jnp.float32),
            pltpu.VMEM((count, model), jnp.bfloat16),
            pltpu.VMEM((3, count, features), jnp.bfloat16),
            pltpu.VMEM((count, features), jnp.bfloat16),
            pltpu.VMEM((3, model, features), jnp.bfloat16),
            pltpu.VMEM((features, model), jnp.bfloat16),
            pltpu.SemaphoreType.DMA((3, 4)),
            pltpu.SemaphoreType.DMA,
        ],
        compiler_params=pltpu.CompilerParams(vmem_limit_bytes=14 * MIB),
        cost_estimate=pl.CostEstimate(
            flops=40 * count * model * 4 * features,
            transcendentals=count * width * ROW_HEADS,
            bytes_accessed=10 * 1024 * 1024,
        ),
        name="row_heads",
    )(
        tokens,
        intra,
        inter,
        peg_weight,
        peg_bias,
        gain,
        nbias,
        qkv_bias[:, :features],
        out_bias,
        in_hbm(qkv_weight),
        in_hbm(out_weight),
    )


def last_kernel(partial_ref, heads_ref, out_weight_ref, out_hbm, result_scr, sems):
    devices, tiles, sub, features = heads_ref.shape
    bands, width, model = result_scr.shape
    first = ROW_HEADS * DH
    block = model // sems.shape[0]
    heads = heads_ref[...].reshape(devices * tiles * sub, features)
    upper = lax.broadcasted_iota(jnp.int32, (1, sub, block), 1) < HALF
    copies = []
    for step in range(sems.shape[0]):
        lanes = slice(step * block, (step + 1) * block)
        projected = jnp.dot(
            heads, out_weight_ref[first:, lanes], preferred_element_type=jnp.float32
        )
        pairs = projected.reshape(devices * tiles // 2, 2, sub, block)
        low, high = pairs[:, 0], pairs[:, 1]
        rows = (
            jnp.where(upper, low, pltpu.roll(high, HALF, 1)),
            jnp.where(upper, pltpu.roll(low, HALF, 1), high),
        )
        for band, value in enumerate(rows):
            result_scr[band, :, lanes] = (
                partial_ref[band, :, lanes] + value.reshape(width, block)
            ).astype(jnp.bfloat16)
        copy = pltpu.make_async_copy(
            result_scr.at[:, :, lanes], out_hbm.at[:, :, lanes], sems.at[step]
        )
        copy.start()
        copies.append(copy)
    for copy in copies:
        copy.wait()


def last_part(partial, heads, out_weight, bands, width):
    features = heads.shape[3]
    model = out_weight.shape[1]
    return pl.pallas_call(
        last_kernel,
        in_specs=[pl.BlockSpec(memory_space=pltpu.VMEM)] * 3,
        out_specs=pl.BlockSpec(memory_space=pltpu.HBM),
        out_shape=jax.ShapeDtypeStruct((bands, width, model), jnp.bfloat16),
        scratch_shapes=[
            pltpu.VMEM((bands, width, model), jnp.bfloat16),
            pltpu.SemaphoreType.DMA((4,)),
        ],
        compiler_params=pltpu.CompilerParams(vmem_limit_bytes=8 * MIB),
        cost_estimate=pl.CostEstimate(
            flops=2 * bands * width * features * model,
            transcendentals=0,
            bytes_accessed=5 * MIB,
        ),
        name="last_projection",
    )(partial.reshape(bands, width, model), heads, out_weight)


def on_device(
    tokens, peg_weight, peg_bias, norm_gain, norm_bias, qkv_weight, qkv_bias, out_weight, out_bias
):
    devices = lax.axis_size("rows")
    bands, width, model = tokens.shape
    cols = width // devices
    fits = (
        bands == 2
        and width % LANES == 0
        and cols % 16 == 0
        and devices * SUB == LANES
        and model == 2 * ROW_HEADS * DH
        and model % LANES == 0
    )
    if not fits:
        return plain(
            tokens,
            peg_weight,
            peg_bias,
            norm_gain,
            norm_bias,
            qkv_weight,
            qkv_bias,
            out_weight,
            out_bias,
        )
    peg_bias = peg_bias.reshape(1, model)
    gain = norm_gain.reshape(1, model)
    nbias = norm_bias.reshape(1, model)
    out_bias = out_bias.reshape(1, model)
    qkv_bias = qkv_bias.reshape(3, model)

    packed = pack(tokens, devices)
    odd = lax.rem(lax.axis_index("rows"), 2)
    intra = lax.dynamic_slice_in_dim(tokens, 1 - odd, 1, axis=0)
    inter = lax.dynamic_slice_in_dim(tokens, odd, 1, axis=0)
    same_chip = [(i, i ^ 1) for i in range(devices)]
    other_chip = [(i, i + 1 if i % 2 else i - 1) for i in range(1, devices - 1)]
    intra = lax.ppermute(intra, "rows", same_chip)
    inter = lax.ppermute(inter, "rows", other_chip)
    received = lax.all_to_all(packed, "rows", split_axis=0, concat_axis=0, tiled=True)
    partial = row_part(
        tokens,
        in_hbm(intra),
        in_hbm(inter),
        peg_weight,
        peg_bias,
        gain,
        nbias,
        qkv_weight,
        qkv_bias,
        out_weight,
        out_bias,
    )
    col_heads = column_part(
        received, (partial,), peg_weight, peg_bias, gain, nbias, qkv_weight, qkv_bias
    )
    returned = lax.all_to_all(col_heads, "rows", split_axis=0, concat_axis=0, tiled=True)
    return last_part(partial, returned, out_weight, bands, width)


def solution(mesh):
    placed = (P(("groups", "rows"), None, None), P(), P(), P(), P(), P(), P(), P(), P())
    return jax.shard_map(
        on_device,
        mesh=mesh,
        in_specs=placed,
        out_specs=P(("groups", "rows"), None, None),
        check_vma=False,
    )
```

```python
import functools
import math

import jax
import jax.numpy as jnp
from jax import lax
from jax.experimental import pallas as pl
from jax.experimental.pallas import tpu as pltpu
from jax.sharding import PartitionSpec as P

HEADS = 16
DH = 64
ROW_HEADS = 8
LANES = 128
SUB = 8
HALF = SUB // 2
PAIR = LANES // DH
EPS = 1e-06
LOG2E = math.log2(math.e)
MIB = 1024 * 1024


def halo_rows(tokens):
    devices, bands = lax.axis_size("rows"), tokens.shape[0]
    up = [(i, i + 1) for i in range(devices - 1)]
    down = [(j, i) for i, j in up]
    before = lax.ppermute(tokens[bands - 1 :], "rows", up)
    after = lax.ppermute(tokens[:1], "rows", down)
    return before, after


def plain_convolve(padded, peg_weight, peg_bias, count_rows, count_cols):
    total = padded[1 : count_rows + 1, 1 : count_cols + 1, :].astype(jnp.float32) + peg_bias
    for offset_row in range(3):
        for offset_col in range(3):
            piece = padded[
                offset_row : offset_row + count_rows, offset_col : offset_col + count_cols, :
            ]
            total = total + piece.astype(jnp.float32) * peg_weight[offset_row, offset_col]
    return total.astype(jnp.bfloat16)


def plain_layer_norm(mixed, norm_gain, norm_bias):
    values = mixed.astype(jnp.float32)
    center = jnp.mean(values, axis=-1, keepdims=True)
    spread = jnp.mean((values - center) ** 2, axis=-1, keepdims=True)
    return ((values - center) * lax.rsqrt(spread + EPS) * norm_gain + norm_bias).astype(
        jnp.bfloat16
    )


def plain_project(normed, qkv_weight, qkv_bias, first_col, last_col):
    model = normed.shape[-1]
    flat_rows = normed.reshape(-1, model)
    outputs = []
    for part_index in range(3):
        lower = part_index * model + first_col
        upper = part_index * model + last_col
        projected = (
            jnp.dot(flat_rows, qkv_weight[:, lower:upper], preferred_element_type=jnp.float32)
            + qkv_bias[lower:upper]
        )
        outputs.append(
            projected.astype(jnp.bfloat16).reshape(normed.shape[:-1] + (last_col - first_col,))
        )
    return outputs


def plain_attend(query, key, value, head_count, tau, scoring, mixing):
    outputs = []
    for head in range(head_count):
        cols = slice(head * DH, (head + 1) * DH)
        logits = (
            jnp.einsum(
                scoring, query[..., cols], key[..., cols], preferred_element_type=jnp.float32
            )
            * tau
        )
        probs = jnp.exp(logits - jnp.max(logits, axis=-1, keepdims=True))
        probs = (probs / jnp.sum(probs, axis=-1, keepdims=True)).astype(jnp.bfloat16)
        outputs.append(
            jnp.einsum(
                mixing, probs, value[..., cols], preferred_element_type=jnp.float32
            ).astype(jnp.bfloat16)
        )
    return jnp.concatenate(outputs, axis=-1)


def plain(
    tokens, peg_weight, peg_bias, norm_gain, norm_bias, qkv_weight, qkv_bias, out_weight, out_bias
):
    bands, width, model = tokens.shape
    height = bands * lax.axis_size("rows")
    row_features = ROW_HEADS * DH
    before, after = halo_rows(tokens)
    padded = jnp.pad(
        jnp.concatenate([before, tokens, after], axis=0), ((0, 0), (1, 1), (0, 0))
    )
    mixed = plain_convolve(padded, peg_weight, peg_bias, bands, width)
    normed = plain_layer_norm(mixed, norm_gain, norm_bias)
    row_qkv = plain_project(normed, qkv_weight, qkv_bias, 0, row_features)
    arrived = lax.all_to_all(normed, "rows", split_axis=1, concat_axis=0, tiled=True)
    col_qkv = plain_project(arrived, qkv_weight, qkv_bias, row_features, model)
    row_heads = plain_attend(
        *row_qkv, ROW_HEADS, score_scale(width), "bld,bmd->blm", "blm,bmd->bld"
    )
    col_heads = plain_attend(
        *col_qkv, HEADS - ROW_HEADS, score_scale(height), "lbd,mbd->blm", "blm,mbd->lbd"
    )
    returned = lax.all_to_all(col_heads, "rows", split_axis=0, concat_axis=1, tiled=True)
    attended = jnp.concatenate([row_heads, returned], axis=2).reshape(bands * width, model)
    result = (
        mixed.reshape(bands * width, model).astype(jnp.float32)
        + jnp.dot(attended, out_weight, preferred_element_type=jnp.float32)
        + out_bias
    )
    return result.astype(jnp.bfloat16).reshape(bands, width, model)


def score_scale(count):
    return math.log(count) / (math.log(16.0) * math.sqrt(DH))


def interleave(first, second):
    upper = lax.broadcasted_iota(jnp.int32, first.shape, 0) < HALF
    low = jnp.where(upper, first, pltpu.roll(second, HALF, 0))
    high = jnp.where(upper, pltpu.roll(first, HALF, 0), second)
    return low, high


def front_kernel(
    devices,
    tokens_hbm,
    packed_hbm,
    intra_ref,
    inter_ref,
    tokens_scr,
    packed_scr,
    in_sems,
    row_sems,
    out_sems,
):
    _, width, model = tokens_scr.shape
    cols = width // devices
    slabs = model // LANES
    tiles = cols // HALF
    steps = in_sems.shape[0]
    per_step = devices // steps
    place = lax.broadcasted_iota(jnp.int32, (SUB, LANES), 0)

    arrivals = []
    for step in range(steps):
        span = pl.ds(step * per_step * cols, per_step * cols)
        arrivals.append(
            pltpu.make_async_copy(
                tokens_hbm.at[:, span], tokens_scr.at[:, span], in_sems.at[step]
            )
        )
    odd = lax.rem(lax.axis_index("rows"), 2)
    cuts = [
        pltpu.make_async_copy(tokens_hbm.at[pl.ds(odd, 1)], inter_ref, row_sems.at[0]),
        pltpu.make_async_copy(tokens_hbm.at[pl.ds(1 - odd, 1)], intra_ref, row_sems.at[1]),
    ]
    for copy in arrivals + cuts:
        copy.start()

    def columns(dest, band):
        return tokens_scr[band, dest * cols : (dest + 1) * cols, :].astype(jnp.float32)

    def fill(dest):
        own = [columns(dest, band) for band in range(2)]
        for eight in range(cols // SUB):
            rows = slice(eight * SUB, (eight + 1) * SUB)
            pair = interleave(own[0][rows], own[1][rows])
            for which in range(2):
                tile = pair[which].astype(jnp.bfloat16)
                for slab in range(slabs):
                    base = (slab * tiles + eight * 2 + which) * SUB
                    packed_scr[dest, base : base + SUB, :] = tile[
                        :, slab * LANES : (slab + 1) * LANES
                    ]
        outside = jnp.zeros((1, model), jnp.float32)
        lefts, rights = [outside, outside], [outside, outside]
        if dest > 0:
            lefts = [columns(dest - 1, band)[cols - 1 : cols] for band in range(2)]
        if dest < devices - 1:
            rights = [columns(dest + 1, band)[0:1] for band in range(2)]
        for two in range(slabs // 2):
            one = slice(2 * two * LANES, (2 * two + 1) * LANES)
            other = slice((2 * two + 1) * LANES, (2 * two + 2) * LANES)
            order = [rights[0][:, one], rights[0][:, other], lefts[0][:, other], lefts[0][:, one]]
            order += [rights[1][:, one], rights[1][:, other], lefts[1][:, other], lefts[1][:, one]]
            tile = jnp.broadcast_to(order[0], (SUB, LANES))
            for index in range(1, SUB):
                tile = jnp.where(place == index, order[index], tile)
            base = (slabs * tiles + two) * SUB
            packed_scr[dest, base : base + SUB, :] = tile.astype(jnp.bfloat16)

    sent = []
    arrivals[0].wait()
    for step in range(steps):
        if step + 1 < steps:
            arrivals[step + 1].wait()
        for dest in range(step * per_step, (step + 1) * per_step):
            fill(dest)
            sent.append(
                pltpu.make_async_copy(
                    packed_scr.at[dest], packed_hbm.at[dest], out_sems.at[dest]
                )
            )
            sent[-1].start()
    for copy in cuts + sent:
        copy.wait()


def front(tokens, devices):
    bands, width, model = tokens.shape
    cols = width // devices
    slabs = model // LANES
    rows = slabs * bands * (cols + 2)
    return pl.pallas_call(
        functools.partial(front_kernel, devices),
        in_specs=[pl.BlockSpec(memory_space=pltpu.HBM)],
        out_specs=[pl.BlockSpec(memory_space=pltpu.HBM)]
        + [pl.BlockSpec(memory_space=pltpu.VMEM)] * 2,
        out_shape=[jax.ShapeDtypeStruct((devices, rows, LANES), jnp.bfloat16)]
        + [pltpu.VMEM((1, width, model), jnp.bfloat16)] * 2,
        scratch_shapes=[
            pltpu.VMEM((bands, width, model), jnp.bfloat16),
            pltpu.VMEM((devices, rows, LANES), jnp.bfloat16),
            pltpu.SemaphoreType.DMA((4,)),
            pltpu.SemaphoreType.DMA((2,)),
            pltpu.SemaphoreType.DMA((devices,)),
        ],
        compiler_params=pltpu.CompilerParams(vmem_limit_bytes=6 * MIB),
        name="front",
    )(in_hbm(tokens))


def in_hbm(value):
    return pltpu.with_memory_space_constraint(value, pltpu.HBM)


def normalise(values, gain, bias):
    center = jnp.mean(values, axis=-1, keepdims=True)
    shifted = values - center
    spread = jnp.mean(shifted * shifted, axis=-1, keepdims=True)
    return (shifted * lax.rsqrt(spread + EPS) * gain + bias).astype(jnp.bfloat16)


def attend_pair(query, key, value, scale, mask):
    count = query.shape[0]
    lane = lax.broadcasted_iota(jnp.int32, query.shape, 1)
    zero = jnp.zeros_like(query)
    both = jnp.concatenate(
        [jnp.where(lane < DH, query, zero), jnp.where(lane < DH, zero, query)], axis=0
    )
    scores = lax.dot_general(
        both, key, (((1,), (1,)), ((), ())), preferred_element_type=jnp.float32
    )
    if mask is not None:
        scores = jnp.where(mask, scores.reshape((-1,) + mask.shape[1:]), -1e30)
        scores = scores.reshape(PAIR * count, -1)
    highest = jnp.max(scores, axis=-1, keepdims=True)
    probs = jnp.exp2((scores - highest) * (scale * LOG2E))
    total = jnp.sum(probs, axis=-1, keepdims=True)
    probs = (probs * (1.0 / total)).astype(jnp.bfloat16)
    mixed = jnp.dot(probs, value, preferred_element_type=jnp.float32)
    return jnp.where(lane < DH, mixed[:count], mixed[count:])


def weight_copies(qkv_hbm, weight_scr, sems, first):
    model = qkv_hbm.shape[0]
    width = weight_scr.shape[2]
    pieces = sems.shape[1]
    depth = model // pieces
    return [
        [
            pltpu.make_async_copy(
                qkv_hbm.at[pl.ds(piece * depth, depth), pl.ds(part * model + first, width)],
                weight_scr.at[part, pl.ds(piece * depth, depth)],
                sems.at[part, piece],
            )
            for piece in range(pieces)
        ]
        for part in range(3)
    ]


def column_kernel(
    recv_ref,
    peg_ref,
    peg_bias_ref,
    gain_ref,
    nbias_ref,
    qkv_bias_ref,
    qkv_hbm,
    *refs,
):
    out_hbm, mixed_scr, normed_scr, qkv_scr, weight_scr, heads_scr, sems, out_sems = refs[-8:]

    devices = recv_ref.shape[0]
    slabs, _, tiles, _, _ = mixed_scr.shape
    height = 2 * devices
    first = ROW_HEADS * DH
    features = weight_scr.shape[2]
    group = devices * SUB

    weights = weight_copies(qkv_hbm, weight_scr, sems, first)
    for copies in weights:
        for copy in copies:
            copy.start()

    place = lax.broadcasted_iota(jnp.int32, (SUB, LANES), 0)
    upper = place < HALF
    column = lax.rem(place, HALF)
    zero = jnp.zeros((SUB, LANES), jnp.float32)

    def convolve_slab(slab, base, edge_base, local):
        lanes = pl.ds(pl.multiple_of(slab * LANES, LANES), LANES)
        weights = [
            [jnp.broadcast_to(peg_ref[a, b : b + 1, lanes], (SUB, LANES)) for b in range(3)]
            for a in range(3)
        ]
        weights[1][1] = weights[1][1] + 1.0
        bias = jnp.broadcast_to(peg_bias_ref[:, lanes], (SUB, LANES))

        def load(device):
            own = [
                recv_ref[device, pl.ds(pl.multiple_of(base + tile * SUB, SUB), SUB), :].astype(
                    jnp.float32
                )
                for tile in range(tiles)
            ]
            edge = recv_ref[device, pl.ds(pl.multiple_of(edge_base, SUB), SUB), :]
            edge = edge.astype(jnp.float32)
            if local == 0:
                return [edge] + own + [edge]
            return [pltpu.roll(edge, 1, 0)] + own + [pltpu.roll(edge, SUB - 1, 0)]

        swapped = [zero] * (tiles + 2)
        values = load(0)
        following = [pltpu.roll(value, HALF, 0) for value in values]
        above = [jnp.where(upper, p, n) for p, n in zip(swapped, following)]
        for device in range(devices):
            swapped = following
            if device + 1 < devices:
                coming = load(device + 1)
                following = [pltpu.roll(value, HALF, 0) for value in coming]
            else:
                coming, following = None, [zero] * (tiles + 2)
            below = [jnp.where(upper, p, n) for p, n in zip(swapped, following)]

            def stencil(index, offset):
                return (
                    above[index] * weights[0][offset]
                    + values[index] * weights[1][offset]
                    + below[index] * weights[2][offset]
                )

            lefts = [stencil(index, 0) for index in range(tiles + 1)]
            rights = [stencil(index, 2) for index in range(1, tiles + 2)]
            for tile in range(tiles):
                from_left = jnp.where(
                    column == 0,
                    pltpu.roll(lefts[tile], SUB - 3, 0),
                    pltpu.roll(lefts[tile + 1], 1, 0),
                )
                from_right = jnp.where(
                    column == HALF - 1,
                    pltpu.roll(rights[tile + 1], 3, 0),
                    pltpu.roll(rights[tile], SUB - 1, 0),
                )
                total = (stencil(tile + 1, 1) + bias) + (from_left + from_right)
                mixed_scr[slab, device, tile] = total.astype(jnp.bfloat16).astype(jnp.float32)
            values, above = coming, below

    def two_slabs(two, carry):
        for local in range(2):
            slab = 2 * two + local
            convolve_slab(slab, slab * tiles * SUB, (slabs * tiles + two) * SUB, local)
        return carry

    lax.fori_loop(0, slabs // 2, two_slabs, 0)

    row_id = lax.broadcasted_iota(jnp.int32, (1, SUB, group), 1)
    col_id = lax.broadcasted_iota(jnp.int32, (1, SUB, group), 2)
    mask = lax.rem(row_id, HALF) == lax.rem(col_id, HALF)
    scale = score_scale(height)
    block = 2 * group
    sent = []
    for half in range(tiles // 2):
        for tile in range(2 * half, 2 * half + 2):
            for start in range(0, devices, HALF):
                values = jnp.concatenate(
                    [
                        mixed_scr[slab, start : start + HALF, tile].reshape(
                            HALF * SUB, LANES
                        )
                        for slab in range(slabs)
                    ],
                    axis=1,
                )
                base = tile * group + start * SUB
                normed_scr[base : base + HALF * SUB, :] = normalise(
                    values, gain_ref[...], nbias_ref[...]
                )
        span = slice(half * block, (half + 1) * block)
        for part in range(3):
            if half == 0:
                for copy in weights[part]:
                    copy.wait()
            projected = (
                jnp.dot(
                    normed_scr[span, :],
                    weight_scr[part],
                    preferred_element_type=jnp.float32,
                )
                + qkv_bias_ref[part : part + 1, :]
            )
            qkv_scr[part, span, :] = projected.astype(jnp.bfloat16)
        for tile in range(2 * half, 2 * half + 2):
            rows = slice(tile * group, (tile + 1) * group)
            for pair in range(features // LANES):
                lanes = slice(pair * LANES, (pair + 1) * LANES)
                heads = attend_pair(
                    qkv_scr[0, rows, lanes],
                    qkv_scr[1, rows, lanes],
                    qkv_scr[2, rows, lanes],
                    scale,
                    mask,
                )
                heads_scr[tile, :, :, lanes] = heads.astype(jnp.bfloat16).reshape(
                    devices, SUB, LANES
                )
            sent.append(
                pltpu.make_async_copy(heads_scr.at[tile], out_hbm.at[:, tile], out_sems.at[tile])
            )
            sent[-1].start()
    for copy in sent:
        copy.wait()


def column_part(recv, after, peg_weight, peg_bias, gain, nbias, qkv_weight, qkv_bias):
    devices, rows, _ = recv.shape
    model = gain.shape[-1]
    slabs = model // LANES
    cols = rows // (2 * slabs) - 2
    tiles = cols // HALF
    first = ROW_HEADS * DH
    features = model - first
    tokens = 2 * devices * cols
    vmem = pl.BlockSpec(memory_space=pltpu.VMEM)
    return pl.pallas_call(
        column_kernel,
        in_specs=[vmem] * 6 + [pl.BlockSpec(memory_space=pltpu.HBM)] * (1 + len(after)),
        out_specs=pl.BlockSpec(memory_space=pltpu.HBM),
        out_shape=pltpu.HBM((devices, tiles, SUB, features), jnp.bfloat16),
        scratch_shapes=[
            pltpu.VMEM((slabs, devices, tiles, SUB, LANES), jnp.float32),
            pltpu.VMEM((tokens, model), jnp.bfloat16),
            pltpu.VMEM((3, tokens, features), jnp.bfloat16),
            pltpu.VMEM((3, model, features), jnp.bfloat16),
            pltpu.VMEM((tiles, devices, SUB, features), jnp.bfloat16),
            pltpu.SemaphoreType.DMA((3, 1)),
            pltpu.SemaphoreType.DMA((tiles,)),
        ],
        compiler_params=pltpu.CompilerParams(vmem_limit_bytes=9 * MIB),
        cost_estimate=pl.CostEstimate(
            flops=2 * tokens * model * 3 * features,
            transcendentals=tokens * LANES * features // DH,
            bytes_accessed=8 * MIB,
        ),
        name="column_heads",
    )(
        recv,
        peg_weight,
        peg_bias,
        gain,
        nbias,
        qkv_bias[:, first:],
        in_hbm(qkv_weight),
        *map(in_hbm, after),
    )


def row_kernel(
    tokens_ref,
    intra_ref,
    inter_ref,
    peg_ref,
    peg_bias_ref,
    gain_ref,
    nbias_ref,
    qkv_bias_ref,
    out_bias_ref,
    qkv_hbm,
    out_hbm,
    partial_ref,
    mixed_scr,
    normed_scr,
    qkv_scr,
    heads_scr,
    weight_scr,
    out_scr,
    sems,
    out_sem,
):
    step = pl.program_id(0)
    slabs = pl.num_programs(0)
    bands, width, _ = tokens_ref.shape
    here = pl.ds(pl.multiple_of(step * LANES, LANES), LANES)
    features = weight_scr.shape[2]

    def copies():
        copy = pltpu.make_async_copy(out_hbm.at[pl.ds(0, features), :], out_scr, out_sem)
        return weight_copies(qkv_hbm, weight_scr, sems, 0) + [[copy]]

    @pl.when(step == 0)
    def _():
        for group in copies():
            for copy in group:
                copy.start()

    odd = lax.rem(lax.axis_index("rows"), 2) == 1
    intra = intra_ref[0, :, here].astype(jnp.float32)
    inter = inter_ref[0, :, here].astype(jnp.float32)
    rows = [jnp.where(odd, intra, inter)]
    rows += [tokens_ref[band, :, here].astype(jnp.float32) for band in range(bands)]
    rows += [jnp.where(odd, inter, intra)]
    position = lax.broadcasted_iota(jnp.int32, (width, LANES), 0)
    for band in range(bands):

        def stencil(offset_col):
            return (
                rows[band] * peg_ref[0, offset_col : offset_col + 1, :]
                + rows[band + 1] * peg_ref[1, offset_col : offset_col + 1, :]
                + rows[band + 2] * peg_ref[2, offset_col : offset_col + 1, :]
            )

        from_left = jnp.where(position == 0, 0.0, pltpu.roll(stencil(0), 1, 0))
        from_right = jnp.where(position == width - 1, 0.0, pltpu.roll(stencil(2), width - 1, 0))
        total = rows[band + 1] + peg_bias_ref[...] + stencil(1) + from_left + from_right
        mixed_scr[step, band * width : (band + 1) * width, :] = total.astype(
            jnp.bfloat16
        ).astype(jnp.float32)

    @pl.when(step == slabs - 1)
    def _():
        count = mixed_scr.shape[0]
        chunk = 64
        for start in range(0, bands * width, chunk):
            values = jnp.concatenate(
                [mixed_scr[slab, start : start + chunk, :] for slab in range(count)], axis=1
            )
            normed_scr[start : start + chunk, :] = normalise(
                values, gain_ref[...], nbias_ref[...]
            )
        waits = copies()
        for part in range(3):
            for copy in waits[part]:
                copy.wait()
            projected = (
                jnp.dot(normed_scr[...], weight_scr[part], preferred_element_type=jnp.float32)
                + qkv_bias_ref[part : part + 1, :]
            )
            qkv_scr[part] = projected.astype(jnp.bfloat16)
        scale = score_scale(width)
        for band in range(bands):
            span = slice(band * width, (band + 1) * width)
            for pair in range(features // LANES):
                lanes = slice(pair * LANES, (pair + 1) * LANES)
                heads_scr[span, lanes] = attend_pair(
                    qkv_scr[0, span, lanes],
                    qkv_scr[1, span, lanes],
                    qkv_scr[2, span, lanes],
                    scale,
                    None,
                ).astype(jnp.bfloat16)
        waits[3][0].wait()
        for slab in range(count):
            lanes = slice(slab * LANES, (slab + 1) * LANES)
            partial_ref[:, lanes] = (
                jnp.dot(heads_scr[...], out_scr[:, lanes], preferred_element_type=jnp.float32)
                + mixed_scr[slab]
                + out_bias_ref[:, lanes]
            )


def row_part(
    tokens,
    intra,
    inter,
    peg_weight,
    peg_bias,
    gain,
    nbias,
    qkv_weight,
    qkv_bias,
    out_weight,
    out_bias,
):
    bands, width, model = tokens.shape
    slabs = model // LANES
    features = ROW_HEADS * DH
    count = bands * width
    whole2 = lambda i: (0, 0)
    return pl.pallas_call(
        row_kernel,
        grid=(slabs,),
        in_specs=[
            pl.BlockSpec(memory_space=pltpu.VMEM),
            pl.BlockSpec(memory_space=pltpu.VMEM),
            pl.BlockSpec(memory_space=pltpu.VMEM),
            pl.BlockSpec((3, 3, LANES), lambda i: (0, 0, i)),
            pl.BlockSpec((1, LANES), lambda i: (0, i)),
            pl.BlockSpec((1, model), whole2),
            pl.BlockSpec((1, model), whole2),
            pl.BlockSpec((3, features), whole2),
            pl.BlockSpec((1, model), whole2),
            pl.BlockSpec(memory_space=pltpu.HBM),
            pl.BlockSpec(memory_space=pltpu.HBM),
        ],
        out_specs=pl.BlockSpec((count, model), whole2),
        out_shape=pltpu.HBM((count, model), jnp.float32),
        scratch_shapes=[
            pltpu.VMEM((slabs, count, LANES), jnp.float32),
            pltpu.VMEM((count, model), jnp.bfloat16),
            pltpu.VMEM((3, count, features), jnp.bfloat16),
            pltpu.VMEM((count, features), jnp.bfloat16),
            pltpu.VMEM((3, model, features), jnp.bfloat16),
            pltpu.VMEM((features, model), jnp.bfloat16),
            pltpu.SemaphoreType.DMA((3, 4)),
            pltpu.SemaphoreType.DMA,
        ],
        compiler_params=pltpu.CompilerParams(vmem_limit_bytes=14 * MIB),
        cost_estimate=pl.CostEstimate(
            flops=40 * count * model * 4 * features,
            transcendentals=count * width * ROW_HEADS,
            bytes_accessed=10 * 1024 * 1024,
        ),
        name="row_heads",
    )(
        tokens,
        intra,
        inter,
        peg_weight,
        peg_bias,
        gain,
        nbias,
        qkv_bias[:, :features],
        out_bias,
        in_hbm(qkv_weight),
        in_hbm(out_weight),
    )


def last_kernel(partial_ref, heads_ref, out_weight_ref, out_hbm, result_scr, sems):
    devices, tiles, sub, features = heads_ref.shape
    bands, width, model = result_scr.shape
    first = ROW_HEADS * DH
    block = model // sems.shape[0]
    heads = heads_ref[...].reshape(devices * tiles * sub, features)
    upper = lax.broadcasted_iota(jnp.int32, (1, sub, block), 1) < HALF
    copies = []
    for step in range(sems.shape[0]):
        lanes = slice(step * block, (step + 1) * block)
        projected = jnp.dot(
            heads, out_weight_ref[first:, lanes], preferred_element_type=jnp.float32
        )
        pairs = projected.reshape(devices * tiles // 2, 2, sub, block)
        low, high = pairs[:, 0], pairs[:, 1]
        rows = (
            jnp.where(upper, low, pltpu.roll(high, HALF, 1)),
            jnp.where(upper, pltpu.roll(low, HALF, 1), high),
        )
        for band, value in enumerate(rows):
            result_scr[band, :, lanes] = (
                partial_ref[band, :, lanes] + value.reshape(width, block)
            ).astype(jnp.bfloat16)
        copy = pltpu.make_async_copy(
            result_scr.at[:, :, lanes], out_hbm.at[:, :, lanes], sems.at[step]
        )
        copy.start()
        copies.append(copy)
    for copy in copies:
        copy.wait()


def last_part(partial, heads, out_weight, bands, width):
    features = heads.shape[3]
    model = out_weight.shape[1]
    return pl.pallas_call(
        last_kernel,
        in_specs=[pl.BlockSpec(memory_space=pltpu.VMEM)] * 3,
        out_specs=pl.BlockSpec(memory_space=pltpu.HBM),
        out_shape=jax.ShapeDtypeStruct((bands, width, model), jnp.bfloat16),
        scratch_shapes=[
            pltpu.VMEM((bands, width, model), jnp.bfloat16),
            pltpu.SemaphoreType.DMA((4,)),
        ],
        compiler_params=pltpu.CompilerParams(vmem_limit_bytes=8 * MIB),
        cost_estimate=pl.CostEstimate(
            flops=2 * bands * width * features * model,
            transcendentals=0,
            bytes_accessed=5 * MIB,
        ),
        name="last_projection",
    )(partial.reshape(bands, width, model), heads, out_weight)


def on_device(
    tokens, peg_weight, peg_bias, norm_gain, norm_bias, qkv_weight, qkv_bias, out_weight, out_bias
):
    devices = lax.axis_size("rows")
    bands, width, model = tokens.shape
    cols = width // devices
    fits = (
        bands == 2
        and width % LANES == 0
        and cols % 16 == 0
        and devices * SUB == LANES
        and model == 2 * ROW_HEADS * DH
        and model % LANES == 0
    )
    if not fits:
        return plain(
            tokens,
            peg_weight,
            peg_bias,
            norm_gain,
            norm_bias,
            qkv_weight,
            qkv_bias,
            out_weight,
            out_bias,
        )
    peg_bias = peg_bias.reshape(1, model)
    gain = norm_gain.reshape(1, model)
    nbias = norm_bias.reshape(1, model)
    out_bias = out_bias.reshape(1, model)
    qkv_bias = qkv_bias.reshape(3, model)

    packed, intra, inter = front(tokens, devices)
    same_chip = [(i, i ^ 1) for i in range(devices)]
    other_chip = [(i, i + 1 if i % 2 else i - 1) for i in range(1, devices - 1)]
    inter = lax.ppermute(inter, "rows", other_chip)
    intra = lax.ppermute(intra, "rows", same_chip)
    received = lax.all_to_all(packed, "rows", split_axis=0, concat_axis=0, tiled=True)
    partial = row_part(
        tokens,
        in_hbm(intra),
        in_hbm(inter),
        peg_weight,
        peg_bias,
        gain,
        nbias,
        qkv_weight,
        qkv_bias,
        out_weight,
        out_bias,
    )
    col_heads = column_part(
        received, (partial,), peg_weight, peg_bias, gain, nbias, qkv_weight, qkv_bias
    )
    returned = lax.all_to_all(col_heads, "rows", split_axis=0, concat_axis=0, tiled=True)
    return last_part(partial, returned, out_weight, bands, width)


def solution(mesh):
    placed = (P(("groups", "rows"), None, None), P(), P(), P(), P(), P(), P(), P(), P())
    return jax.shard_map(
        on_device,
        mesh=mesh,
        in_specs=placed,
        out_specs=P(("groups", "rows"), None, None),
        check_vma=False,
    )
```

```python
import functools
import math

import jax
import jax.numpy as jnp
from jax import lax
from jax.experimental import pallas as pl
from jax.experimental.pallas import tpu as pltpu
from jax.sharding import PartitionSpec as P

HEADS = 16
DH = 64
ROW_HEADS = 8
LANES = 128
SUB = 8
HALF = SUB // 2
PAIR = LANES // DH
EPS = 1e-06
LOG2E = math.log2(math.e)
MIB = 1024 * 1024


def halo_rows(tokens):
    devices, bands = lax.axis_size("rows"), tokens.shape[0]
    up = [(i, i + 1) for i in range(devices - 1)]
    down = [(j, i) for i, j in up]
    before = lax.ppermute(tokens[bands - 1 :], "rows", up)
    after = lax.ppermute(tokens[:1], "rows", down)
    return before, after


def plain_convolve(padded, peg_weight, peg_bias, count_rows, count_cols):
    total = padded[1 : count_rows + 1, 1 : count_cols + 1, :].astype(jnp.float32) + peg_bias
    for offset_row in range(3):
        for offset_col in range(3):
            piece = padded[
                offset_row : offset_row + count_rows, offset_col : offset_col + count_cols, :
            ]
            total = total + piece.astype(jnp.float32) * peg_weight[offset_row, offset_col]
    return total.astype(jnp.bfloat16)


def plain_layer_norm(mixed, norm_gain, norm_bias):
    values = mixed.astype(jnp.float32)
    center = jnp.mean(values, axis=-1, keepdims=True)
    spread = jnp.mean((values - center) ** 2, axis=-1, keepdims=True)
    return ((values - center) * lax.rsqrt(spread + EPS) * norm_gain + norm_bias).astype(
        jnp.bfloat16
    )


def plain_project(normed, qkv_weight, qkv_bias, first_col, last_col):
    model = normed.shape[-1]
    flat_rows = normed.reshape(-1, model)
    outputs = []
    for part_index in range(3):
        lower = part_index * model + first_col
        upper = part_index * model + last_col
        projected = (
            jnp.dot(flat_rows, qkv_weight[:, lower:upper], preferred_element_type=jnp.float32)
            + qkv_bias[lower:upper]
        )
        outputs.append(
            projected.astype(jnp.bfloat16).reshape(normed.shape[:-1] + (last_col - first_col,))
        )
    return outputs


def plain_attend(query, key, value, head_count, tau, scoring, mixing):
    outputs = []
    for head in range(head_count):
        cols = slice(head * DH, (head + 1) * DH)
        logits = (
            jnp.einsum(
                scoring, query[..., cols], key[..., cols], preferred_element_type=jnp.float32
            )
            * tau
        )
        probs = jnp.exp(logits - jnp.max(logits, axis=-1, keepdims=True))
        probs = (probs / jnp.sum(probs, axis=-1, keepdims=True)).astype(jnp.bfloat16)
        outputs.append(
            jnp.einsum(
                mixing, probs, value[..., cols], preferred_element_type=jnp.float32
            ).astype(jnp.bfloat16)
        )
    return jnp.concatenate(outputs, axis=-1)


def plain(
    tokens, peg_weight, peg_bias, norm_gain, norm_bias, qkv_weight, qkv_bias, out_weight, out_bias
):
    bands, width, model = tokens.shape
    height = bands * lax.axis_size("rows")
    row_features = ROW_HEADS * DH
    before, after = halo_rows(tokens)
    padded = jnp.pad(
        jnp.concatenate([before, tokens, after], axis=0), ((0, 0), (1, 1), (0, 0))
    )
    mixed = plain_convolve(padded, peg_weight, peg_bias, bands, width)
    normed = plain_layer_norm(mixed, norm_gain, norm_bias)
    row_qkv = plain_project(normed, qkv_weight, qkv_bias, 0, row_features)
    arrived = lax.all_to_all(normed, "rows", split_axis=1, concat_axis=0, tiled=True)
    col_qkv = plain_project(arrived, qkv_weight, qkv_bias, row_features, model)
    row_heads = plain_attend(
        *row_qkv, ROW_HEADS, score_scale(width), "bld,bmd->blm", "blm,bmd->bld"
    )
    col_heads = plain_attend(
        *col_qkv, HEADS - ROW_HEADS, score_scale(height), "lbd,mbd->blm", "blm,mbd->lbd"
    )
    returned = lax.all_to_all(col_heads, "rows", split_axis=0, concat_axis=1, tiled=True)
    attended = jnp.concatenate([row_heads, returned], axis=2).reshape(bands * width, model)
    result = (
        mixed.reshape(bands * width, model).astype(jnp.float32)
        + jnp.dot(attended, out_weight, preferred_element_type=jnp.float32)
        + out_bias
    )
    return result.astype(jnp.bfloat16).reshape(bands, width, model)


def score_scale(count):
    return math.log(count) / (math.log(16.0) * math.sqrt(DH))


def interleave(first, second):
    upper = lax.broadcasted_iota(jnp.int32, first.shape, 0) < HALF
    low = jnp.where(upper, first, pltpu.roll(second, HALF, 0))
    high = jnp.where(upper, pltpu.roll(first, HALF, 0), second)
    return low, high


def front_kernel(
    devices,
    tokens_hbm,
    packed_hbm,
    intra_ref,
    inter_ref,
    tokens_scr,
    packed_scr,
    in_sems,
    row_sems,
    out_sems,
):
    _, width, model = tokens_scr.shape
    cols = width // devices
    slabs = model // LANES
    tiles = cols // HALF
    steps = in_sems.shape[0]
    per_step = devices // steps
    place = lax.broadcasted_iota(jnp.int32, (SUB, LANES), 0)

    arrivals = []
    for step in range(steps):
        span = pl.ds(step * per_step * cols, per_step * cols)
        arrivals.append(
            pltpu.make_async_copy(
                tokens_hbm.at[:, span], tokens_scr.at[:, span], in_sems.at[step]
            )
        )
    odd = lax.rem(lax.axis_index("rows"), 2)
    cuts = [
        pltpu.make_async_copy(tokens_hbm.at[pl.ds(odd, 1)], inter_ref, row_sems.at[0]),
        pltpu.make_async_copy(tokens_hbm.at[pl.ds(1 - odd, 1)], intra_ref, row_sems.at[1]),
    ]
    for copy in arrivals + cuts:
        copy.start()

    def columns(dest, band):
        return tokens_scr[band, dest * cols : (dest + 1) * cols, :].astype(jnp.float32)

    def fill(dest):
        own = [columns(dest, band) for band in range(2)]
        for eight in range(cols // SUB):
            rows = slice(eight * SUB, (eight + 1) * SUB)
            pair = interleave(own[0][rows], own[1][rows])
            for which in range(2):
                tile = pair[which].astype(jnp.bfloat16)
                for slab in range(slabs):
                    base = (slab * tiles + eight * 2 + which) * SUB
                    packed_scr[dest, base : base + SUB, :] = tile[
                        :, slab * LANES : (slab + 1) * LANES
                    ]
        outside = jnp.zeros((1, model), jnp.float32)
        lefts, rights = [outside, outside], [outside, outside]
        if dest > 0:
            lefts = [columns(dest - 1, band)[cols - 1 : cols] for band in range(2)]
        if dest < devices - 1:
            rights = [columns(dest + 1, band)[0:1] for band in range(2)]
        for two in range(slabs // 2):
            one = slice(2 * two * LANES, (2 * two + 1) * LANES)
            other = slice((2 * two + 1) * LANES, (2 * two + 2) * LANES)
            order = [rights[0][:, one], rights[0][:, other], lefts[0][:, other], lefts[0][:, one]]
            order += [rights[1][:, one], rights[1][:, other], lefts[1][:, other], lefts[1][:, one]]
            tile = jnp.broadcast_to(order[0], (SUB, LANES))
            for index in range(1, SUB):
                tile = jnp.where(place == index, order[index], tile)
            base = (slabs * tiles + two) * SUB
            packed_scr[dest, base : base + SUB, :] = tile.astype(jnp.bfloat16)

    sent = []
    arrivals[0].wait()
    for step in range(steps):
        if step + 1 < steps:
            arrivals[step + 1].wait()
        for dest in range(step * per_step, (step + 1) * per_step):
            fill(dest)
            sent.append(
                pltpu.make_async_copy(
                    packed_scr.at[dest], packed_hbm.at[dest], out_sems.at[dest]
                )
            )
            sent[-1].start()
    for copy in cuts + sent:
        copy.wait()


def front(tokens, devices):
    bands, width, model = tokens.shape
    cols = width // devices
    slabs = model // LANES
    rows = slabs * bands * (cols + 2)
    return pl.pallas_call(
        functools.partial(front_kernel, devices),
        in_specs=[pl.BlockSpec(memory_space=pltpu.HBM)],
        out_specs=[pl.BlockSpec(memory_space=pltpu.HBM)]
        + [pl.BlockSpec(memory_space=pltpu.VMEM)] * 2,
        out_shape=[jax.ShapeDtypeStruct((devices, rows, LANES), jnp.bfloat16)]
        + [pltpu.VMEM((1, width, model), jnp.bfloat16)] * 2,
        scratch_shapes=[
            pltpu.VMEM((bands, width, model), jnp.bfloat16),
            pltpu.VMEM((devices, rows, LANES), jnp.bfloat16),
            pltpu.SemaphoreType.DMA((4,)),
            pltpu.SemaphoreType.DMA((2,)),
            pltpu.SemaphoreType.DMA((devices,)),
        ],
        compiler_params=pltpu.CompilerParams(vmem_limit_bytes=6 * MIB),
        name="front",
    )(in_hbm(tokens))


def in_hbm(value):
    return pltpu.with_memory_space_constraint(value, pltpu.HBM)


def normalise(values, gain, bias):
    center = jnp.mean(values, axis=-1, keepdims=True)
    shifted = values - center
    spread = jnp.mean(shifted * shifted, axis=-1, keepdims=True)
    return (shifted * lax.rsqrt(spread + EPS) * gain + bias).astype(jnp.bfloat16)


def attend_pair(query, key, value, scale, mask):
    count = query.shape[0]
    lane = lax.broadcasted_iota(jnp.int32, query.shape, 1)
    zero = jnp.zeros_like(query)
    both = jnp.concatenate(
        [jnp.where(lane < DH, query, zero), jnp.where(lane < DH, zero, query)], axis=0
    )
    scores = lax.dot_general(
        both, key, (((1,), (1,)), ((), ())), preferred_element_type=jnp.float32
    )
    if mask is not None:
        scores = jnp.where(mask, scores.reshape((-1,) + mask.shape[1:]), -1e30)
        scores = scores.reshape(PAIR * count, -1)
    highest = jnp.max(scores, axis=-1, keepdims=True)
    probs = jnp.exp2((scores - highest) * (scale * LOG2E))
    total = jnp.sum(probs, axis=-1, keepdims=True)
    probs = (probs * (1.0 / total)).astype(jnp.bfloat16)
    mixed = jnp.dot(probs, value, preferred_element_type=jnp.float32)
    return jnp.where(lane < DH, mixed[:count], mixed[count:])


def weight_copies(qkv_hbm, weight_scr, sems, first):
    model = qkv_hbm.shape[0]
    width = weight_scr.shape[2]
    pieces = sems.shape[1]
    depth = model // pieces
    return [
        [
            pltpu.make_async_copy(
                qkv_hbm.at[pl.ds(piece * depth, depth), pl.ds(part * model + first, width)],
                weight_scr.at[part, pl.ds(piece * depth, depth)],
                sems.at[part, piece],
            )
            for piece in range(pieces)
        ]
        for part in range(3)
    ]


def column_kernel(
    recv_ref,
    peg_ref,
    peg_bias_ref,
    gain_ref,
    nbias_ref,
    qkv_bias_ref,
    qkv_hbm,
    *refs,
):
    out_hbm, mixed_scr, normed_scr, qkv_scr, weight_scr, heads_scr, sems, out_sems = refs[-8:]

    devices = recv_ref.shape[0]
    slabs, _, tiles, _, _ = mixed_scr.shape
    height = 2 * devices
    first = ROW_HEADS * DH
    features = weight_scr.shape[2]
    group = devices * SUB

    weights = weight_copies(qkv_hbm, weight_scr, sems, first)
    for copies in weights:
        for copy in copies:
            copy.start()

    place = lax.broadcasted_iota(jnp.int32, (SUB, LANES), 0)
    upper = place < HALF
    column = lax.rem(place, HALF)
    zero = jnp.zeros((SUB, LANES), jnp.float32)

    def convolve_slab(slab, base, edge_base, local):
        lanes = pl.ds(pl.multiple_of(slab * LANES, LANES), LANES)
        weights = [
            [jnp.broadcast_to(peg_ref[a, b : b + 1, lanes], (SUB, LANES)) for b in range(3)]
            for a in range(3)
        ]
        weights[1][1] = weights[1][1] + 1.0
        bias = jnp.broadcast_to(peg_bias_ref[:, lanes], (SUB, LANES))
        outer = [jnp.where(column >= 2, weights[a][0], weights[a][2]) for a in range(3)]

        def load(device):
            own = [
                recv_ref[device, pl.ds(pl.multiple_of(base + tile * SUB, SUB), SUB), :].astype(
                    jnp.float32
                )
                for tile in range(tiles)
            ]
            edge = recv_ref[device, pl.ds(pl.multiple_of(edge_base, SUB), SUB), :]
            return own + [edge.astype(jnp.float32)]

        swapped = [zero] * (tiles + 1)
        values = load(0)
        following = [pltpu.roll(value, HALF, 0) for value in values]
        above = [jnp.where(upper, p, n) for p, n in zip(swapped, following)]
        for device in range(devices):
            swapped = following
            if device + 1 < devices:
                coming = load(device + 1)
                following = [pltpu.roll(value, HALF, 0) for value in coming]
            else:
                coming, following = None, [zero] * (tiles + 1)
            below = [jnp.where(upper, p, n) for p, n in zip(swapped, following)]

            def stencil(index, offset):
                return (
                    above[index] * weights[0][offset]
                    + values[index] * weights[1][offset]
                    + below[index] * weights[2][offset]
                )

            lefts = [stencil(index, 0) for index in range(tiles)]
            rights = [stencil(index, 2) for index in range(tiles)]
            beside = (
                above[tiles] * outer[0] + values[tiles] * outer[1] + below[tiles] * outer[2]
            )
            for tile in range(tiles):
                if tile > 0:
                    before = pltpu.roll(lefts[tile - 1], SUB - 3, 0)
                else:
                    before = pltpu.roll(beside, SUB - 3 + local, 0)
                if tile < tiles - 1:
                    after = pltpu.roll(rights[tile + 1], 3, 0)
                else:
                    after = pltpu.roll(beside, 3 - local, 0)
                from_left = jnp.where(column == 0, before, pltpu.roll(lefts[tile], 1, 0))
                from_right = jnp.where(
                    column == HALF - 1, after, pltpu.roll(rights[tile], SUB - 1, 0)
                )
                total = (stencil(tile, 1) + bias) + (from_left + from_right)
                mixed_scr[slab, device, tile] = total.astype(jnp.bfloat16).astype(jnp.float32)
            values, above = coming, below

    def two_slabs(two, carry):
        for local in range(2):
            slab = 2 * two + local
            convolve_slab(slab, slab * tiles * SUB, (slabs * tiles + two) * SUB, local)
        return carry

    lax.fori_loop(0, slabs // 2, two_slabs, 0, unroll=True)

    row_id = lax.broadcasted_iota(jnp.int32, (1, SUB, group), 1)
    col_id = lax.broadcasted_iota(jnp.int32, (1, SUB, group), 2)
    mask = lax.rem(row_id, HALF) == lax.rem(col_id, HALF)
    scale = score_scale(height)
    block = 2 * group
    sent = []
    for half in range(tiles // 2):
        for tile in range(2 * half, 2 * half + 2):
            for start in range(0, devices, HALF):
                values = jnp.concatenate(
                    [
                        mixed_scr[slab, start : start + HALF, tile].reshape(
                            HALF * SUB, LANES
                        )
                        for slab in range(slabs)
                    ],
                    axis=1,
                )
                base = tile * group + start * SUB
                normed_scr[base : base + HALF * SUB, :] = normalise(
                    values, gain_ref[...], nbias_ref[...]
                )
        span = slice(half * block, (half + 1) * block)
        for part in range(3):
            if half == 0:
                for copy in weights[part]:
                    copy.wait()
            projected = (
                jnp.dot(
                    normed_scr[span, :],
                    weight_scr[part],
                    preferred_element_type=jnp.float32,
                )
                + qkv_bias_ref[part : part + 1, :]
            )
            qkv_scr[part, span, :] = projected.astype(jnp.bfloat16)
        for tile in range(2 * half, 2 * half + 2):
            rows = slice(tile * group, (tile + 1) * group)
            for pair in range(features // LANES):
                lanes = slice(pair * LANES, (pair + 1) * LANES)
                heads = attend_pair(
                    qkv_scr[0, rows, lanes],
                    qkv_scr[1, rows, lanes],
                    qkv_scr[2, rows, lanes],
                    scale,
                    mask,
                )
                heads_scr[tile, :, :, lanes] = heads.astype(jnp.bfloat16).reshape(
                    devices, SUB, LANES
                )
            sent.append(
                pltpu.make_async_copy(heads_scr.at[tile], out_hbm.at[:, tile], out_sems.at[tile])
            )
            sent[-1].start()
    for copy in sent:
        copy.wait()


def column_part(recv, after, peg_weight, peg_bias, gain, nbias, qkv_weight, qkv_bias):
    devices, rows, _ = recv.shape
    model = gain.shape[-1]
    slabs = model // LANES
    cols = rows // (2 * slabs) - 2
    tiles = cols // HALF
    first = ROW_HEADS * DH
    features = model - first
    tokens = 2 * devices * cols
    vmem = pl.BlockSpec(memory_space=pltpu.VMEM)
    return pl.pallas_call(
        column_kernel,
        in_specs=[vmem] * 6 + [pl.BlockSpec(memory_space=pltpu.HBM)] * (1 + len(after)),
        out_specs=pl.BlockSpec(memory_space=pltpu.HBM),
        out_shape=pltpu.HBM((devices, tiles, SUB, features), jnp.bfloat16),
        scratch_shapes=[
            pltpu.VMEM((slabs, devices, tiles, SUB, LANES), jnp.float32),
            pltpu.VMEM((tokens, model), jnp.bfloat16),
            pltpu.VMEM((3, tokens, features), jnp.bfloat16),
            pltpu.VMEM((3, model, features), jnp.bfloat16),
            pltpu.VMEM((tiles, devices, SUB, features), jnp.bfloat16),
            pltpu.SemaphoreType.DMA((3, 1)),
            pltpu.SemaphoreType.DMA((tiles,)),
        ],
        compiler_params=pltpu.CompilerParams(vmem_limit_bytes=9 * MIB),
        cost_estimate=pl.CostEstimate(
            flops=2 * tokens * model * 3 * features,
            transcendentals=tokens * LANES * features // DH,
            bytes_accessed=8 * MIB,
        ),
        name="column_heads",
    )(
        recv,
        peg_weight,
        peg_bias,
        gain,
        nbias,
        qkv_bias[:, first:],
        in_hbm(qkv_weight),
        *map(in_hbm, after),
    )


def row_kernel(
    tokens_ref,
    intra_ref,
    inter_ref,
    peg_ref,
    peg_bias_ref,
    gain_ref,
    nbias_ref,
    qkv_bias_ref,
    out_bias_ref,
    qkv_hbm,
    out_hbm,
    partial_ref,
    mixed_scr,
    normed_scr,
    qkv_scr,
    heads_scr,
    weight_scr,
    out_scr,
    sems,
    out_sem,
):
    step = pl.program_id(0)
    slabs = pl.num_programs(0)
    bands, width, _ = tokens_ref.shape
    here = pl.ds(pl.multiple_of(step * LANES, LANES), LANES)
    features = weight_scr.shape[2]

    def copies():
        copy = pltpu.make_async_copy(out_hbm.at[pl.ds(0, features), :], out_scr, out_sem)
        return weight_copies(qkv_hbm, weight_scr, sems, 0) + [[copy]]

    @pl.when(step == 0)
    def _():
        for group in copies():
            for copy in group:
                copy.start()

    odd = lax.rem(lax.axis_index("rows"), 2) == 1
    intra = intra_ref[0, :, here].astype(jnp.float32)
    inter = inter_ref[0, :, here].astype(jnp.float32)
    rows = [jnp.where(odd, intra, inter)]
    rows += [tokens_ref[band, :, here].astype(jnp.float32) for band in range(bands)]
    rows += [jnp.where(odd, inter, intra)]
    position = lax.broadcasted_iota(jnp.int32, (width, LANES), 0)
    for band in range(bands):

        def stencil(offset_col):
            return (
                rows[band] * peg_ref[0, offset_col : offset_col + 1, :]
                + rows[band + 1] * peg_ref[1, offset_col : offset_col + 1, :]
                + rows[band + 2] * peg_ref[2, offset_col : offset_col + 1, :]
            )

        from_left = jnp.where(position == 0, 0.0, pltpu.roll(stencil(0), 1, 0))
        from_right = jnp.where(position == width - 1, 0.0, pltpu.roll(stencil(2), width - 1, 0))
        total = rows[band + 1] + peg_bias_ref[...] + stencil(1) + from_left + from_right
        mixed_scr[step, band * width : (band + 1) * width, :] = total.astype(
            jnp.bfloat16
        ).astype(jnp.float32)

    @pl.when(step == slabs - 1)
    def _():
        count = mixed_scr.shape[0]
        chunk = 64
        for start in range(0, bands * width, chunk):
            values = jnp.concatenate(
                [mixed_scr[slab, start : start + chunk, :] for slab in range(count)], axis=1
            )
            normed_scr[start : start + chunk, :] = normalise(
                values, gain_ref[...], nbias_ref[...]
            )
        waits = copies()
        for part in range(3):
            for copy in waits[part]:
                copy.wait()
            projected = (
                jnp.dot(normed_scr[...], weight_scr[part], preferred_element_type=jnp.float32)
                + qkv_bias_ref[part : part + 1, :]
            )
            qkv_scr[part] = projected.astype(jnp.bfloat16)
        scale = score_scale(width)
        for band in range(bands):
            span = slice(band * width, (band + 1) * width)
            for pair in range(features // LANES):
                lanes = slice(pair * LANES, (pair + 1) * LANES)
                heads_scr[span, lanes] = attend_pair(
                    qkv_scr[0, span, lanes],
                    qkv_scr[1, span, lanes],
                    qkv_scr[2, span, lanes],
                    scale,
                    None,
                ).astype(jnp.bfloat16)
        waits[3][0].wait()
        for slab in range(count):
            lanes = slice(slab * LANES, (slab + 1) * LANES)
            partial_ref[:, lanes] = (
                jnp.dot(heads_scr[...], out_scr[:, lanes], preferred_element_type=jnp.float32)
                + mixed_scr[slab]
                + out_bias_ref[:, lanes]
            )


def row_part(
    tokens,
    intra,
    inter,
    peg_weight,
    peg_bias,
    gain,
    nbias,
    qkv_weight,
    qkv_bias,
    out_weight,
    out_bias,
):
    bands, width, model = tokens.shape
    slabs = model // LANES
    features = ROW_HEADS * DH
    count = bands * width
    whole2 = lambda i: (0, 0)
    return pl.pallas_call(
        row_kernel,
        grid=(slabs,),
        in_specs=[
            pl.BlockSpec(memory_space=pltpu.VMEM),
            pl.BlockSpec(memory_space=pltpu.VMEM),
            pl.BlockSpec(memory_space=pltpu.VMEM),
            pl.BlockSpec((3, 3, LANES), lambda i: (0, 0, i)),
            pl.BlockSpec((1, LANES), lambda i: (0, i)),
            pl.BlockSpec((1, model), whole2),
            pl.BlockSpec((1, model), whole2),
            pl.BlockSpec((3, features), whole2),
            pl.BlockSpec((1, model), whole2),
            pl.BlockSpec(memory_space=pltpu.HBM),
            pl.BlockSpec(memory_space=pltpu.HBM),
        ],
        out_specs=pl.BlockSpec((count, model), whole2),
        out_shape=pltpu.HBM((count, model), jnp.float32),
        scratch_shapes=[
            pltpu.VMEM((slabs, count, LANES), jnp.float32),
            pltpu.VMEM((count, model), jnp.bfloat16),
            pltpu.VMEM((3, count, features), jnp.bfloat16),
            pltpu.VMEM((count, features), jnp.bfloat16),
            pltpu.VMEM((3, model, features), jnp.bfloat16),
            pltpu.VMEM((features, model), jnp.bfloat16),
            pltpu.SemaphoreType.DMA((3, 4)),
            pltpu.SemaphoreType.DMA,
        ],
        compiler_params=pltpu.CompilerParams(vmem_limit_bytes=14 * MIB),
        cost_estimate=pl.CostEstimate(
            flops=40 * count * model * 4 * features,
            transcendentals=count * width * ROW_HEADS,
            bytes_accessed=10 * 1024 * 1024,
        ),
        name="row_heads",
    )(
        tokens,
        intra,
        inter,
        peg_weight,
        peg_bias,
        gain,
        nbias,
        qkv_bias[:, :features],
        out_bias,
        in_hbm(qkv_weight),
        in_hbm(out_weight),
    )


def last_kernel(partial_ref, heads_ref, out_weight_ref, out_hbm, result_scr, sems):
    devices, tiles, sub, features = heads_ref.shape
    bands, width, model = result_scr.shape
    first = ROW_HEADS * DH
    block = model // sems.shape[0]
    heads = heads_ref[...].reshape(devices * tiles * sub, features)
    upper = lax.broadcasted_iota(jnp.int32, (1, sub, block), 1) < HALF
    copies = []
    for step in range(sems.shape[0]):
        lanes = slice(step * block, (step + 1) * block)
        projected = jnp.dot(
            heads, out_weight_ref[first:, lanes], preferred_element_type=jnp.float32
        )
        pairs = projected.reshape(devices * tiles // 2, 2, sub, block)
        low, high = pairs[:, 0], pairs[:, 1]
        rows = (
            jnp.where(upper, low, pltpu.roll(high, HALF, 1)),
            jnp.where(upper, pltpu.roll(low, HALF, 1), high),
        )
        for band, value in enumerate(rows):
            result_scr[band, :, lanes] = (
                partial_ref[band, :, lanes] + value.reshape(width, block)
            ).astype(jnp.bfloat16)
        copy = pltpu.make_async_copy(
            result_scr.at[:, :, lanes], out_hbm.at[:, :, lanes], sems.at[step]
        )
        copy.start()
        copies.append(copy)
    for copy in copies:
        copy.wait()


def last_part(partial, heads, out_weight, bands, width):
    features = heads.shape[3]
    model = out_weight.shape[1]
    return pl.pallas_call(
        last_kernel,
        in_specs=[pl.BlockSpec(memory_space=pltpu.VMEM)] * 3,
        out_specs=pl.BlockSpec(memory_space=pltpu.HBM),
        out_shape=jax.ShapeDtypeStruct((bands, width, model), jnp.bfloat16),
        scratch_shapes=[
            pltpu.VMEM((bands, width, model), jnp.bfloat16),
            pltpu.SemaphoreType.DMA((4,)),
        ],
        compiler_params=pltpu.CompilerParams(vmem_limit_bytes=8 * MIB),
        cost_estimate=pl.CostEstimate(
            flops=2 * bands * width * features * model,
            transcendentals=0,
            bytes_accessed=5 * MIB,
        ),
        name="last_projection",
    )(partial.reshape(bands, width, model), heads, out_weight)


def on_device(
    tokens, peg_weight, peg_bias, norm_gain, norm_bias, qkv_weight, qkv_bias, out_weight, out_bias
):
    devices = lax.axis_size("rows")
    bands, width, model = tokens.shape
    cols = width // devices
    fits = (
        bands == 2
        and width % LANES == 0
        and cols % 16 == 0
        and devices * SUB == LANES
        and model == 2 * ROW_HEADS * DH
        and model % LANES == 0
    )
    if not fits:
        return plain(
            tokens,
            peg_weight,
            peg_bias,
            norm_gain,
            norm_bias,
            qkv_weight,
            qkv_bias,
            out_weight,
            out_bias,
        )
    peg_bias = peg_bias.reshape(1, model)
    gain = norm_gain.reshape(1, model)
    nbias = norm_bias.reshape(1, model)
    out_bias = out_bias.reshape(1, model)
    qkv_bias = qkv_bias.reshape(3, model)

    packed, intra, inter = front(tokens, devices)
    same_chip = [(i, i ^ 1) for i in range(devices)]
    other_chip = [(i, i + 1 if i % 2 else i - 1) for i in range(1, devices - 1)]
    inter = lax.ppermute(inter, "rows", other_chip)
    intra = lax.ppermute(intra, "rows", same_chip)
    received = lax.all_to_all(packed, "rows", split_axis=0, concat_axis=0, tiled=True)
    partial = row_part(
        tokens,
        in_hbm(intra),
        in_hbm(inter),
        peg_weight,
        peg_bias,
        gain,
        nbias,
        qkv_weight,
        qkv_bias,
        out_weight,
        out_bias,
    )
    col_heads = column_part(
        received, (partial,), peg_weight, peg_bias, gain, nbias, qkv_weight, qkv_bias
    )
    returned = lax.all_to_all(col_heads, "rows", split_axis=0, concat_axis=0, tiled=True)
    return last_part(partial, returned, out_weight, bands, width)


def solution(mesh):
    placed = (P(("groups", "rows"), None, None), P(), P(), P(), P(), P(), P(), P(), P())
    return jax.shard_map(
        on_device,
        mesh=mesh,
        in_specs=placed,
        out_specs=P(("groups", "rows"), None, None),
        check_vma=False,
    )
```

```python
import functools
import math

import jax
import jax.numpy as jnp
from jax import lax
from jax.experimental import pallas as pl
from jax.experimental.pallas import tpu as pltpu
from jax.sharding import PartitionSpec as P

HEADS = 16
DH = 64
ROW_HEADS = 8
LANES = 128
SUB = 8
HALF = SUB // 2
PAIR = LANES // DH
EPS = 1e-06
LOG2E = math.log2(math.e)
MIB = 1024 * 1024


def halo_rows(tokens):
    devices, bands = lax.axis_size("rows"), tokens.shape[0]
    up = [(i, i + 1) for i in range(devices - 1)]
    down = [(j, i) for i, j in up]
    before = lax.ppermute(tokens[bands - 1 :], "rows", up)
    after = lax.ppermute(tokens[:1], "rows", down)
    return before, after


def plain_convolve(padded, peg_weight, peg_bias, count_rows, count_cols):
    total = padded[1 : count_rows + 1, 1 : count_cols + 1, :].astype(jnp.float32) + peg_bias
    for offset_row in range(3):
        for offset_col in range(3):
            piece = padded[
                offset_row : offset_row + count_rows, offset_col : offset_col + count_cols, :
            ]
            total = total + piece.astype(jnp.float32) * peg_weight[offset_row, offset_col]
    return total.astype(jnp.bfloat16)


def plain_layer_norm(mixed, norm_gain, norm_bias):
    values = mixed.astype(jnp.float32)
    center = jnp.mean(values, axis=-1, keepdims=True)
    spread = jnp.mean((values - center) ** 2, axis=-1, keepdims=True)
    return ((values - center) * lax.rsqrt(spread + EPS) * norm_gain + norm_bias).astype(
        jnp.bfloat16
    )


def plain_project(normed, qkv_weight, qkv_bias, first_col, last_col):
    model = normed.shape[-1]
    flat_rows = normed.reshape(-1, model)
    outputs = []
    for part_index in range(3):
        lower = part_index * model + first_col
        upper = part_index * model + last_col
        projected = (
            jnp.dot(flat_rows, qkv_weight[:, lower:upper], preferred_element_type=jnp.float32)
            + qkv_bias[lower:upper]
        )
        outputs.append(
            projected.astype(jnp.bfloat16).reshape(normed.shape[:-1] + (last_col - first_col,))
        )
    return outputs


def plain_attend(query, key, value, head_count, tau, scoring, mixing):
    outputs = []
    for head in range(head_count):
        cols = slice(head * DH, (head + 1) * DH)
        logits = (
            jnp.einsum(
                scoring, query[..., cols], key[..., cols], preferred_element_type=jnp.float32
            )
            * tau
        )
        probs = jnp.exp(logits - jnp.max(logits, axis=-1, keepdims=True))
        probs = (probs / jnp.sum(probs, axis=-1, keepdims=True)).astype(jnp.bfloat16)
        outputs.append(
            jnp.einsum(
                mixing, probs, value[..., cols], preferred_element_type=jnp.float32
            ).astype(jnp.bfloat16)
        )
    return jnp.concatenate(outputs, axis=-1)


def plain(
    tokens, peg_weight, peg_bias, norm_gain, norm_bias, qkv_weight, qkv_bias, out_weight, out_bias
):
    bands, width, model = tokens.shape
    height = bands * lax.axis_size("rows")
    row_features = ROW_HEADS * DH
    before, after = halo_rows(tokens)
    padded = jnp.pad(
        jnp.concatenate([before, tokens, after], axis=0), ((0, 0), (1, 1), (0, 0))
    )
    mixed = plain_convolve(padded, peg_weight, peg_bias, bands, width)
    normed = plain_layer_norm(mixed, norm_gain, norm_bias)
    row_qkv = plain_project(normed, qkv_weight, qkv_bias, 0, row_features)
    arrived = lax.all_to_all(normed, "rows", split_axis=1, concat_axis=0, tiled=True)
    col_qkv = plain_project(arrived, qkv_weight, qkv_bias, row_features, model)
    row_heads = plain_attend(
        *row_qkv, ROW_HEADS, score_scale(width), "bld,bmd->blm", "blm,bmd->bld"
    )
    col_heads = plain_attend(
        *col_qkv, HEADS - ROW_HEADS, score_scale(height), "lbd,mbd->blm", "blm,mbd->lbd"
    )
    returned = lax.all_to_all(col_heads, "rows", split_axis=0, concat_axis=1, tiled=True)
    attended = jnp.concatenate([row_heads, returned], axis=2).reshape(bands * width, model)
    result = (
        mixed.reshape(bands * width, model).astype(jnp.float32)
        + jnp.dot(attended, out_weight, preferred_element_type=jnp.float32)
        + out_bias
    )
    return result.astype(jnp.bfloat16).reshape(bands, width, model)


def score_scale(count):
    return math.log(count) / (math.log(16.0) * math.sqrt(DH))


def interleave(first, second):
    upper = lax.broadcasted_iota(jnp.int32, first.shape, 0) < HALF
    low = jnp.where(upper, first, pltpu.roll(second, HALF, 0))
    high = jnp.where(upper, pltpu.roll(first, HALF, 0), second)
    return low, high


def front_kernel(
    devices,
    tokens_hbm,
    packed_hbm,
    intra_ref,
    inter_ref,
    tokens_scr,
    packed_scr,
    in_sems,
    row_sems,
    out_sems,
):
    _, width, model = tokens_scr.shape
    cols = width // devices
    slabs = model // LANES
    tiles = cols // HALF
    steps = in_sems.shape[0]
    per_step = devices // steps
    place = lax.broadcasted_iota(jnp.int32, (SUB, LANES), 0)

    arrivals = []
    for step in range(steps):
        span = pl.ds(step * per_step * cols, per_step * cols)
        arrivals.append(
            pltpu.make_async_copy(
                tokens_hbm.at[:, span], tokens_scr.at[:, span], in_sems.at[step]
            )
        )
    odd = lax.rem(lax.axis_index("rows"), 2)
    cuts = [
        pltpu.make_async_copy(tokens_hbm.at[pl.ds(odd, 1)], inter_ref, row_sems.at[0]),
        pltpu.make_async_copy(tokens_hbm.at[pl.ds(1 - odd, 1)], intra_ref, row_sems.at[1]),
    ]
    for copy in arrivals + cuts:
        copy.start()

    def columns(dest, band):
        return tokens_scr[band, dest * cols : (dest + 1) * cols, :].astype(jnp.float32)

    def fill(dest):
        own = [columns(dest, band) for band in range(2)]
        for eight in range(cols // SUB):
            rows = slice(eight * SUB, (eight + 1) * SUB)
            pair = interleave(own[0][rows], own[1][rows])
            for which in range(2):
                tile = pair[which].astype(jnp.bfloat16)
                for slab in range(slabs):
                    base = (slab * tiles + eight * 2 + which) * SUB
                    packed_scr[dest, base : base + SUB, :] = tile[
                        :, slab * LANES : (slab + 1) * LANES
                    ]
        outside = jnp.zeros((1, model), jnp.float32)
        lefts, rights = [outside, outside], [outside, outside]
        if dest > 0:
            lefts = [columns(dest - 1, band)[cols - 1 : cols] for band in range(2)]
        if dest < devices - 1:
            rights = [columns(dest + 1, band)[0:1] for band in range(2)]
        for two in range(slabs // 2):
            one = slice(2 * two * LANES, (2 * two + 1) * LANES)
            other = slice((2 * two + 1) * LANES, (2 * two + 2) * LANES)
            order = [rights[0][:, one], rights[0][:, other], lefts[0][:, other], lefts[0][:, one]]
            order += [rights[1][:, one], rights[1][:, other], lefts[1][:, other], lefts[1][:, one]]
            tile = jnp.broadcast_to(order[0], (SUB, LANES))
            for index in range(1, SUB):
                tile = jnp.where(place == index, order[index], tile)
            base = (slabs * tiles + two) * SUB
            packed_scr[dest, base : base + SUB, :] = tile.astype(jnp.bfloat16)

    sent = []
    arrivals[0].wait()
    for step in range(steps):
        if step + 1 < steps:
            arrivals[step + 1].wait()
        for dest in range(step * per_step, (step + 1) * per_step):
            fill(dest)
            sent.append(
                pltpu.make_async_copy(
                    packed_scr.at[dest], packed_hbm.at[dest], out_sems.at[dest]
                )
            )
            sent[-1].start()
    for copy in cuts + sent:
        copy.wait()


def front(tokens, devices):
    bands, width, model = tokens.shape
    cols = width // devices
    slabs = model // LANES
    rows = slabs * bands * (cols + 2)
    return pl.pallas_call(
        functools.partial(front_kernel, devices),
        in_specs=[pl.BlockSpec(memory_space=pltpu.HBM)],
        out_specs=[pl.BlockSpec(memory_space=pltpu.HBM)]
        + [pl.BlockSpec(memory_space=pltpu.VMEM)] * 2,
        out_shape=[jax.ShapeDtypeStruct((devices, rows, LANES), jnp.bfloat16)]
        + [pltpu.VMEM((1, width, model), jnp.bfloat16)] * 2,
        scratch_shapes=[
            pltpu.VMEM((bands, width, model), jnp.bfloat16),
            pltpu.VMEM((devices, rows, LANES), jnp.bfloat16),
            pltpu.SemaphoreType.DMA((8,)),
            pltpu.SemaphoreType.DMA((2,)),
            pltpu.SemaphoreType.DMA((devices,)),
        ],
        compiler_params=pltpu.CompilerParams(vmem_limit_bytes=6 * MIB),
        name="front",
    )(in_hbm(tokens))


def in_hbm(value):
    return pltpu.with_memory_space_constraint(value, pltpu.HBM)


def normalise(values, gain, bias):
    center = jnp.mean(values, axis=-1, keepdims=True)
    shifted = values - center
    spread = jnp.mean(shifted * shifted, axis=-1, keepdims=True)
    return (shifted * lax.rsqrt(spread + EPS) * gain + bias).astype(jnp.bfloat16)


def attend_pair(query, key, value, scale, mask):
    count = query.shape[0]
    lane = lax.broadcasted_iota(jnp.int32, query.shape, 1)
    zero = jnp.zeros_like(query)
    both = jnp.concatenate(
        [jnp.where(lane < DH, query, zero), jnp.where(lane < DH, zero, query)], axis=0
    )
    scores = lax.dot_general(
        both, key, (((1,), (1,)), ((), ())), preferred_element_type=jnp.float32
    )
    if mask is not None:
        scores = jnp.where(mask, scores.reshape((-1,) + mask.shape[1:]), -1e30)
        scores = scores.reshape(PAIR * count, -1)
    highest = jnp.max(scores, axis=-1, keepdims=True)
    probs = jnp.exp2((scores - highest) * (scale * LOG2E))
    total = jnp.sum(probs, axis=-1, keepdims=True)
    probs = (probs * (1.0 / total)).astype(jnp.bfloat16)
    mixed = jnp.dot(probs, value, preferred_element_type=jnp.float32)
    return jnp.where(lane < DH, mixed[:count], mixed[count:])


def weight_copies(qkv_hbm, weight_scr, sems, first):
    model = qkv_hbm.shape[0]
    width = weight_scr.shape[2]
    pieces = sems.shape[1]
    depth = model // pieces
    return [
        [
            pltpu.make_async_copy(
                qkv_hbm.at[pl.ds(piece * depth, depth), pl.ds(part * model + first, width)],
                weight_scr.at[part, pl.ds(piece * depth, depth)],
                sems.at[part, piece],
            )
            for piece in range(pieces)
        ]
        for part in range(3)
    ]


def column_kernel(
    recv_ref,
    peg_ref,
    peg_bias_ref,
    gain_ref,
    nbias_ref,
    qkv_bias_ref,
    qkv_hbm,
    *refs,
):
    out_hbm, mixed_scr, normed_scr, qkv_scr, weight_scr, heads_scr, sems, out_sems = refs[-8:]

    devices = recv_ref.shape[0]
    slabs, _, tiles, _, _ = mixed_scr.shape
    height = 2 * devices
    first = ROW_HEADS * DH
    features = weight_scr.shape[2]
    group = devices * SUB

    weights = weight_copies(qkv_hbm, weight_scr, sems, first)
    for copies in weights:
        for copy in copies:
            copy.start()

    place = lax.broadcasted_iota(jnp.int32, (SUB, LANES), 0)
    upper = place < HALF
    column = lax.rem(place, HALF)
    zero = jnp.zeros((SUB, LANES), jnp.float32)

    def convolve_slab(slab, base, edge_base, local):
        lanes = pl.ds(pl.multiple_of(slab * LANES, LANES), LANES)
        weights = [
            [jnp.broadcast_to(peg_ref[a, b : b + 1, lanes], (SUB, LANES)) for b in range(3)]
            for a in range(3)
        ]
        weights[1][1] = weights[1][1] + 1.0
        bias = jnp.broadcast_to(peg_bias_ref[:, lanes], (SUB, LANES))
        outer = [jnp.where(column >= 2, weights[a][0], weights[a][2]) for a in range(3)]

        def load(device):
            own = [
                recv_ref[device, pl.ds(pl.multiple_of(base + tile * SUB, SUB), SUB), :].astype(
                    jnp.float32
                )
                for tile in range(tiles)
            ]
            edge = recv_ref[device, pl.ds(pl.multiple_of(edge_base, SUB), SUB), :]
            return own + [edge.astype(jnp.float32)]

        swapped = [zero] * (tiles + 1)
        values = load(0)
        following = [pltpu.roll(value, HALF, 0) for value in values]
        above = [jnp.where(upper, p, n) for p, n in zip(swapped, following)]
        for device in range(devices):
            swapped = following
            if device + 1 < devices:
                coming = load(device + 1)
                following = [pltpu.roll(value, HALF, 0) for value in coming]
            else:
                coming, following = None, [zero] * (tiles + 1)
            below = [jnp.where(upper, p, n) for p, n in zip(swapped, following)]

            def stencil(index, offset):
                return (
                    above[index] * weights[0][offset]
                    + values[index] * weights[1][offset]
                    + below[index] * weights[2][offset]
                )

            lefts = [stencil(index, 0) for index in range(tiles)]
            rights = [stencil(index, 2) for index in range(tiles)]
            beside = (
                above[tiles] * outer[0] + values[tiles] * outer[1] + below[tiles] * outer[2]
            )
            for tile in range(tiles):
                if tile > 0:
                    before = pltpu.roll(lefts[tile - 1], SUB - 3, 0)
                else:
                    before = pltpu.roll(beside, SUB - 3 + local, 0)
                if tile < tiles - 1:
                    after = pltpu.roll(rights[tile + 1], 3, 0)
                else:
                    after = pltpu.roll(beside, 3 - local, 0)
                from_left = jnp.where(column == 0, before, pltpu.roll(lefts[tile], 1, 0))
                from_right = jnp.where(
                    column == HALF - 1, after, pltpu.roll(rights[tile], SUB - 1, 0)
                )
                total = (stencil(tile, 1) + bias) + (from_left + from_right)
                mixed_scr[slab, device, tile] = total.astype(jnp.bfloat16).astype(jnp.float32)
            values, above = coming, below

    def two_slabs(two, carry):
        for local in range(2):
            slab = 2 * two + local
            convolve_slab(slab, slab * tiles * SUB, (slabs * tiles + two) * SUB, local)
        return carry

    lax.fori_loop(0, slabs // 2, two_slabs, 0, unroll=True)

    row_id = lax.broadcasted_iota(jnp.int32, (1, SUB, group), 1)
    col_id = lax.broadcasted_iota(jnp.int32, (1, SUB, group), 2)
    mask = lax.rem(row_id, HALF) == lax.rem(col_id, HALF)
    scale = score_scale(height)
    block = 2 * group
    sent = []
    for half in range(tiles // 2):
        for tile in range(2 * half, 2 * half + 2):
            for start in range(0, devices, HALF):
                values = jnp.concatenate(
                    [
                        mixed_scr[slab, start : start + HALF, tile].reshape(
                            HALF * SUB, LANES
                        )
                        for slab in range(slabs)
                    ],
                    axis=1,
                )
                base = tile * group + start * SUB
                normed_scr[base : base + HALF * SUB, :] = normalise(
                    values, gain_ref[...], nbias_ref[...]
                )
        span = slice(half * block, (half + 1) * block)
        for part in range(3):
            if half == 0:
                for copy in weights[part]:
                    copy.wait()
            projected = (
                jnp.dot(
                    normed_scr[span, :],
                    weight_scr[part],
                    preferred_element_type=jnp.float32,
                )
                + qkv_bias_ref[part : part + 1, :]
            )
            qkv_scr[part, span, :] = projected.astype(jnp.bfloat16)
        for tile in range(2 * half, 2 * half + 2):
            rows = slice(tile * group, (tile + 1) * group)
            for pair in range(features // LANES):
                lanes = slice(pair * LANES, (pair + 1) * LANES)
                heads = attend_pair(
                    qkv_scr[0, rows, lanes],
                    qkv_scr[1, rows, lanes],
                    qkv_scr[2, rows, lanes],
                    scale,
                    mask,
                )
                heads_scr[tile, :, :, lanes] = heads.astype(jnp.bfloat16).reshape(
                    devices, SUB, LANES
                )
            sent.append(
                pltpu.make_async_copy(heads_scr.at[tile], out_hbm.at[:, tile], out_sems.at[tile])
            )
            sent[-1].start()
    for copy in sent:
        copy.wait()


def column_part(recv, after, peg_weight, peg_bias, gain, nbias, qkv_weight, qkv_bias):
    devices, rows, _ = recv.shape
    model = gain.shape[-1]
    slabs = model // LANES
    cols = rows // (2 * slabs) - 2
    tiles = cols // HALF
    first = ROW_HEADS * DH
    features = model - first
    tokens = 2 * devices * cols
    vmem = pl.BlockSpec(memory_space=pltpu.VMEM)
    return pl.pallas_call(
        column_kernel,
        in_specs=[vmem] * 6 + [pl.BlockSpec(memory_space=pltpu.HBM)] * (1 + len(after)),
        out_specs=pl.BlockSpec(memory_space=pltpu.HBM),
        out_shape=pltpu.HBM((devices, tiles, SUB, features), jnp.bfloat16),
        scratch_shapes=[
            pltpu.VMEM((slabs, devices, tiles, SUB, LANES), jnp.float32),
            pltpu.VMEM((tokens, model), jnp.bfloat16),
            pltpu.VMEM((3, tokens, features), jnp.bfloat16),
            pltpu.VMEM((3, model, features), jnp.bfloat16),
            pltpu.VMEM((tiles, devices, SUB, features), jnp.bfloat16),
            pltpu.SemaphoreType.DMA((3, 1)),
            pltpu.SemaphoreType.DMA((tiles,)),
        ],
        compiler_params=pltpu.CompilerParams(vmem_limit_bytes=9 * MIB),
        cost_estimate=pl.CostEstimate(
            flops=2 * tokens * model * 3 * features,
            transcendentals=tokens * LANES * features // DH,
            bytes_accessed=8 * MIB,
        ),
        name="column_heads",
    )(
        recv,
        peg_weight,
        peg_bias,
        gain,
        nbias,
        qkv_bias[:, first:],
        in_hbm(qkv_weight),
        *map(in_hbm, after),
    )


def row_kernel(
    tokens_ref,
    intra_ref,
    inter_ref,
    peg_ref,
    peg_bias_ref,
    gain_ref,
    nbias_ref,
    qkv_bias_ref,
    out_bias_ref,
    qkv_hbm,
    out_hbm,
    partial_ref,
    mixed_scr,
    normed_scr,
    qkv_scr,
    heads_scr,
    weight_scr,
    out_scr,
    sems,
    out_sem,
):
    step = pl.program_id(0)
    slabs = pl.num_programs(0)
    bands, width, _ = tokens_ref.shape
    here = pl.ds(pl.multiple_of(step * LANES, LANES), LANES)
    features = weight_scr.shape[2]

    def copies():
        copy = pltpu.make_async_copy(out_hbm.at[pl.ds(0, features), :], out_scr, out_sem)
        return weight_copies(qkv_hbm, weight_scr, sems, 0) + [[copy]]

    @pl.when(step == 0)
    def _():
        for group in copies():
            for copy in group:
                copy.start()

    odd = lax.rem(lax.axis_index("rows"), 2) == 1
    intra = intra_ref[0, :, here].astype(jnp.float32)
    inter = inter_ref[0, :, here].astype(jnp.float32)
    rows = [jnp.where(odd, intra, inter)]
    rows += [tokens_ref[band, :, here].astype(jnp.float32) for band in range(bands)]
    rows += [jnp.where(odd, inter, intra)]
    position = lax.broadcasted_iota(jnp.int32, (width, LANES), 0)
    for band in range(bands):

        def stencil(offset_col):
            return (
                rows[band] * peg_ref[0, offset_col : offset_col + 1, :]
                + rows[band + 1] * peg_ref[1, offset_col : offset_col + 1, :]
                + rows[band + 2] * peg_ref[2, offset_col : offset_col + 1, :]
            )

        from_left = jnp.where(position == 0, 0.0, pltpu.roll(stencil(0), 1, 0))
        from_right = jnp.where(position == width - 1, 0.0, pltpu.roll(stencil(2), width - 1, 0))
        total = rows[band + 1] + peg_bias_ref[...] + stencil(1) + from_left + from_right
        mixed_scr[step, band * width : (band + 1) * width, :] = total.astype(
            jnp.bfloat16
        ).astype(jnp.float32)

    @pl.when(step == slabs - 1)
    def _():
        count = mixed_scr.shape[0]
        chunk = 64
        for start in range(0, bands * width, chunk):
            values = jnp.concatenate(
                [mixed_scr[slab, start : start + chunk, :] for slab in range(count)], axis=1
            )
            normed_scr[start : start + chunk, :] = normalise(
                values, gain_ref[...], nbias_ref[...]
            )
        waits = copies()
        for part in range(3):
            for copy in waits[part]:
                copy.wait()
            projected = (
                jnp.dot(normed_scr[...], weight_scr[part], preferred_element_type=jnp.float32)
                + qkv_bias_ref[part : part + 1, :]
            )
            qkv_scr[part] = projected.astype(jnp.bfloat16)
        scale = score_scale(width)
        for band in range(bands):
            span = slice(band * width, (band + 1) * width)
            for pair in range(features // LANES):
                lanes = slice(pair * LANES, (pair + 1) * LANES)
                heads_scr[span, lanes] = attend_pair(
                    qkv_scr[0, span, lanes],
                    qkv_scr[1, span, lanes],
                    qkv_scr[2, span, lanes],
                    scale,
                    None,
                ).astype(jnp.bfloat16)
        waits[3][0].wait()
        for slab in range(count):
            lanes = slice(slab * LANES, (slab + 1) * LANES)
            partial_ref[:, lanes] = (
                jnp.dot(heads_scr[...], out_scr[:, lanes], preferred_element_type=jnp.float32)
                + mixed_scr[slab]
                + out_bias_ref[:, lanes]
            )


def row_part(
    tokens,
    intra,
    inter,
    peg_weight,
    peg_bias,
    gain,
    nbias,
    qkv_weight,
    qkv_bias,
    out_weight,
    out_bias,
):
    bands, width, model = tokens.shape
    slabs = model // LANES
    features = ROW_HEADS * DH
    count = bands * width
    whole2 = lambda i: (0, 0)
    return pl.pallas_call(
        row_kernel,
        grid=(slabs,),
        in_specs=[
            pl.BlockSpec(memory_space=pltpu.VMEM),
            pl.BlockSpec(memory_space=pltpu.VMEM),
            pl.BlockSpec(memory_space=pltpu.VMEM),
            pl.BlockSpec((3, 3, LANES), lambda i: (0, 0, i)),
            pl.BlockSpec((1, LANES), lambda i: (0, i)),
            pl.BlockSpec((1, model), whole2),
            pl.BlockSpec((1, model), whole2),
            pl.BlockSpec((3, features), whole2),
            pl.BlockSpec((1, model), whole2),
            pl.BlockSpec(memory_space=pltpu.HBM),
            pl.BlockSpec(memory_space=pltpu.HBM),
        ],
        out_specs=pl.BlockSpec((count, model), whole2),
        out_shape=pltpu.HBM((count, model), jnp.float32),
        scratch_shapes=[
            pltpu.VMEM((slabs, count, LANES), jnp.float32),
            pltpu.VMEM((count, model), jnp.bfloat16),
            pltpu.VMEM((3, count, features), jnp.bfloat16),
            pltpu.VMEM((count, features), jnp.bfloat16),
            pltpu.VMEM((3, model, features), jnp.bfloat16),
            pltpu.VMEM((features, model), jnp.bfloat16),
            pltpu.SemaphoreType.DMA((3, 4)),
            pltpu.SemaphoreType.DMA,
        ],
        compiler_params=pltpu.CompilerParams(vmem_limit_bytes=14 * MIB),
        cost_estimate=pl.CostEstimate(
            flops=40 * count * model * 4 * features,
            transcendentals=count * width * ROW_HEADS,
            bytes_accessed=10 * 1024 * 1024,
        ),
        name="row_heads",
    )(
        tokens,
        intra,
        inter,
        peg_weight,
        peg_bias,
        gain,
        nbias,
        qkv_bias[:, :features],
        out_bias,
        in_hbm(qkv_weight),
        in_hbm(out_weight),
    )


def last_kernel(partial_ref, heads_ref, out_weight_ref, out_hbm, result_scr, sems):
    devices, tiles, sub, features = heads_ref.shape
    bands, width, model = result_scr.shape
    first = ROW_HEADS * DH
    block = model // sems.shape[0]
    heads = heads_ref[...].reshape(devices * tiles * sub, features)
    upper = lax.broadcasted_iota(jnp.int32, (1, sub, block), 1) < HALF
    copies = []
    for step in range(sems.shape[0]):
        lanes = slice(step * block, (step + 1) * block)
        projected = jnp.dot(
            heads, out_weight_ref[first:, lanes], preferred_element_type=jnp.float32
        )
        pairs = projected.reshape(devices * tiles // 2, 2, sub, block)
        low, high = pairs[:, 0], pairs[:, 1]
        rows = (
            jnp.where(upper, low, pltpu.roll(high, HALF, 1)),
            jnp.where(upper, pltpu.roll(low, HALF, 1), high),
        )
        for band, value in enumerate(rows):
            result_scr[band, :, lanes] = (
                partial_ref[band, :, lanes] + value.reshape(width, block)
            ).astype(jnp.bfloat16)
        copy = pltpu.make_async_copy(
            result_scr.at[:, :, lanes], out_hbm.at[:, :, lanes], sems.at[step]
        )
        copy.start()
        copies.append(copy)
    for copy in copies:
        copy.wait()


def last_part(partial, heads, out_weight, bands, width):
    features = heads.shape[3]
    model = out_weight.shape[1]
    return pl.pallas_call(
        last_kernel,
        in_specs=[pl.BlockSpec(memory_space=pltpu.VMEM)] * 3,
        out_specs=pl.BlockSpec(memory_space=pltpu.HBM),
        out_shape=jax.ShapeDtypeStruct((bands, width, model), jnp.bfloat16),
        scratch_shapes=[
            pltpu.VMEM((bands, width, model), jnp.bfloat16),
            pltpu.SemaphoreType.DMA((4,)),
        ],
        compiler_params=pltpu.CompilerParams(vmem_limit_bytes=8 * MIB),
        cost_estimate=pl.CostEstimate(
            flops=2 * bands * width * features * model,
            transcendentals=0,
            bytes_accessed=5 * MIB,
        ),
        name="last_projection",
    )(partial.reshape(bands, width, model), heads, out_weight)


def on_device(
    tokens, peg_weight, peg_bias, norm_gain, norm_bias, qkv_weight, qkv_bias, out_weight, out_bias
):
    devices = lax.axis_size("rows")
    bands, width, model = tokens.shape
    cols = width // devices
    fits = (
        bands == 2
        and width % LANES == 0
        and cols % 16 == 0
        and devices * SUB == LANES
        and model == 2 * ROW_HEADS * DH
        and model % LANES == 0
    )
    if not fits:
        return plain(
            tokens,
            peg_weight,
            peg_bias,
            norm_gain,
            norm_bias,
            qkv_weight,
            qkv_bias,
            out_weight,
            out_bias,
        )
    peg_bias = peg_bias.reshape(1, model)
    gain = norm_gain.reshape(1, model)
    nbias = norm_bias.reshape(1, model)
    out_bias = out_bias.reshape(1, model)
    qkv_bias = qkv_bias.reshape(3, model)

    packed, intra, inter = front(tokens, devices)
    same_chip = [(i, i ^ 1) for i in range(devices)]
    other_chip = [(i, i + 1 if i % 2 else i - 1) for i in range(1, devices - 1)]
    inter = lax.ppermute(inter, "rows", other_chip)
    intra = lax.ppermute(intra, "rows", same_chip)
    received = lax.all_to_all(packed, "rows", split_axis=0, concat_axis=0, tiled=True)
    partial = row_part(
        tokens,
        in_hbm(intra),
        in_hbm(inter),
        peg_weight,
        peg_bias,
        gain,
        nbias,
        qkv_weight,
        qkv_bias,
        out_weight,
        out_bias,
    )
    col_heads = column_part(
        received, (partial,), peg_weight, peg_bias, gain, nbias, qkv_weight, qkv_bias
    )
    returned = lax.all_to_all(col_heads, "rows", split_axis=0, concat_axis=0, tiled=True)
    return last_part(partial, returned, out_weight, bands, width)


def solution(mesh):
    placed = (P(("groups", "rows"), None, None), P(), P(), P(), P(), P(), P(), P(), P())
    return jax.shard_map(
        on_device,
        mesh=mesh,
        in_specs=placed,
        out_specs=P(("groups", "rows"), None, None),
        check_vma=False,
    )
```
